128 devices in a mesh: row: 8 (over x, z_hi), col: 16 (over y, z_lo, core).
Axes of the slice: x: 4, y: 4, z: 4 (z_hi: 2, z_lo: 2; z = z_hi * 2 + z_lo), core: 2. Of those that a mesh axis runs over, the one named last changes fastest.
Arguments:
- residual: bfloat16 [256, 5120], P('row', 'col'), may hold values from -6 to 6
- attn_gain: float32 [5120], P('col'), may hold values from 0.1 to 1.9
- w_query: bfloat16 [5120, 5120], P('col', 'row'), may hold values from -0.078125 to 0.078125
- w_key: bfloat16 [5120, 1024], P('col', 'row'), may hold values from -0.078125 to 0.078125
- w_value: bfloat16 [5120, 1024], P('col', 'row'), may hold values from -0.078125 to 0.078125
- w_out: bfloat16 [5120, 5120], P('row', 'col'), may hold values from -0.078125 to 0.078125
- mlp_gain: float32 [5120], P('col'), may hold values from 0.1 to 1.9
- w_gate: bfloat16 [2, 5120, 13824], P(None, 'col', 'row'), may hold values from -0.078125 to 0.078125
- w_up: bfloat16 [2, 5120, 13824], P(None, 'col', 'row'), may hold values from -0.078125 to 0.078125
- w_down: bfloat16 [2, 13824, 5120], P(None, 'row', 'col'), may hold values from -0.0546875 to 0.0546875
- final_gain: float32 [5120], P('col'), may hold values from 0.1 to 1.9
- w_head: bfloat16 [5120, 81920], P(None, ('row', 'col')), may hold values from -32 to 32
- seq_lengths: int32 [8], replicated, may hold values from 1 to 64, 256 in all
- targets: int32 [256], replicated, may hold values from 0 to 81919
Outputs:
- seq_diff: float32 [8], replicated
The draws below stay inside these ranges and needn't reach their ends.
Inputs may be any that keep to these rules, and one draw needn't show every extreme that they name: `seq_lengths`: the lengths sum to 256 and the largest is exactly 64.
All inputs are finite; a program needn't handle non-finite values.
Results may differ from the reference program's by a relative error of at most 0.02.
Values may be sent and summed in bfloat16 or wider, within the bound.
A program may use at most 64 MiB of HBM per device.

```python
import math
import jax
import jax.numpy as jnp
import numpy as np
from jax import lax

D = 5120
HEADS = 40
KV_HEADS = 8
HEAD_DIM = 128
FF = 13824
VOCAB = 81920
TOKENS = 256
SEQS = 8


def draw_w_head(key, part):
    base_key = jax.random.fold_in(key, 11)
    spread = 3.0 / math.sqrt(D)
    base = jnp.clip(jax.random.normal(base_key, (D, VOCAB), jnp.float32), -6.0, 6.0) * spread
    return base.astype(jnp.bfloat16)


def touch_ends(array, rng, smallest, largest):
    extent = array.shape
    place = [jax.random.randint(jax.random.fold_in(rng, axis), (), 0, extent[axis]) for axis in range(len(extent))]
    array = array.at[tuple(place)].set(smallest)
    longest = extent.index(max(extent))
    place[longest] = (place[longest] + 1) % extent[longest]
    return array.at[tuple(place)].set(largest)


def shard_levels(own_key, extent, pieces, smallest, largest):
    def one(position, parts):
        heights = jax.random.uniform(jax.random.fold_in(jax.random.fold_in(own_key, 6), position), (parts,), jnp.float32, smallest / len(pieces), largest / len(pieces))
        return jnp.repeat(jnp.exp(heights), extent[position] // parts).reshape((-1,) + (1,) * (len(extent) - position - 1))

    level = one(*pieces[0])
    for cut in pieces[1:]:
        level = level * one(*cut)
    return level


def skewed_wide(key, shape, count, skew):
    portions = [min(1 << octave, count + 1 - (1 << octave)) * (1 << 20) // math.isqrt((1 << octave) ** skew) + 1 for octave in range((count + 1).bit_length()) if 1 << octave <= count]
    scale = 1 + sum(portions) // (1 << 30)
    table = np.cumsum(np.array([max(1, weight // scale) for weight in portions]))
    ticket = jax.random.randint(jax.random.fold_in(key, 1), shape, 0, int(table[len(portions) - 1]))
    start = jnp.left_shift(1, jnp.searchsorted(jnp.asarray(table, jnp.int32), ticket, side="right").astype(jnp.int32))
    standing = start - 1 + jax.random.randint(jax.random.fold_in(key, 4), shape, 0, 1 << 30) % jnp.minimum(start, count + 1 - start)
    return jax.random.permutation(jax.random.fold_in(key, 2), count)[standing].astype(jnp.int32)


def length_profile(number_of, total, most, lean):
    weights = [(1 << 20) // math.isqrt(standing ** lean) + 1 for standing in range(2, number_of + 1)]
    spare, given = total - most - (number_of - 1), [1] * (number_of - 1)
    while spare > 0:
        free = [i for i in range(number_of - 1) if given[i] < most]
        whole, left = sum([weights[i] for i in free]), spare
        for i in free:
            addition = min(most - given[i], max(1, left * weights[i] // whole), spare)
            given[i] = given[i] + addition
            spare = spare - addition
    return np.array([most] + given)


def uneven_parts(own_key, amount, total, limit, slope):
    if amount == 2:
        one = jax.random.randint(own_key, (), max(1, total - limit), min(limit, total - 1) + 1)
        return jnp.stack([one, total - one])
    sizes = jnp.asarray(length_profile(amount, total, limit, slope), jnp.int32)
    pairs = (amount - 1) // 2
    giver, receiver = sizes[1:1 + 2 * pairs:2], sizes[2:2 + 2 * pairs:2]
    slack = jnp.minimum(giver - 1, limit - receiver)
    moved = jax.random.randint(jax.random.fold_in(own_key, 1), (pairs,), 0, 1 << 20) % (slack + 1)
    sizes = sizes.at[1:1 + 2 * pairs:2].set(giver - moved).at[2:2 + 2 * pairs:2].set(receiver + moved)
    return sizes[jax.random.permutation(jax.random.fold_in(own_key, 2), amount)]


def centred(stream_key, dims, width, most, shards=(), kind=jnp.bfloat16):
    drawn = jax.random.normal(stream_key, dims, jnp.float32) * width
    if len(shards) > 0:
        drawn = shard_levels(stream_key, dims, shards, -0.22, 0.18) * drawn
    return jnp.clip(drawn, min=-most, max=most).astype(kind)


def setup_inputs(seed: int = 0) -> dict:
    arg_keys = jax.random.split(jax.random.key(seed), 15)
    residual = centred(arg_keys[0], (TOKENS, D), 1.0, 6.0, ((0, 8), (1, 16)))
    attn_gain = jnp.clip(1.0 + 0.18 * jax.random.normal(arg_keys[1], (D,), jnp.float32), 0.1, 1.9)
    w_query = centred(arg_keys[2], (D, HEADS * HEAD_DIM), D ** -0.5, 0.078125, ((0, 16), (1, 8)))
    w_key = centred(arg_keys[3], (D, KV_HEADS * HEAD_DIM), D ** -0.5, 0.078125, ((0, 16), (1, 8)))
    w_value = centred(arg_keys[4], (D, KV_HEADS * HEAD_DIM), D ** -0.5, 0.078125, ((0, 16), (1, 8)))
    w_out = centred(arg_keys[5], (HEADS * HEAD_DIM, D), (HEADS * HEAD_DIM) ** -0.5, 0.078125, ((0, 8), (1, 16)))
    mlp_gain = jnp.clip(1.0 + 0.18 * jax.random.normal(arg_keys[6], (D,), jnp.float32), 0.1, 1.9)
    w_gate = centred(arg_keys[7], (2, D, FF), D ** -0.5, 0.078125, ((1, 16), (2, 8)))
    w_up = centred(arg_keys[8], (2, D, FF), D ** -0.5, 0.078125, ((1, 16), (2, 8)))
    w_down = centred(arg_keys[9], (2, FF, D), FF ** -0.5, 0.0546875, ((1, 8), (2, 16)))
    final_gain = jnp.clip(1.0 + 0.18 * jax.random.normal(arg_keys[10], (D,), jnp.float32), 0.1, 1.9)
    w_head = draw_w_head(jax.random.fold_in(arg_keys[14], 71), 0)
    seq_lengths = uneven_parts(arg_keys[12], SEQS, TOKENS, TOKENS // 4, 2).astype(jnp.int32)
    targets = touch_ends(skewed_wide(arg_keys[13], (TOKENS,), VOCAB, 2), jax.random.fold_in(arg_keys[13], 3), 0, VOCAB - 1).astype(jnp.int32)
    return dict(residual=residual, attn_gain=attn_gain, w_query=w_query, w_key=w_key, w_value=w_value, w_out=w_out, mlp_gain=mlp_gain, w_gate=w_gate, w_up=w_up, w_down=w_down, final_gain=final_gain, w_head=w_head, seq_lengths=seq_lengths, targets=targets)


EPSILON = 1e-06
ROPE_BASE = 1000000.0
MASKED = -1e+30

def normalize(features, gain_vector):
    mean_square = lax.optimization_barrier(jnp.mean(features * features, axis=-1, keepdims=True))
    return features * lax.rsqrt(mean_square + EPSILON) * gain_vector[None, :]

def sequence_layout(seq_lengths, token_index):
    ends_at = jnp.cumsum(seq_lengths).astype(jnp.int32)
    before = ends_at[None, :] <= token_index[:, None]
    segment = lax.optimization_barrier(jnp.sum(before.astype(jnp.int32), axis=1)).astype(jnp.int32)
    starts_at = lax.optimization_barrier(jnp.sum(jnp.where(before, seq_lengths[None, :], 0), axis=1)).astype(jnp.int32)
    return (segment, (token_index - starts_at).astype(jnp.float32))

def angles_for(positions, head_width):
    exponent = jnp.arange(head_width // 2, dtype=jnp.float32) * 2.0 / head_width
    frequency = ROPE_BASE ** (-exponent)
    return positions[:, None] * frequency[None, :]

def rotate(features, angles):
    half_width = features.shape[-1] // 2
    lower_half = features[..., :half_width]
    upper_half = features[..., half_width:]
    cosine = jnp.cos(angles)[:, None, :]
    sine_part = jnp.sin(angles)[:, None, :]
    return jnp.concatenate([lower_half * cosine - upper_half * sine_part, upper_half * cosine + lower_half * sine_part], axis=-1)

def reference(residual, attn_gain, w_query, w_key, w_value, w_out, mlp_gain, w_gate, w_up, w_down, final_gain, w_head, seq_lengths, targets):
    stream_in = residual.astype(jnp.float32)
    normed = normalize(stream_in, attn_gain).astype(jnp.bfloat16)
    token_index = jnp.arange(TOKENS, dtype=jnp.int32)
    segment, positions = sequence_layout(seq_lengths, token_index)
    angles = angles_for(positions, HEAD_DIM)
    queries = rotate(jnp.dot(normed, w_query, preferred_element_type=jnp.float32).reshape(TOKENS, HEADS, HEAD_DIM), angles).astype(jnp.bfloat16)
    keys_all = rotate(jnp.dot(normed, w_key, preferred_element_type=jnp.float32).reshape(TOKENS, KV_HEADS, HEAD_DIM), angles).astype(jnp.bfloat16)
    values_all = jnp.dot(normed, w_value, preferred_element_type=jnp.float32).astype(jnp.bfloat16).reshape(TOKENS, KV_HEADS, HEAD_DIM)
    group_size = HEADS // KV_HEADS
    grouped = queries.reshape(TOKENS, KV_HEADS, group_size, HEAD_DIM).transpose(1, 2, 0, 3)
    allowed = (segment[:, None] == segment[None, :]) & (token_index[None, :] <= token_index[:, None])

    def one_head(operands):
        query_block, key_block, value_block = operands
        scores = jnp.einsum('gqd,kd->gqk', query_block.astype(jnp.float32), key_block.astype(jnp.float32)) * HEAD_DIM ** (-0.5)
        scores = jnp.where(allowed[None], scores, MASKED)
        top_value = lax.optimization_barrier(jnp.max(scores, axis=-1, keepdims=True))
        weights = jnp.exp(scores - top_value)
        weights = (weights / lax.optimization_barrier(jnp.sum(weights, axis=-1, keepdims=True))).astype(jnp.bfloat16)
        return jnp.einsum('gqk,kd->gqd', weights.astype(jnp.float32), value_block.astype(jnp.float32))
    attended = lax.map(one_head, (grouped, keys_all.transpose(1, 0, 2), values_all.transpose(1, 0, 2)))
    attended = attended.astype(jnp.bfloat16).transpose(2, 0, 1, 3).reshape(TOKENS, HEADS * HEAD_DIM)
    projected = jnp.dot(attended, w_out, preferred_element_type=jnp.float32)
    stream = lax.optimization_barrier((stream_in + projected).astype(jnp.bfloat16))
    stream_f = stream.astype(jnp.float32)
    mlp_in = normalize(stream_f, mlp_gain).astype(jnp.bfloat16)
    logprobs = []
    for member in range(2):
        gate = jnp.dot(mlp_in, w_gate[member], preferred_element_type=jnp.float32)
        upward = jnp.dot(mlp_in, w_up[member], preferred_element_type=jnp.float32)
        hidden = (jax.nn.silu(gate) * upward).astype(jnp.bfloat16)
        output_f = stream_f + jnp.dot(hidden, w_down[member], preferred_element_type=jnp.float32)
        final_state = normalize(output_f, final_gain).astype(jnp.bfloat16)
        logits = jnp.dot(final_state, w_head, preferred_element_type=jnp.float32)
        top_value = lax.optimization_barrier(jnp.max(logits, axis=1))
        log_total = top_value + jnp.log(lax.optimization_barrier(jnp.sum(jnp.exp(logits - top_value[:, None]), axis=1)))
        picked = jnp.take_along_axis(logits, targets[:, None].astype(jnp.int32), axis=1)[:, 0]
        logprobs.append(picked - log_total)
    difference = logprobs[0] - logprobs[1]
    one_hot = (segment[:, None] == jnp.arange(SEQS, dtype=jnp.int32)[None, :]).astype(jnp.float32)
    seq_sums = jnp.dot(difference, one_hot, precision=lax.Precision.HIGHEST)
    return seq_sums / seq_lengths.astype(jnp.float32)
```

```python
import math

import jax
import jax.numpy as jnp
from jax import lax
from jax.experimental import pallas as pl
from jax.experimental.pallas import tpu as pltpu
from jax.sharding import PartitionSpec as P

T = 256
D = 5120
HEAD = 128
Q_HEADS = 5
QW = Q_HEADS * HEAD
QKV = QW + 2 * HEAD
SEQS = 8
FEAT = 320
CHIP = 2 * FEAT
FF = 1728
FFP = 1792
VOCAB = 640
ROWS = 8
COLS = 16
CHIPS = 8
EPSILON = 1e-06
ROPE_BASE = 1000000.0
MASKED = -1e30
MESH = pl.DeviceIdType.MESH
F32 = jnp.float32
BF16 = jnp.bfloat16


def remote(src, dst, send, recv, row, col):
    return pltpu.make_async_remote_copy(
        src_ref=src, dst_ref=dst, send_sem=send, recv_sem=recv,
        device_id={"row": row, "col": col}, device_id_type=MESH,
    )


def each(start, stop, body):
    def step(i, carry):
        body(i)
        return carry

    lax.fori_loop(start, stop, step, 0)


def split_sum(total, width):
    high = total.astype(BF16)
    low = (total - high.astype(F32)).astype(BF16)
    shape = (total.shape[0], width)
    return (
        jnp.broadcast_to(high.astype(F32), shape).astype(BF16),
        jnp.broadcast_to(low.astype(F32), shape).astype(BF16),
    )


def inverse_rms(total):
    return lax.rsqrt(total / D + EPSILON)


def layout_of(lens_ref, token):
    segment = jnp.zeros_like(token)
    start = jnp.zeros_like(token)
    end = jnp.int32(0)
    for s in range(SEQS):
        length = lens_ref[s]
        end = end + length
        before = end <= token
        segment = segment + jnp.where(before, 1, 0)
        start = start + jnp.where(before, length, 0)
    return segment, token - start


def kernel(
    res, attn_gain, w_query, w_key, w_value, w_out, mlp_gain, w_gate, w_up, w_down, final_gain, w_head, lens, targets,
    out,
    x_all, res_chip, wqkv, wo, wg, wu, wd, wh, mg, fg,
    part_send, part_recv, qkv_all, attended, proj_send, proj_recv, stream_all,
    gate_send, gate_recv, up_send, up_recv, hidden_all, down_send, down_recv,
    fin_a, fin_b, fin_c, logits, stat_send, stat_recv, stat2_recv,
    local_sem, swap_send, swap_recv, x_s, x_r, part_s, part_r, qkv_s, qkv_r, proj_s, proj_r, stream_s, stream_r,
    gu_s, gu_r, hid_s, hid_r, down_s, down_r, fin_s, fin_r, st_s, st_r, st2_s, st2_r,
):
    row, col = lax.axis_index("row"), lax.axis_index("col")
    core = lax.rem(col, 2)
    other = 1 - core
    chip = lax.div(col, 2)
    cx, zh = lax.div(row, 2), lax.rem(row, 2)
    cy, zl = lax.div(chip, 2), lax.rem(chip, 2)
    cz = zh * 2 + zl
    sib = chip * 2 + other

    def row_at(d):
        return lax.rem(row + d, ROWS)

    def chip_at(d):
        return lax.rem(chip + d, CHIPS)

    def col_at(d):
        return lax.rem(col + d, COLS)

    def at_xyz(x, y, z):
        return x * 2 + lax.div(z, 2), (y * 2 + lax.rem(z, 2)) * 2 + core

    mine = pl.ds(pl.multiple_of(core * FEAT, 64), FEAT)
    local = [
        (res, x_all.at[row]),
        (w_query, wqkv.at[:, 0:QW]),
        (w_key, wqkv.at[:, QW:QW + HEAD]),
        (w_value, wqkv.at[:, QW + HEAD:QKV]),
        (res, res_chip.at[core]),
        (mlp_gain, mg.at[core]),
        (final_gain, fg.at[core]),
        (w_out, wo.at[core]),
        (w_gate.at[core], wg.at[mine]),
        (w_up.at[core], wu.at[mine]),
        (w_down.at[core], wd.at[core]),
        (w_head, wh.at[core]),
    ]
    local = [pltpu.make_async_copy(s, d, local_sem.at[i]) for i, (s, d) in enumerate(local)]
    for copy in local:
        copy.start()

    barrier = pltpu.get_barrier_semaphore()

    def greet(r, c):
        pl.semaphore_signal(barrier, inc=1, device_id={"row": r, "col": c}, device_id_type=MESH)

    each(1, ROWS, lambda d: greet(row_at(d), col))
    each(1, ROWS, lambda d: greet(row_at(d), sib))
    each(1, COLS, lambda d: greet(row, col_at(d)))
    cross_z = lax.rem(cz + 1 + 2 * (1 - zl), 4)
    cross_row, cross_col = at_xyz(cx, cy, cross_z)
    greet(cross_row, cross_col)
    pl.semaphore_wait(barrier, 2 * (ROWS - 1) + (COLS - 1) + 1)

    def x_copy(d):
        return remote(res, x_all.at[row], x_s.at[d], x_r.at[d], row_at(d), col)

    each(1, ROWS, lambda d: x_copy(d).start())

    swaps = [
        (res, res_chip.at[core]),
        (mlp_gain, mg.at[core]),
        (final_gain, fg.at[core]),
        (w_out, wo.at[core]),
        (w_gate.at[other], wg.at[mine]),
        (w_up.at[other], wu.at[mine]),
        (w_down.at[other], wd.at[core]),
        (w_head, wh.at[core]),
    ]
    swaps = [remote(s, d, swap_send.at[i], swap_recv.at[i], row, sib) for i, (s, d) in enumerate(swaps)]
    for copy in swaps:
        copy.start()

    own_token = COLS * col + lax.broadcasted_iota(jnp.int32, (16, HEAD), 0)
    position = layout_of(lens, own_token)[1].astype(F32)
    lane = lax.broadcasted_iota(jnp.int32, (16, HEAD), 1)
    low_half = lane < HEAD // 2
    frequency = jnp.exp(jnp.where(low_half, lane, lane - HEAD // 2).astype(F32) * (-2.0 * math.log(ROPE_BASE) / HEAD))
    angle = position * frequency
    cosine = jnp.cos(angle)
    sine = jnp.where(low_half, -jnp.sin(angle), jnp.sin(angle))

    for i in range(4):
        local[i].wait()
    each(1, ROWS, lambda d: x_copy(d).wait_recv())

    x = x_all[...].reshape(T, FEAT).astype(F32)
    square_hi, square_lo = split_sum(jnp.sum(x * x, axis=1, keepdims=True), 64)
    xg = (x * attn_gain[...]).astype(BF16)
    part = jnp.dot(xg, wqkv[...], preferred_element_type=F32).astype(BF16)
    part_send[:, :, 0:QKV] = part.reshape(COLS, 16, QKV)
    part_send[:, :, QKV:QKV + 64] = square_hi.reshape(COLS, 16, 64)
    part_send[:, :, QKV + 64:QKV + 128] = square_lo.reshape(COLS, 16, 64)

    def part_copy(d):
        c = col_at(d)
        return remote(part_send.at[c], part_recv.at[d], part_s.at[d], part_r.at[d], row, c)

    each(1, COLS, lambda d: part_copy(d).start())
    part_recv[0] = part_send[col]
    each(1, COLS, lambda d: part_copy(d).wait_recv())

    total = jnp.sum(part_recv[...].astype(F32), axis=0)
    scale = inverse_rms(total[:, QKV:QKV + 1] + total[:, QKV + 64:QKV + 65])
    for h in range(Q_HEADS + 1):
        head = total[:, h * HEAD:(h + 1) * HEAD] * scale
        turned = head * cosine + pltpu.roll(head, HEAD // 2, 1) * sine
        qkv_all[chip, core, :, h * HEAD:(h + 1) * HEAD] = turned.astype(BF16)
    qkv_all[chip, core, :, QW + HEAD:QKV] = (total[:, QW + HEAD:QKV] * scale).astype(BF16)

    own_qkv = qkv_all.at[chip, core]
    own_kv = qkv_all.at[chip, core, :, QW:QKV]

    def qkv_copy(d):
        return remote(own_qkv, own_qkv, qkv_s.at[d], qkv_r.at[d], row, chip_at(d) * 2 + core)

    def kv_copy(d):
        return remote(own_kv, own_kv, qkv_s.at[CHIPS + d], qkv_r.at[CHIPS + d], row, chip_at(d) * 2 + other)

    each(1, CHIPS, lambda d: qkv_copy(d).start())
    each(0, CHIPS, lambda d: kv_copy(d).start())

    row_i = lax.broadcasted_iota(jnp.int32, (T // 2, 1), 0)
    q_token = lax.div(row_i, 16) * 32 + core * 16 + lax.rem(row_i, 16)
    k_token = lax.broadcasted_iota(jnp.int32, (1, T), 1)
    q_segment = layout_of(lens, q_token)[0]
    k_segment = layout_of(lens, k_token)[0]
    allowed = (q_segment == k_segment) & (k_token <= q_token)

    each(1, CHIPS, lambda d: qkv_copy(d).wait_recv())
    each(0, CHIPS, lambda d: kv_copy(d).wait_recv())

    keys = qkv_all[:, :, :, QW:QW + HEAD].reshape(T, HEAD)
    values = qkv_all[:, :, :, QW + HEAD:QKV].reshape(T, HEAD)
    for h in range(Q_HEADS):
        query = qkv_all[:, core, :, h * HEAD:(h + 1) * HEAD].reshape(T // 2, HEAD)
        scores = lax.dot_general(query, keys, (((1,), (1,)), ((), ())), preferred_element_type=F32)
        scores = jnp.where(allowed, scores * HEAD ** (-0.5), MASKED)
        weights = jnp.exp(scores - jnp.max(scores, axis=1, keepdims=True))
        weights = (weights / jnp.sum(weights, axis=1, keepdims=True)).astype(BF16)
        result = jnp.dot(weights, values, preferred_element_type=F32)
        attended[:, h * HEAD:(h + 1) * HEAD] = result.astype(BF16)

    for i in range(4, 8):
        local[i].wait()
    for i in range(0, 4):
        swaps[i].wait_recv()
    heads = attended[...]
    for j in range(2):
        half = jnp.dot(heads, wo[j], preferred_element_type=F32).astype(BF16)
        proj_send[:, :, j * FEAT:(j + 1) * FEAT] = half.reshape(ROWS, 16, FEAT)

    def proj_copy(d):
        r = row_at(d)
        return remote(proj_send.at[r], proj_recv.at[d], proj_s.at[d], proj_r.at[d], r, col)

    each(1, ROWS, lambda d: proj_copy(d).start())
    proj_recv[0] = proj_send[row]
    each(1, ROWS, lambda d: proj_copy(d).wait_recv())
    half_rows = pl.ds(pl.multiple_of(core * 16, 16), 16)
    residual = jnp.concatenate([res_chip[0, half_rows, :], res_chip[1, half_rows, :]], axis=1).astype(F32)
    stream_all[row, core] = (residual + jnp.sum(proj_recv[...].astype(F32), axis=0)).astype(BF16)

    own_stream = stream_all.at[row, core]

    def stream_copy(d):
        return remote(own_stream, own_stream, stream_s.at[d], stream_r.at[d], row_at(d), col)

    def stream_cross(d):
        return remote(own_stream, own_stream, stream_s.at[ROWS + d], stream_r.at[ROWS + d], row_at(d), sib)

    each(1, ROWS, lambda d: stream_copy(d).start())
    each(0, ROWS, lambda d: stream_cross(d).start())
    for i in range(8, 11):
        local[i].wait()
    for i in range(4, 6):
        swaps[i].wait_recv()
    each(1, ROWS, lambda d: stream_copy(d).wait_recv())
    each(0, ROWS, lambda d: stream_cross(d).wait_recv())

    stream = stream_all[...].reshape(T, CHIP).astype(F32)
    square_hi, square_lo = split_sum(jnp.sum(stream * stream, axis=1, keepdims=True), FFP - FF)
    gain = jnp.concatenate([mg[0], mg[1]], axis=1)
    xg = (stream * gain).astype(BF16)

    def gu_copy(kind, send, recv, d):
        c = chip_at(d)
        return remote(
            send.at[c], recv.at[d], gu_s.at[kind, d], gu_r.at[kind, d], row, c * 2 + core
        )

    gate_send[:, :, 0:FF] = jnp.dot(xg, wg[...], preferred_element_type=F32).astype(BF16).reshape(CHIPS, 32, FF)
    gate_send[:, :, FF:FFP] = square_hi.reshape(CHIPS, 32, FFP - FF)
    each(1, CHIPS, lambda d: gu_copy(0, gate_send, gate_recv, d).start())
    up_send[:, :, 0:FF] = jnp.dot(xg, wu[...], preferred_element_type=F32).astype(BF16).reshape(CHIPS, 32, FF)
    up_send[:, :, FF:FFP] = square_lo.reshape(CHIPS, 32, FFP - FF)
    each(1, CHIPS, lambda d: gu_copy(1, up_send, up_recv, d).start())
    gate_recv[0] = gate_send[chip]
    up_recv[0] = up_send[chip]
    each(1, CHIPS, lambda d: gu_copy(0, gate_send, gate_recv, d).wait_recv())
    each(1, CHIPS, lambda d: gu_copy(1, up_send, up_recv, d).wait_recv())
    gate_sum = jnp.sum(gate_recv[...].astype(F32), axis=0)
    up_sum = jnp.sum(up_recv[...].astype(F32), axis=0)
    scale = inverse_rms(gate_sum[:, FF:FF + 1] + up_sum[:, FF:FF + 1])
    gate = gate_sum[:, 0:FF] * scale
    hidden_all[chip] = (gate / (1.0 + jnp.exp(-gate)) * (up_sum[:, 0:FF] * scale)).astype(BF16)

    own_hidden = hidden_all.at[chip]

    def hid_copy(d):
        return remote(own_hidden, own_hidden, hid_s.at[d], hid_r.at[d], row, chip_at(d) * 2 + core)

    each(1, CHIPS, lambda d: hid_copy(d).start())
    swaps[6].wait_recv()
    each(1, CHIPS, lambda d: hid_copy(d).wait_recv())

    hidden = hidden_all[...].reshape(T, FF)
    for j in range(2):
        half = jnp.dot(hidden, wd[j], preferred_element_type=F32).astype(BF16)
        down_send[:, :, j * FEAT:(j + 1) * FEAT] = half.reshape(ROWS, 32, FEAT)

    def down_copy(d):
        r = row_at(d)
        return remote(down_send.at[r], down_recv.at[d], down_s.at[d], down_r.at[d], r, col)

    each(1, ROWS, lambda d: down_copy(d).start())
    down_recv[0] = down_send[row]
    each(1, ROWS, lambda d: down_copy(d).wait_recv())
    final = stream_all[row].reshape(32, CHIP).astype(F32) + jnp.sum(down_recv[...].astype(F32), axis=0)
    square_hi, square_lo = split_sum(jnp.sum(final * final, axis=1, keepdims=True), 64)
    final = (final * jnp.concatenate([fg[0], fg[1]], axis=1)).astype(BF16)

    fin_a[cy, zl, cx, zh] = final[:, 0:256]
    fin_b[cy, zl, cx, zh] = final[:, 256:512]
    fin_c[cy, zl, cx, zh, :, 0:128] = final[:, 512:640]
    fin_c[cy, zl, cx, zh, :, 128:192] = square_hi
    fin_c[cy, zl, cx, zh, :, 192:256] = square_lo

    parts = (fin_a, fin_b, fin_c)
    orders = ("zyx", "xzy", "yxz")

    def axis_copies(p, stage):
        order = orders[p]
        axis, done = order[stage], order[:stage]
        one = {"y": pl.ds(cy, 1), "x": pl.ds(cx, 1), "zl": pl.ds(zl, 1), "zh": pl.ds(zh, 1)}
        full = {"y": pl.ds(0, 4), "x": pl.ds(0, 4), "zl": pl.ds(0, 2), "zh": pl.ds(0, 2)}
        pick = {k: full[k] if k[0] in done else one[k] for k in one}
        ref = parts[p].at[pick["y"], pick["zl"], pick["x"], pick["zh"]]
        copies = []
        for d in (2, 1, 3):
            x = lax.rem(cx + d, 4) if axis == "x" else cx
            y = lax.rem(cy + d, 4) if axis == "y" else cy
            z = lax.rem(cz + d, 4) if axis == "z" else cz
            r, c = at_xyz(x, y, z)
            i = (p * 3 + stage) * 3 + d - 1
            copies.append(remote(ref, ref, fin_s.at[i], fin_r.at[i], r, c))
        return copies

    gathers = [[axis_copies(p, stage) for p in range(3)] for stage in range(3)]
    for stage in range(3):
        for p in range(3):
            if stage:
                for copy in gathers[stage - 1][p]:
                    copy.wait_recv()
            for copy in gathers[stage][p]:
                copy.start()
    local[11].wait()
    swaps[7].wait_recv()
    diagonal = lax.broadcasted_iota(jnp.int32, (T, T), 0) == lax.broadcasted_iota(jnp.int32, (T, T), 1)
    target = jnp.sum(jnp.where(diagonal, targets[...].astype(F32), 0.0), axis=1, keepdims=True).astype(jnp.int32)
    for p in range(3):
        for copy in gathers[2][p]:
            copy.wait_recv()

    square = jnp.zeros((T, 1), F32)
    for cc in range(CHIPS):
        a = fin_a[cc // 2, cc % 2].reshape(T, 256)
        b = fin_b[cc // 2, cc % 2].reshape(T, 256)
        c = fin_c[cc // 2, cc % 2].reshape(T, 256)
        square = square + c[:, 128:129].astype(F32) + c[:, 192:193].astype(F32)
        base = cc * CHIP
        for j in range(2):
            product = jnp.dot(a, wh[j, base:base + 256], preferred_element_type=F32)
            product += jnp.dot(b, wh[j, base + 256:base + 512], preferred_element_type=F32)
            product += jnp.dot(c[:, 0:128], wh[j, base + 512:base + 640], preferred_element_type=F32)
            if cc == 0:
                logits[j] = product
            else:
                logits[j] = logits[j] + product
    scale = inverse_rms(square)
    both = [logits[j] * scale for j in range(2)]
    top = jnp.maximum(*[jnp.max(l, axis=1, keepdims=True) for l in both])
    exponential = sum(jnp.sum(jnp.exp(l - top), axis=1, keepdims=True) for l in both)
    picked = jnp.zeros((T, 1), F32)
    for j in range(2):
        first = (row * COLS + chip * 2 + j) * VOCAB
        ids = first + lax.broadcasted_iota(jnp.int32, (T, VOCAB), 1)
        picked = picked + jnp.sum(jnp.where(ids == target, both[j], 0.0), axis=1, keepdims=True)
    lane = lax.broadcasted_iota(jnp.int32, (T, HEAD), 1)
    packed = jnp.where(lane == 0, top, jnp.where(lane == 1, exponential, picked))
    stat_recv[0] = jnp.transpose(packed)[0:8, :]

    def st_copy(d):
        return remote(stat_recv.at[0], stat_recv.at[d], st_s.at[d], st_r.at[d], row, chip_at(d) * 2 + core)

    each(1, CHIPS, lambda d: st_copy(d).start())
    each(1, CHIPS, lambda d: st_copy(d).wait_recv())

    def merge(blocks):
        top = jnp.max(blocks[:, 0:1, :], axis=0)
        exponential = jnp.sum(blocks[:, 1:2, :] * jnp.exp(blocks[:, 0:1, :] - top[None]), axis=0)
        return top, exponential, jnp.sum(blocks[:, 2:3, :], axis=0)

    top, exponential, picked = merge(stat_recv[...])
    line = lax.broadcasted_iota(jnp.int32, (8, T), 0)
    stat_send[...] = jnp.where(line == 0, top, jnp.where(line == 1, exponential, picked))
    own_stat = stat2_recv.at[core, row]
    stat2_recv[core, row] = stat_send[...]

    def st2_copy(d):
        return remote(stat_send, own_stat, st2_s.at[d], st2_r.at[d], row_at(d), col)

    def st2_cross(d):
        return remote(stat_send, own_stat, st2_s.at[ROWS + d], st2_r.at[ROWS + d], row_at(d), sib)

    each(1, ROWS, lambda d: st2_copy(d).start())
    each(0, ROWS, lambda d: st2_cross(d).start())
    each(1, ROWS, lambda d: st2_copy(d).wait_recv())
    each(0, ROWS, lambda d: st2_cross(d).wait_recv())
    logprob = []
    for m in range(2):
        top, exponential, picked = merge(stat2_recv[m])
        logprob.append(picked - (top + jnp.log(exponential)))
    difference = logprob[0] - logprob[1]
    hit = line == k_segment
    sums = jnp.sum(jnp.where(hit, difference, 0.0), axis=1, keepdims=True)
    length = jnp.sum(jnp.where(hit, 1.0, 0.0), axis=1, keepdims=True)
    square8 = lax.broadcasted_iota(jnp.int32, (8, 8), 0) == lax.broadcasted_iota(jnp.int32, (8, 8), 1)
    out[...] = jnp.sum(jnp.where(square8, sums / length, 0.0), axis=0, keepdims=True)

    each(1, ROWS, lambda d: x_copy(d).wait_send())
    for copy in swaps:
        copy.wait_send()
    each(1, COLS, lambda d: part_copy(d).wait_send())
    each(1, CHIPS, lambda d: qkv_copy(d).wait_send())
    each(0, CHIPS, lambda d: kv_copy(d).wait_send())
    each(1, ROWS, lambda d: proj_copy(d).wait_send())
    each(1, ROWS, lambda d: stream_copy(d).wait_send())
    each(0, ROWS, lambda d: stream_cross(d).wait_send())
    each(1, CHIPS, lambda d: gu_copy(0, gate_send, gate_recv, d).wait_send())
    each(1, CHIPS, lambda d: gu_copy(1, up_send, up_recv, d).wait_send())
    each(1, CHIPS, lambda d: hid_copy(d).wait_send())
    each(1, ROWS, lambda d: down_copy(d).wait_send())
    for stage in gathers:
        for copies in stage:
            for copy in copies:
                copy.wait_send()
    each(1, CHIPS, lambda d: st_copy(d).wait_send())
    each(1, ROWS, lambda d: st2_copy(d).wait_send())
    each(0, ROWS, lambda d: st2_cross(d).wait_send())


def per_device(
    residual, attn_gain, w_query, w_key, w_value, w_out, mlp_gain, w_gate, w_up, w_down, final_gain, w_head,
    seq_lengths, targets,
):
    anywhere = pl.BlockSpec(memory_space=pl.ANY)
    vmem = pl.BlockSpec(memory_space=pltpu.VMEM)
    smem = pl.BlockSpec(memory_space=pltpu.SMEM)
    dma = pltpu.SemaphoreType.DMA
    result = pl.pallas_call(
        kernel,
        out_shape=jax.ShapeDtypeStruct((1, SEQS), F32),
        in_specs=[anywhere, vmem] + [anywhere] * 10 + [smem, vmem],
        out_specs=vmem,
        scratch_shapes=[
            pltpu.VMEM((ROWS, 32, FEAT), BF16),
            pltpu.VMEM((2, 32, FEAT), BF16),
            pltpu.VMEM((FEAT, QKV), BF16),
            pltpu.VMEM((2, QW, FEAT), BF16),
            pltpu.VMEM((CHIP, FF), BF16),
            pltpu.VMEM((CHIP, FF), BF16),
            pltpu.VMEM((2, FF, FEAT), BF16),
            pltpu.VMEM((2, D, VOCAB), BF16),
            pltpu.VMEM((2, 1, FEAT), F32),
            pltpu.VMEM((2, 1, FEAT), F32),
            pltpu.VMEM((COLS, 16, QKV + 128), BF16),
            pltpu.VMEM((COLS, 16, QKV + 128), BF16),
            pltpu.VMEM((CHIPS, 2, 16, QKV), BF16),
            pltpu.VMEM((T // 2, QW), BF16),
            pltpu.VMEM((ROWS, 16, CHIP), BF16),
            pltpu.VMEM((ROWS, 16, CHIP), BF16),
            pltpu.VMEM((ROWS, 2, 16, CHIP), BF16),
            pltpu.VMEM((CHIPS, 32, FFP), BF16),
            pltpu.VMEM((CHIPS, 32, FFP), BF16),
            pltpu.VMEM((CHIPS, 32, FFP), BF16),
            pltpu.VMEM((CHIPS, 32, FFP), BF16),
            pltpu.VMEM((CHIPS, 32, FF), BF16),
            pltpu.VMEM((ROWS, 32, CHIP), BF16),
            pltpu.VMEM((ROWS, 32, CHIP), BF16),
            pltpu.VMEM((4, 2, 4, 2, 32, 256), BF16),
            pltpu.VMEM((4, 2, 4, 2, 32, 256), BF16),
            pltpu.VMEM((4, 2, 4, 2, 32, 256), BF16),
            pltpu.VMEM((2, T, VOCAB), F32),
            pltpu.VMEM((8, T), F32),
            pltpu.VMEM((CHIPS, 8, T), F32),
            pltpu.VMEM((2, ROWS, 8, T), F32),
            dma((12,)), dma((8,)), dma((8,)),
            dma((ROWS,)), dma((ROWS,)),
            dma((COLS,)), dma((COLS,)),
            dma((COLS,)), dma((COLS,)),
            dma((ROWS,)), dma((ROWS,)),
            dma((2 * ROWS,)), dma((2 * ROWS,)),
            dma((2, CHIPS)), dma((2, CHIPS)),
            dma((CHIPS,)), dma((CHIPS,)),
            dma((ROWS,)), dma((ROWS,)),
            dma((27,)), dma((27,)),
            dma((CHIPS,)), dma((CHIPS,)),
            dma((2 * ROWS,)), dma((2 * ROWS,)),
        ],
        compiler_params=pltpu.CompilerParams(
            collective_id=0, has_side_effects=True, vmem_limit_bytes=60 * 1024 * 1024
        ),
    )(
        residual, attn_gain.reshape(1, FEAT), w_query, w_key, w_value, w_out, mlp_gain.reshape(1, FEAT), w_gate, w_up,
        w_down, final_gain.reshape(1, FEAT), w_head, seq_lengths, targets.reshape(1, T),
    )
    return result.reshape(SEQS)


def solution(mesh):
    placed = (
        P("row", "col"), P("col"), P("col", "row"), P("col", "row"), P("col", "row"), P("row", "col"), P("col"),
        P(None, "col", "row"), P(None, "col", "row"), P(None, "row", "col"), P("col"), P(None, ("row", "col")), P(), P(),
    )
    return jax.shard_map(per_device, mesh=mesh, in_specs=placed, out_specs=P(), check_vma=False)
```

```python
import math

import jax
import jax.numpy as jnp
from jax import lax
from jax.experimental import pallas as pl
from jax.experimental.pallas import tpu as pltpu
from jax.sharding import PartitionSpec as P

T = 256
D = 5120
HEAD = 128
Q_HEADS = 5
QW = Q_HEADS * HEAD
QKV = QW + 2 * HEAD
SEQS = 8
FEAT = 320
CHIP = 2 * FEAT
FF = 1728
FFP = 1792
VOCAB = 640
ROWS = 8
COLS = 16
CHIPS = 8
EPSILON = 1e-06
ROPE_BASE = 1000000.0
MASKED = -1e30
MESH = pl.DeviceIdType.MESH
F32 = jnp.float32
BF16 = jnp.bfloat16


def remote(src, dst, send, recv, row, col):
    return pltpu.make_async_remote_copy(
        src_ref=src, dst_ref=dst, send_sem=send, recv_sem=recv,
        device_id={"row": row, "col": col}, device_id_type=MESH,
    )


def each(start, stop, body):
    def step(i, carry):
        body(i)
        return carry

    lax.fori_loop(start, stop, step, 0)


def dot_nt(a, b):
    return lax.dot_general(a, b, (((1,), (1,)), ((), ())), preferred_element_type=F32)


def split_sum(total, width):
    high = total.astype(BF16)
    low = (total - high.astype(F32)).astype(BF16)
    shape = (total.shape[0], width)
    return (
        jnp.broadcast_to(high.astype(F32), shape).astype(BF16),
        jnp.broadcast_to(low.astype(F32), shape).astype(BF16),
    )


def inverse_rms(total):
    return lax.rsqrt(total / D + EPSILON)


def layout_of(lens_ref, token):
    segment = jnp.zeros_like(token)
    start = jnp.zeros_like(token)
    end = jnp.int32(0)
    for s in range(SEQS):
        length = lens_ref[s]
        end = end + length
        before = end <= token
        segment = segment + jnp.where(before, 1, 0)
        start = start + jnp.where(before, length, 0)
    return segment, token - start


def kernel(
    res, attn_gain, w_query, w_key, w_value, w_out, mlp_gain, w_gate, w_up, w_down, final_gain, w_head, lens, targets,
    out,
    x_all, res_chip, wqkv, wo, wg, wu, wd, wh, gain_a, gain_m, gain_f, mg, fg,
    part_send, part_recv, qkv_all, attended, proj_send, proj_recv, stream_all,
    gate_send, gate_recv, up_send, up_recv, hidden_all, down_send, down_recv,
    fin_a, fin_b, fin_c, logits, stat_send, stat_recv, stat2_recv,
    local_sem, swap_send, swap_recv, x_s, x_r, part_s, part_r, qkv_s, qkv_r, proj_s, proj_r, stream_s, stream_r,
    gu_s, gu_r, hid_s, hid_r, down_s, down_r, fin_s, fin_r, st_s, st_r, st2_s, st2_r,
):
    row, col = lax.axis_index("row"), lax.axis_index("col")
    core = lax.rem(col, 2)
    other = 1 - core
    chip = lax.div(col, 2)
    cx, zh = lax.div(row, 2), lax.rem(row, 2)
    cy, zl = lax.div(chip, 2), lax.rem(chip, 2)
    cz = zh * 2 + zl
    sib = chip * 2 + other

    def row_at(d):
        return lax.rem(row + d, ROWS)

    def chip_at(d):
        return lax.rem(chip + d, CHIPS)

    def col_at(d):
        return lax.rem(col + d, COLS)

    def at_xyz(x, y, z):
        return x * 2 + lax.div(z, 2), (y * 2 + lax.rem(z, 2)) * 2 + core

    mine = pl.ds(pl.multiple_of(core * FEAT, 64), FEAT)
    local = [
        (res, x_all.at[row]),
        (w_query, wqkv.at[:, 0:QW]),
        (w_key, wqkv.at[:, QW:QW + HEAD]),
        (w_value, wqkv.at[:, QW + HEAD:QKV]),
        (attn_gain, gain_a),
        (mlp_gain, gain_m),
        (final_gain, gain_f),
        (res, res_chip.at[core]),
        (w_out, wo.at[mine]),
        (w_gate.at[core], wg.at[mine]),
        (w_up.at[core], wu.at[mine]),
        (w_down.at[core], wd.at[mine]),
        (w_head, wh.at[core]),
    ]
    local = [pltpu.make_async_copy(s, d, local_sem.at[i]) for i, (s, d) in enumerate(local)]
    for copy in local:
        copy.start()

    barrier = pltpu.get_barrier_semaphore()

    def greet(r, c):
        pl.semaphore_signal(barrier, inc=1, device_id={"row": r, "col": c}, device_id_type=MESH)

    each(1, ROWS, lambda d: greet(row_at(d), col))
    each(1, ROWS, lambda d: greet(row_at(d), sib))
    each(1, COLS, lambda d: greet(row, col_at(d)))
    cross_z = lax.rem(cz + 1 + 2 * (1 - zl), 4)
    cross_row, cross_col = at_xyz(cx, cy, cross_z)
    greet(cross_row, cross_col)
    pl.semaphore_wait(barrier, 2 * (ROWS - 1) + (COLS - 1) + 1)

    def x_copy(d):
        return remote(res, x_all.at[row], x_s.at[d], x_r.at[d], row_at(d), col)

    each(1, ROWS, lambda d: x_copy(d).start())

    for i in range(4, 7):
        local[i].wait()
    mg[core] = gain_m[...].reshape(1, FEAT)
    fg[core] = gain_f[...].reshape(1, FEAT)
    swaps = [
        (res, res_chip.at[core]),
        (mg.at[core], mg.at[core]),
        (fg.at[core], fg.at[core]),
        (w_out, wo.at[mine]),
        (w_gate.at[other], wg.at[mine]),
        (w_up.at[other], wu.at[mine]),
        (w_down.at[other], wd.at[mine]),
        (w_head, wh.at[core]),
    ]
    swaps = [remote(s, d, swap_send.at[i], swap_recv.at[i], row, sib) for i, (s, d) in enumerate(swaps)]
    for copy in swaps:
        copy.start()

    own_token = COLS * col + lax.broadcasted_iota(jnp.int32, (16, HEAD), 0)
    position = layout_of(lens, own_token)[1].astype(F32)
    lane = lax.broadcasted_iota(jnp.int32, (16, HEAD), 1)
    low_half = lane < HEAD // 2
    frequency = jnp.exp(jnp.where(low_half, lane, lane - HEAD // 2).astype(F32) * (-2.0 * math.log(ROPE_BASE) / HEAD))
    angle = position * frequency
    cosine = jnp.cos(angle)
    sine = jnp.where(low_half, -jnp.sin(angle), jnp.sin(angle))

    for i in range(4):
        local[i].wait()
    each(1, ROWS, lambda d: x_copy(d).wait_recv())

    x = x_all[...].reshape(T, FEAT).astype(F32)
    square_hi, square_lo = split_sum(jnp.sum(x * x, axis=1, keepdims=True), 64)
    xg = (x * gain_a[...].reshape(1, FEAT)).astype(BF16)
    part = jnp.dot(xg, wqkv[...], preferred_element_type=F32).astype(BF16)
    part_send[:, :, 0:QKV] = part.reshape(COLS, 16, QKV)
    part_send[:, :, QKV:QKV + 64] = square_hi.reshape(COLS, 16, 64)
    part_send[:, :, QKV + 64:QKV + 128] = square_lo.reshape(COLS, 16, 64)

    def part_copy(d):
        c = col_at(d)
        return remote(part_send.at[c], part_recv.at[d], part_s.at[d], part_r.at[d], row, c)

    each(1, COLS, lambda d: part_copy(d).start())
    part_recv[0] = part_send[col]
    each(1, COLS, lambda d: part_copy(d).wait_recv())

    total = jnp.sum(part_recv[...].astype(F32), axis=0)
    scale = inverse_rms(total[:, QKV:QKV + 1] + total[:, QKV + 64:QKV + 65])
    for h in range(Q_HEADS + 1):
        head = total[:, h * HEAD:(h + 1) * HEAD] * scale
        turned = head * cosine + pltpu.roll(head, HEAD // 2, 1) * sine
        qkv_all[chip, core, :, h * HEAD:(h + 1) * HEAD] = turned.astype(BF16)
    qkv_all[chip, core, :, QW + HEAD:QKV] = (total[:, QW + HEAD:QKV] * scale).astype(BF16)

    own_qkv = qkv_all.at[chip, core]
    own_kv = qkv_all.at[chip, core, :, QW:QKV]

    def qkv_copy(d):
        return remote(own_qkv, own_qkv, qkv_s.at[d], qkv_r.at[d], row, chip_at(d) * 2 + core)

    def kv_copy(d):
        return remote(own_kv, own_kv, qkv_s.at[CHIPS + d], qkv_r.at[CHIPS + d], row, chip_at(d) * 2 + other)

    each(1, CHIPS, lambda d: qkv_copy(d).start())
    each(0, CHIPS, lambda d: kv_copy(d).start())

    row_i = lax.broadcasted_iota(jnp.int32, (T // 2, 1), 0)
    q_token = lax.div(row_i, 16) * 32 + core * 16 + lax.rem(row_i, 16)
    k_token = lax.broadcasted_iota(jnp.int32, (1, T), 1)
    q_segment = layout_of(lens, q_token)[0]
    k_segment = layout_of(lens, k_token)[0]
    allowed = (q_segment == k_segment) & (k_token <= q_token)

    each(1, CHIPS, lambda d: qkv_copy(d).wait_recv())
    each(0, CHIPS, lambda d: kv_copy(d).wait_recv())

    keys = qkv_all[:, :, :, QW:QW + HEAD].reshape(T, HEAD)
    values = qkv_all[:, :, :, QW + HEAD:QKV].reshape(T, HEAD)
    for h in range(Q_HEADS):
        query = qkv_all[:, core, :, h * HEAD:(h + 1) * HEAD].reshape(T // 2, HEAD)
        scores = dot_nt(query, keys)
        scores = jnp.where(allowed, scores * HEAD ** (-0.5), MASKED)
        weights = jnp.exp(scores - jnp.max(scores, axis=1, keepdims=True))
        weights = (weights / jnp.sum(weights, axis=1, keepdims=True)).astype(BF16)
        result = jnp.dot(weights, values, preferred_element_type=F32)
        attended[:, h * HEAD:(h + 1) * HEAD] = result.astype(BF16)

    for i in range(7, 9):
        local[i].wait()
    for i in range(0, 4):
        swaps[i].wait_recv()
    proj_send[...] = dot_nt(attended[...], wo[...]).astype(BF16).reshape(ROWS, 16, CHIP)

    def proj_copy(d):
        r = row_at(d)
        return remote(proj_send.at[r], proj_recv.at[d], proj_s.at[d], proj_r.at[d], r, col)

    each(1, ROWS, lambda d: proj_copy(d).start())
    proj_recv[0] = proj_send[row]
    each(1, ROWS, lambda d: proj_copy(d).wait_recv())
    half_rows = pl.ds(pl.multiple_of(core * 16, 16), 16)
    residual = jnp.concatenate([res_chip[0, half_rows, :], res_chip[1, half_rows, :]], axis=1).astype(F32)
    stream_all[row, core] = (residual + jnp.sum(proj_recv[...].astype(F32), axis=0)).astype(BF16)

    own_stream = stream_all.at[row, core]

    def stream_copy(d):
        return remote(own_stream, own_stream, stream_s.at[d], stream_r.at[d], row_at(d), col)

    def stream_cross(d):
        return remote(own_stream, own_stream, stream_s.at[ROWS + d], stream_r.at[ROWS + d], row_at(d), sib)

    each(1, ROWS, lambda d: stream_copy(d).start())
    each(0, ROWS, lambda d: stream_cross(d).start())
    for i in range(9, 12):
        local[i].wait()
    for i in range(4, 6):
        swaps[i].wait_recv()
    each(1, ROWS, lambda d: stream_copy(d).wait_recv())
    each(0, ROWS, lambda d: stream_cross(d).wait_recv())

    stream = stream_all[...].reshape(T, CHIP).astype(F32)
    square_hi, square_lo = split_sum(jnp.sum(stream * stream, axis=1, keepdims=True), FFP - FF)
    gain = jnp.concatenate([mg[0], mg[1]], axis=1)
    xg = (stream * gain).astype(BF16)

    def gu_copy(kind, send, recv, d):
        c = chip_at(d)
        return remote(
            send.at[c], recv.at[d], gu_s.at[kind, d], gu_r.at[kind, d], row, c * 2 + core
        )

    gate_send[:, :, 0:FF] = jnp.dot(xg, wg[...], preferred_element_type=F32).astype(BF16).reshape(CHIPS, 32, FF)
    gate_send[:, :, FF:FFP] = square_hi.reshape(CHIPS, 32, FFP - FF)
    each(1, CHIPS, lambda d: gu_copy(0, gate_send, gate_recv, d).start())
    up_send[:, :, 0:FF] = jnp.dot(xg, wu[...], preferred_element_type=F32).astype(BF16).reshape(CHIPS, 32, FF)
    up_send[:, :, FF:FFP] = square_lo.reshape(CHIPS, 32, FFP - FF)
    each(1, CHIPS, lambda d: gu_copy(1, up_send, up_recv, d).start())
    gate_recv[0] = gate_send[chip]
    up_recv[0] = up_send[chip]
    each(1, CHIPS, lambda d: gu_copy(0, gate_send, gate_recv, d).wait_recv())
    each(1, CHIPS, lambda d: gu_copy(1, up_send, up_recv, d).wait_recv())
    gate_sum = jnp.sum(gate_recv[...].astype(F32), axis=0)
    up_sum = jnp.sum(up_recv[...].astype(F32), axis=0)
    scale = inverse_rms(gate_sum[:, FF:FF + 1] + up_sum[:, FF:FF + 1])
    gate = gate_sum[:, 0:FF] * scale
    hidden_all[chip] = (gate / (1.0 + jnp.exp(-gate)) * (up_sum[:, 0:FF] * scale)).astype(BF16)

    own_hidden = hidden_all.at[chip]

    def hid_copy(d):
        return remote(own_hidden, own_hidden, hid_s.at[d], hid_r.at[d], row, chip_at(d) * 2 + core)

    each(1, CHIPS, lambda d: hid_copy(d).start())
    swaps[6].wait_recv()
    each(1, CHIPS, lambda d: hid_copy(d).wait_recv())

    hidden = hidden_all[...].reshape(T, FF)
    down_send[...] = dot_nt(hidden, wd[...]).astype(BF16).reshape(ROWS, 32, CHIP)

    def down_copy(d):
        r = row_at(d)
        return remote(down_send.at[r], down_recv.at[d], down_s.at[d], down_r.at[d], r, col)

    each(1, ROWS, lambda d: down_copy(d).start())
    down_recv[0] = down_send[row]
    each(1, ROWS, lambda d: down_copy(d).wait_recv())
    final = stream_all[row].reshape(32, CHIP).astype(F32) + jnp.sum(down_recv[...].astype(F32), axis=0)
    square_hi, square_lo = split_sum(jnp.sum(final * final, axis=1, keepdims=True), 64)
    final = (final * jnp.concatenate([fg[0], fg[1]], axis=1)).astype(BF16)

    fin_a[cy, zl, cx, zh] = final[:, 0:256]
    fin_b[cy, zl, cx, zh] = final[:, 256:512]
    fin_c[cy, zl, cx, zh, :, 0:128] = final[:, 512:640]
    fin_c[cy, zl, cx, zh, :, 128:192] = square_hi
    fin_c[cy, zl, cx, zh, :, 192:256] = square_lo

    parts = (fin_a, fin_b, fin_c)
    orders = ("zyx", "xzy", "yxz")

    def axis_copies(p, stage):
        order = orders[p]
        axis, done = order[stage], order[:stage]
        one = {"y": pl.ds(cy, 1), "x": pl.ds(cx, 1), "zl": pl.ds(zl, 1), "zh": pl.ds(zh, 1)}
        full = {"y": pl.ds(0, 4), "x": pl.ds(0, 4), "zl": pl.ds(0, 2), "zh": pl.ds(0, 2)}
        pick = {k: full[k] if k[0] in done else one[k] for k in one}
        ref = parts[p].at[pick["y"], pick["zl"], pick["x"], pick["zh"]]
        copies = []
        for d in (2, 1, 3):
            x = lax.rem(cx + d, 4) if axis == "x" else cx
            y = lax.rem(cy + d, 4) if axis == "y" else cy
            z = lax.rem(cz + d, 4) if axis == "z" else cz
            r, c = at_xyz(x, y, z)
            i = (p * 3 + stage) * 3 + d - 1
            copies.append(remote(ref, ref, fin_s.at[i], fin_r.at[i], r, c))
        return copies

    gathers = [[axis_copies(p, stage) for p in range(3)] for stage in range(3)]
    for stage in range(3):
        for p in range(3):
            if stage:
                for copy in gathers[stage - 1][p]:
                    copy.wait_recv()
            for copy in gathers[stage][p]:
                copy.start()
    local[12].wait()
    swaps[7].wait_recv()
    diagonal = lax.broadcasted_iota(jnp.int32, (T, T), 0) == lax.broadcasted_iota(jnp.int32, (T, T), 1)
    target = jnp.sum(jnp.where(diagonal, targets[...].astype(F32), 0.0), axis=1, keepdims=True).astype(jnp.int32)
    for p in range(3):
        for copy in gathers[2][p]:
            copy.wait_recv()

    square = jnp.zeros((T, 1), F32)
    for cc in range(CHIPS):
        a = fin_a[cc // 2, cc % 2].reshape(T, 256)
        b = fin_b[cc // 2, cc % 2].reshape(T, 256)
        c = fin_c[cc // 2, cc % 2].reshape(T, 256)
        square = square + c[:, 128:129].astype(F32) + c[:, 192:193].astype(F32)
        base = cc * CHIP
        for j in range(2):
            product = jnp.dot(a, wh[j, base:base + 256], preferred_element_type=F32)
            product += jnp.dot(b, wh[j, base + 256:base + 512], preferred_element_type=F32)
            product += jnp.dot(c[:, 0:128], wh[j, base + 512:base + 640], preferred_element_type=F32)
            if cc == 0:
                logits[j] = product
            else:
                logits[j] = logits[j] + product
    scale = inverse_rms(square)
    both = [logits[j] * scale for j in range(2)]
    top = jnp.maximum(*[jnp.max(l, axis=1, keepdims=True) for l in both])
    exponential = sum(jnp.sum(jnp.exp(l - top), axis=1, keepdims=True) for l in both)
    picked = jnp.zeros((T, 1), F32)
    for j in range(2):
        first = (row * COLS + chip * 2 + j) * VOCAB
        ids = first + lax.broadcasted_iota(jnp.int32, (T, VOCAB), 1)
        picked = picked + jnp.sum(jnp.where(ids == target, both[j], 0.0), axis=1, keepdims=True)
    lane = lax.broadcasted_iota(jnp.int32, (T, HEAD), 1)
    packed = jnp.where(lane == 0, top, jnp.where(lane == 1, exponential, picked))
    stat_recv[0] = jnp.transpose(packed)[0:8, :]

    def st_copy(d):
        return remote(stat_recv.at[0], stat_recv.at[d], st_s.at[d], st_r.at[d], row, chip_at(d) * 2 + core)

    each(1, CHIPS, lambda d: st_copy(d).start())
    each(1, CHIPS, lambda d: st_copy(d).wait_recv())

    def merge(blocks):
        top = jnp.max(blocks[:, 0:1, :], axis=0)
        exponential = jnp.sum(blocks[:, 1:2, :] * jnp.exp(blocks[:, 0:1, :] - top[None]), axis=0)
        return top, exponential, jnp.sum(blocks[:, 2:3, :], axis=0)

    top, exponential, picked = merge(stat_recv[...])
    line = lax.broadcasted_iota(jnp.int32, (8, T), 0)
    stat_send[...] = jnp.where(line == 0, top, jnp.where(line == 1, exponential, picked))
    own_stat = stat2_recv.at[core, row]
    stat2_recv[core, row] = stat_send[...]

    def st2_copy(d):
        return remote(stat_send, own_stat, st2_s.at[d], st2_r.at[d], row_at(d), col)

    def st2_cross(d):
        return remote(stat_send, own_stat, st2_s.at[ROWS + d], st2_r.at[ROWS + d], row_at(d), sib)

    each(1, ROWS, lambda d: st2_copy(d).start())
    each(0, ROWS, lambda d: st2_cross(d).start())
    each(1, ROWS, lambda d: st2_copy(d).wait_recv())
    each(0, ROWS, lambda d: st2_cross(d).wait_recv())
    logprob = []
    for m in range(2):
        top, exponential, picked = merge(stat2_recv[m])
        logprob.append(picked - (top + jnp.log(exponential)))
    difference = logprob[0] - logprob[1]
    hit = line == k_segment
    sums = jnp.sum(jnp.where(hit, difference, 0.0), axis=1, keepdims=True)
    length = jnp.sum(jnp.where(hit, 1.0, 0.0), axis=1, keepdims=True)
    square8 = lax.broadcasted_iota(jnp.int32, (8, 8), 0) == lax.broadcasted_iota(jnp.int32, (8, 8), 1)
    out[...] = jnp.sum(jnp.where(square8, sums / length, 0.0), axis=0, keepdims=True)

    each(1, ROWS, lambda d: x_copy(d).wait_send())
    for copy in swaps:
        copy.wait_send()
    each(1, COLS, lambda d: part_copy(d).wait_send())
    each(1, CHIPS, lambda d: qkv_copy(d).wait_send())
    each(0, CHIPS, lambda d: kv_copy(d).wait_send())
    each(1, ROWS, lambda d: proj_copy(d).wait_send())
    each(1, ROWS, lambda d: stream_copy(d).wait_send())
    each(0, ROWS, lambda d: stream_cross(d).wait_send())
    each(1, CHIPS, lambda d: gu_copy(0, gate_send, gate_recv, d).wait_send())
    each(1, CHIPS, lambda d: gu_copy(1, up_send, up_recv, d).wait_send())
    each(1, CHIPS, lambda d: hid_copy(d).wait_send())
    each(1, ROWS, lambda d: down_copy(d).wait_send())
    for stage in gathers:
        for copies in stage:
            for copy in copies:
                copy.wait_send()
    each(1, CHIPS, lambda d: st_copy(d).wait_send())
    each(1, ROWS, lambda d: st2_copy(d).wait_send())
    each(0, ROWS, lambda d: st2_cross(d).wait_send())


def per_device(
    residual, attn_gain, w_query, w_key, w_value, w_out, mlp_gain, w_gate, w_up, w_down, final_gain, w_head,
    seq_lengths, targets,
):
    anywhere = pl.BlockSpec(memory_space=pl.ANY)
    vmem = pl.BlockSpec(memory_space=pltpu.VMEM)
    smem = pl.BlockSpec(memory_space=pltpu.SMEM)
    dma = pltpu.SemaphoreType.DMA
    result = pl.pallas_call(
        kernel,
        out_shape=jax.ShapeDtypeStruct((1, SEQS), F32),
        in_specs=[anywhere] * 12 + [smem, vmem],
        out_specs=vmem,
        scratch_shapes=[
            pltpu.VMEM((ROWS, 32, FEAT), BF16),
            pltpu.VMEM((2, 32, FEAT), BF16),
            pltpu.VMEM((FEAT, QKV), BF16),
            pltpu.VMEM((CHIP, QW), BF16),
            pltpu.VMEM((CHIP, FF), BF16),
            pltpu.VMEM((CHIP, FF), BF16),
            pltpu.VMEM((CHIP, FF), BF16),
            pltpu.VMEM((2, D, VOCAB), BF16),
            pltpu.VMEM((FEAT,), F32),
            pltpu.VMEM((FEAT,), F32),
            pltpu.VMEM((FEAT,), F32),
            pltpu.VMEM((2, 1, FEAT), F32),
            pltpu.VMEM((2, 1, FEAT), F32),
            pltpu.VMEM((COLS, 16, QKV + 128), BF16),
            pltpu.VMEM((COLS, 16, QKV + 128), BF16),
            pltpu.VMEM((CHIPS, 2, 16, QKV), BF16),
            pltpu.VMEM((T // 2, QW), BF16),
            pltpu.VMEM((ROWS, 16, CHIP), BF16),
            pltpu.VMEM((ROWS, 16, CHIP), BF16),
            pltpu.VMEM((ROWS, 2, 16, CHIP), BF16),
            pltpu.VMEM((CHIPS, 32, FFP), BF16),
            pltpu.VMEM((CHIPS, 32, FFP), BF16),
            pltpu.VMEM((CHIPS, 32, FFP), BF16),
            pltpu.VMEM((CHIPS, 32, FFP), BF16),
            pltpu.VMEM((CHIPS, 32, FF), BF16),
            pltpu.VMEM((ROWS, 32, CHIP), BF16),
            pltpu.VMEM((ROWS, 32, CHIP), BF16),
            pltpu.VMEM((4, 2, 4, 2, 32, 256), BF16),
            pltpu.VMEM((4, 2, 4, 2, 32, 256), BF16),
            pltpu.VMEM((4, 2, 4, 2, 32, 256), BF16),
            pltpu.VMEM((2, T, VOCAB), F32),
            pltpu.VMEM((8, T), F32),
            pltpu.VMEM((CHIPS, 8, T), F32),
            pltpu.VMEM((2, ROWS, 8, T), F32),
            dma((13,)), dma((8,)), dma((8,)),
            dma((ROWS,)), dma((ROWS,)),
            dma((COLS,)), dma((COLS,)),
            dma((COLS,)), dma((COLS,)),
            dma((ROWS,)), dma((ROWS,)),
            dma((2 * ROWS,)), dma((2 * ROWS,)),
            dma((2, CHIPS)), dma((2, CHIPS)),
            dma((CHIPS,)), dma((CHIPS,)),
            dma((ROWS,)), dma((ROWS,)),
            dma((27,)), dma((27,)),
            dma((CHIPS,)), dma((CHIPS,)),
            dma((2 * ROWS,)), dma((2 * ROWS,)),
        ],
        compiler_params=pltpu.CompilerParams(
            collective_id=0, has_side_effects=True, vmem_limit_bytes=60 * 1024 * 1024
        ),
    )(
        residual, attn_gain, w_query, w_key, w_value, w_out.T, mlp_gain, w_gate, w_up,
        jnp.swapaxes(w_down, 1, 2), final_gain, w_head, seq_lengths, targets.reshape(1, T),
    )
    return result.reshape(SEQS)


def solution(mesh):
    placed = (
        P("row", "col"), P("col"), P("col", "row"), P("col", "row"), P("col", "row"), P("row", "col"), P("col"),
        P(None, "col", "row"), P(None, "col", "row"), P(None, "row", "col"), P("col"), P(None, ("row", "col")), P(), P(),
    )
    return jax.shard_map(per_device, mesh=mesh, in_specs=placed, out_specs=P(), check_vma=False)
```

```python
import math

import jax
import jax.numpy as jnp
from jax import lax
from jax.experimental import pallas as pl
from jax.experimental.pallas import tpu as pltpu
from jax.sharding import PartitionSpec as P

T = 256
D = 5120
HEAD = 128
Q_HEADS = 5
QW = Q_HEADS * HEAD
QKV = QW + 2 * HEAD
SEQS = 8
FEAT = 320
CHIP = 2 * FEAT
FF = 1728
FFP = 1792
VOCAB = 640
ROWS = 8
COLS = 16
CHIPS = 8
EPSILON = 1e-06
ROPE_BASE = 1000000.0
MASKED = -1e30
MESH = pl.DeviceIdType.MESH
F32 = jnp.float32
BF16 = jnp.bfloat16


def remote(src, dst, send, recv, row, col):
    return pltpu.make_async_remote_copy(
        src_ref=src, dst_ref=dst, send_sem=send, recv_sem=recv,
        device_id={"row": row, "col": col}, device_id_type=MESH,
    )


def each(start, stop, body):
    def step(i, carry):
        body(i)
        return carry

    lax.fori_loop(start, stop, step, 0)


def dot_nt(a, b):
    return lax.dot_general(a, b, (((1,), (1,)), ((), ())), preferred_element_type=F32)


def split_sum(total, width):
    high = total.astype(BF16)
    low = (total - high.astype(F32)).astype(BF16)
    shape = (total.shape[0], width)
    return (
        jnp.broadcast_to(high.astype(F32), shape).astype(BF16),
        jnp.broadcast_to(low.astype(F32), shape).astype(BF16),
    )


def inverse_rms(total):
    return lax.rsqrt(total / D + EPSILON)


def layout_of(lens_ref, token):
    segment = jnp.zeros_like(token)
    start = jnp.zeros_like(token)
    end = jnp.int32(0)
    for s in range(SEQS):
        length = lens_ref[s]
        end = end + length
        before = end <= token
        segment = segment + jnp.where(before, 1, 0)
        start = start + jnp.where(before, length, 0)
    return segment, token - start


def kernel(
    res, attn_gain, w_query, w_key, w_value, w_out, mlp_gain, w_gate, w_up, w_down, final_gain, w_head, lens, targets,
    out,
    res_chip, square_all, x_all, wqkv, wo, wg, wu, wd, wh, gain_a, gain_m, gain_f, mg, fg,
    part_own, part_pair, part_send, part_recv, qkv_all, attended, proj_send, proj_recv, stream_all,
    gate_send, gate_recv, up_send, up_recv, hidden_all, down_send, down_recv,
    fin_a, fin_b, fin_c, logits, stat_send, stat_recv, stat2_recv,
    local_sem, swap_send, swap_recv, sq_s, sq_r, x_s, x_r, pair_s, pair_r, part_s, part_r, qkv_s, qkv_r, proj_s, proj_r,
    stream_s, stream_r, gu_s, gu_r, hid_s, hid_r, down_s, down_r, fin_s, fin_r, st_s, st_r, st2_s, st2_r,
):
    row, col = lax.axis_index("row"), lax.axis_index("col")
    core = lax.rem(col, 2)
    other = 1 - core
    chip = lax.div(col, 2)
    cx, zh = lax.div(row, 2), lax.rem(row, 2)
    cy, zl = lax.div(chip, 2), lax.rem(chip, 2)
    cz = zh * 2 + zl
    sib = chip * 2 + other

    def row_at(d):
        return lax.rem(row + d, ROWS)

    def chip_at(d):
        return lax.rem(chip + d, CHIPS)

    def col_at(d):
        return lax.rem(col + d, COLS)

    def at_xyz(x, y, z):
        return x * 2 + lax.div(z, 2), (y * 2 + lax.rem(z, 2)) * 2 + core

    mine = pl.ds(pl.multiple_of(core * FEAT, 64), FEAT)
    waits, pending, numbers = {}, [], {"own": 0, "pair": 0}

    def own(name, src, dst):
        copy = pltpu.make_async_copy(src, dst, local_sem.at[numbers["own"]])
        numbers["own"] += 1
        copy.start()
        waits.setdefault(name, []).append(copy.wait)

    def swap(name, src, dst):
        i = numbers["pair"]
        numbers["pair"] += 1
        copy = remote(src, dst, swap_send.at[i], swap_recv.at[i], row, sib)
        copy.start()
        waits.setdefault(name, []).append(copy.wait_recv)
        pending.append(copy.wait_send)

    def ready(*names):
        for name in names:
            for wait in waits.pop(name):
                wait()

    def start(first, stop, copy):
        each(first, stop, lambda d: copy(d).start())
        pending.append(lambda: each(first, stop, lambda d: copy(d).wait_send()))

    def arrive(first, stop, copy):
        each(first, stop, lambda d: copy(d).wait_recv())

    def flush():
        for finish in pending:
            finish()
        pending.clear()

    own("residual", res, res_chip.at[core])
    own("gains", attn_gain, gain_a)
    own("gains", mlp_gain, gain_m)
    own("gains", final_gain, gain_f)
    own("wqkv", w_query, wqkv.at[:, 0:QW])
    own("wqkv", w_key, wqkv.at[:, QW:QW + HEAD])
    own("wqkv", w_value, wqkv.at[:, QW + HEAD:QKV])

    barrier = pltpu.get_barrier_semaphore()

    def greet(r, c):
        pl.semaphore_signal(barrier, inc=1, device_id={"row": r, "col": c}, device_id_type=MESH)

    each(1, ROWS, lambda d: greet(row_at(d), col))
    each(1, ROWS, lambda d: greet(row_at(d), sib))
    each(1, COLS, lambda d: greet(row, col_at(d)))
    cross_z = lax.rem(cz + 1 + 2 * (1 - zl), 4)
    cross_row, cross_col = at_xyz(cx, cy, cross_z)
    greet(cross_row, cross_col)
    pl.semaphore_wait(barrier, 2 * (ROWS - 1) + (COLS - 1) + 1)

    ready("residual", "gains")
    x = res_chip[core].astype(F32)
    eye = lax.broadcasted_iota(jnp.int32, (32, HEAD), 0) == lax.broadcasted_iota(jnp.int32, (32, HEAD), 1)
    square = jnp.sum(jnp.where(eye, jnp.sum(x * x, axis=1, keepdims=True), 0.0), axis=0, keepdims=True)
    square_all[0] = jnp.broadcast_to(square, (8, HEAD))

    def sq_copy(d):
        return remote(square_all.at[0], square_all.at[d], sq_s.at[d], sq_r.at[d], row, col_at(d))

    start(1, COLS, sq_copy)
    mg[core] = gain_m[...].reshape(1, FEAT)
    fg[core] = gain_f[...].reshape(1, FEAT)

    own_token = COLS * col + lax.broadcasted_iota(jnp.int32, (16, HEAD), 0)
    position = layout_of(lens, own_token)[1].astype(F32)
    lane = lax.broadcasted_iota(jnp.int32, (16, HEAD), 1)
    low_half = lane < HEAD // 2
    frequency = jnp.exp(jnp.where(low_half, lane, lane - HEAD // 2).astype(F32) * (-2.0 * math.log(ROPE_BASE) / HEAD))
    angle = position * frequency
    cosine = jnp.cos(angle)
    sine = jnp.where(low_half, -jnp.sin(angle), jnp.sin(angle))

    arrive(1, COLS, sq_copy)
    square = jnp.sum(square_all[...], axis=0)[0:1]
    square = jnp.sum(jnp.where(eye, square, 0.0), axis=1, keepdims=True)
    x_all[row] = (x * inverse_rms(square) * gain_a[...].reshape(1, FEAT)).astype(BF16)

    def x_copy(d):
        return remote(x_all.at[row], x_all.at[row], x_s.at[d], x_r.at[d], row_at(d), col)

    start(1, ROWS, x_copy)
    swap("residual_pair", res_chip.at[core], res_chip.at[core])
    swap("gains_pair", mg.at[core], mg.at[core])
    swap("gains_pair", fg.at[core], fg.at[core])
    own("wo", w_out, wo.at[mine])
    swap("wo", w_out, wo.at[mine])
    ready("wqkv")
    arrive(1, ROWS, x_copy)

    part = jnp.dot(x_all[...].reshape(T, FEAT), wqkv[...], preferred_element_type=F32)
    part_own[...] = part.reshape(CHIPS, 2, 16, QKV)
    pair = remote(part_own.at[:, other], part_pair, pair_s, pair_r, row, sib)
    pair.start()
    pending.append(pair.wait_send)
    pair.wait_recv()
    part_send[...] = part_own[:, core] + part_pair[...]

    def part_copy(d):
        c = chip_at(d)
        return remote(part_send.at[c], part_recv.at[d], part_s.at[d], part_r.at[d], row, c * 2 + core)

    start(1, CHIPS, part_copy)
    own("wg", w_gate.at[core], wg.at[mine])
    own("wu", w_up.at[core], wu.at[mine])
    swap("wg", w_gate.at[other], wg.at[mine])
    swap("wu", w_up.at[other], wu.at[mine])
    part_recv[0] = part_send[chip]
    arrive(1, CHIPS, part_copy)

    total = jnp.sum(part_recv[...], axis=0)
    for h in range(Q_HEADS + 1):
        head = total[:, h * HEAD:(h + 1) * HEAD]
        turned = head * cosine + pltpu.roll(head, HEAD // 2, 1) * sine
        qkv_all[chip, core, :, h * HEAD:(h + 1) * HEAD] = turned.astype(BF16)
    qkv_all[chip, core, :, QW + HEAD:QKV] = total[:, QW + HEAD:QKV].astype(BF16)

    own_qkv = qkv_all.at[chip, core]
    own_kv = qkv_all.at[chip, core, :, QW:QKV]

    def qkv_copy(d):
        return remote(own_qkv, own_qkv, qkv_s.at[d], qkv_r.at[d], row, chip_at(d) * 2 + core)

    def kv_copy(d):
        return remote(own_kv, own_kv, qkv_s.at[CHIPS + d], qkv_r.at[CHIPS + d], row, chip_at(d) * 2 + other)

    start(1, CHIPS, qkv_copy)
    start(0, CHIPS, kv_copy)
    own("wd", w_down.at[core], wd.at[mine])
    swap("wd", w_down.at[other], wd.at[mine])

    row_i = lax.broadcasted_iota(jnp.int32, (T // 2, 1), 0)
    q_token = lax.div(row_i, 16) * 32 + core * 16 + lax.rem(row_i, 16)
    k_token = lax.broadcasted_iota(jnp.int32, (1, T), 1)
    q_segment = layout_of(lens, q_token)[0]
    k_segment = layout_of(lens, k_token)[0]
    allowed = (q_segment == k_segment) & (k_token <= q_token)

    arrive(1, CHIPS, qkv_copy)
    arrive(0, CHIPS, kv_copy)

    keys = qkv_all[:, :, :, QW:QW + HEAD].reshape(T, HEAD)
    values = qkv_all[:, :, :, QW + HEAD:QKV].reshape(T, HEAD)
    for h in range(Q_HEADS):
        query = qkv_all[:, core, :, h * HEAD:(h + 1) * HEAD].reshape(T // 2, HEAD)
        scores = dot_nt(query, keys)
        scores = jnp.where(allowed, scores * HEAD ** (-0.5), MASKED)
        weights = jnp.exp(scores - jnp.max(scores, axis=1, keepdims=True))
        weights = (weights / jnp.sum(weights, axis=1, keepdims=True)).astype(BF16)
        result = jnp.dot(weights, values, preferred_element_type=F32)
        attended[:, h * HEAD:(h + 1) * HEAD] = result.astype(BF16)

    ready("wo", "residual_pair")
    proj_send[...] = dot_nt(attended[...], wo[...]).reshape(ROWS, 16, CHIP)

    def proj_copy(d):
        r = row_at(d)
        return remote(proj_send.at[r], proj_recv.at[d], proj_s.at[d], proj_r.at[d], r, col)

    start(1, ROWS, proj_copy)
    proj_recv[0] = proj_send[row]
    arrive(1, ROWS, proj_copy)
    half_rows = pl.ds(pl.multiple_of(core * 16, 16), 16)
    residual = jnp.concatenate([res_chip[0, half_rows, :], res_chip[1, half_rows, :]], axis=1).astype(F32)
    stream_all[row, core] = (residual + jnp.sum(proj_recv[...], axis=0)).astype(BF16)

    own_stream = stream_all.at[row, core]

    def stream_copy(d):
        return remote(own_stream, own_stream, stream_s.at[d], stream_r.at[d], row_at(d), col)

    def stream_cross(d):
        return remote(own_stream, own_stream, stream_s.at[ROWS + d], stream_r.at[ROWS + d], row_at(d), sib)

    start(1, ROWS, stream_copy)
    start(0, ROWS, stream_cross)
    own("wh", w_head, wh.at[core])
    swap("wh", w_head, wh.at[core])
    wh_at = len(pending) - 1
    ready("wg", "wu", "gains_pair")
    arrive(1, ROWS, stream_copy)
    arrive(0, ROWS, stream_cross)

    stream = stream_all[...].reshape(T, CHIP).astype(F32)
    square_hi, square_lo = split_sum(jnp.sum(stream * stream, axis=1, keepdims=True), FFP - FF)
    gain = jnp.concatenate([mg[0], mg[1]], axis=1)
    xg = (stream * gain).astype(BF16)

    def gu_copy(kind, send, recv, d):
        c = chip_at(d)
        return remote(
            send.at[c], recv.at[d], gu_s.at[kind, d], gu_r.at[kind, d], row, c * 2 + core
        )

    gate_send[:, :, 0:FF] = jnp.dot(xg, wg[...], preferred_element_type=F32).astype(BF16).reshape(CHIPS, 32, FF)
    gate_send[:, :, FF:FFP] = square_hi.reshape(CHIPS, 32, FFP - FF)
    start(1, CHIPS, lambda d: gu_copy(0, gate_send, gate_recv, d))
    up_send[:, :, 0:FF] = jnp.dot(xg, wu[...], preferred_element_type=F32).astype(BF16).reshape(CHIPS, 32, FF)
    up_send[:, :, FF:FFP] = square_lo.reshape(CHIPS, 32, FFP - FF)
    start(1, CHIPS, lambda d: gu_copy(1, up_send, up_recv, d))
    gate_recv[0] = gate_send[chip]
    up_recv[0] = up_send[chip]
    held = pending[-2:]
    del pending[-2:]
    wh_swap = [pending.pop(i) for i in (wh_at,)]
    flush()
    pending.extend(wh_swap + held)
    arrive(1, CHIPS, lambda d: gu_copy(0, gate_send, gate_recv, d))
    gate_sum = jnp.sum(gate_recv[...].astype(F32), axis=0)
    arrive(1, CHIPS, lambda d: gu_copy(1, up_send, up_recv, d))
    up_sum = jnp.sum(up_recv[...].astype(F32), axis=0)
    scale = inverse_rms(gate_sum[:, FF:FF + 1] + up_sum[:, FF:FF + 1])
    gate = gate_sum[:, 0:FF] * scale
    hidden_all[chip] = (gate / (1.0 + jnp.exp(-gate)) * (up_sum[:, 0:FF] * scale)).astype(BF16)

    own_hidden = hidden_all.at[chip]

    def hid_copy(d):
        return remote(own_hidden, own_hidden, hid_s.at[d], hid_r.at[d], row, chip_at(d) * 2 + core)

    start(1, CHIPS, hid_copy)
    ready("wd")
    arrive(1, CHIPS, hid_copy)

    hidden = hidden_all[...].reshape(T, FF)
    down_send[...] = dot_nt(hidden, wd[...]).reshape(ROWS, 32, CHIP)

    def down_copy(d):
        r = row_at(d)
        return remote(down_send.at[r], down_recv.at[d], down_s.at[d], down_r.at[d], r, col)

    start(1, ROWS, down_copy)
    down_recv[0] = down_send[row]
    arrive(1, ROWS, down_copy)
    final = stream_all[row].reshape(32, CHIP).astype(F32) + jnp.sum(down_recv[...], axis=0)
    square_hi, square_lo = split_sum(jnp.sum(final * final, axis=1, keepdims=True), 64)
    final = (final * jnp.concatenate([fg[0], fg[1]], axis=1)).astype(BF16)

    fin_a[cy, zl, cx, zh] = final[:, 0:256]
    fin_b[cy, zl, cx, zh] = final[:, 256:512]
    fin_c[cy, zl, cx, zh, :, 0:128] = final[:, 512:640]
    fin_c[cy, zl, cx, zh, :, 128:192] = square_hi
    fin_c[cy, zl, cx, zh, :, 192:256] = square_lo

    parts = (fin_a, fin_b, fin_c)
    orders = ("zyx", "xzy", "yxz")

    def axis_copies(p, stage):
        order = orders[p]
        axis, done = order[stage], order[:stage]
        one = {"y": pl.ds(cy, 1), "x": pl.ds(cx, 1), "zl": pl.ds(zl, 1), "zh": pl.ds(zh, 1)}
        full = {"y": pl.ds(0, 4), "x": pl.ds(0, 4), "zl": pl.ds(0, 2), "zh": pl.ds(0, 2)}
        pick = {k: full[k] if k[0] in done else one[k] for k in one}
        ref = parts[p].at[pick["y"], pick["zl"], pick["x"], pick["zh"]]
        copies = []
        for d in (2, 1, 3):
            x = lax.rem(cx + d, 4) if axis == "x" else cx
            y = lax.rem(cy + d, 4) if axis == "y" else cy
            z = lax.rem(cz + d, 4) if axis == "z" else cz
            r, c = at_xyz(x, y, z)
            i = (p * 3 + stage) * 3 + d - 1
            copies.append(remote(ref, ref, fin_s.at[i], fin_r.at[i], r, c))
        return copies

    gathers = [[axis_copies(p, stage) for p in range(3)] for stage in range(3)]
    for stage in range(3):
        for p in range(3):
            if stage:
                for copy in gathers[stage - 1][p]:
                    copy.wait_recv()
            for copy in gathers[stage][p]:
                copy.start()
                pending.append(copy.wait_send)
    last = pending[-9:]
    del pending[-9:]
    flush()
    pending.extend(last)
    ready("wh")
    diagonal = lax.broadcasted_iota(jnp.int32, (T, T), 0) == lax.broadcasted_iota(jnp.int32, (T, T), 1)
    target = jnp.sum(jnp.where(diagonal, targets[...].astype(F32), 0.0), axis=1, keepdims=True).astype(jnp.int32)
    for p in range(3):
        for copy in gathers[2][p]:
            copy.wait_recv()

    square = jnp.zeros((T, 1), F32)
    for y in range(4):
        pieces = []
        for z in range(2):
            c = fin_c[y, z].reshape(T, 256)
            square = square + c[:, 128:129].astype(F32) + c[:, 192:193].astype(F32)
            pieces += [fin_a[y, z].reshape(T, 256), fin_b[y, z].reshape(T, 256), c[:, 0:128]]
        states = jnp.concatenate(pieces, axis=1)
        for j in range(2):
            product = jnp.dot(states, wh[j, y * 2 * CHIP:(y + 1) * 2 * CHIP], preferred_element_type=F32)
            logits[j] = product if y == 0 else logits[j] + product
    scale = inverse_rms(square)
    both = [logits[j] * scale for j in range(2)]
    top = jnp.maximum(*[jnp.max(l, axis=1, keepdims=True) for l in both])
    exponential = sum(jnp.sum(jnp.exp(l - top), axis=1, keepdims=True) for l in both)
    picked = jnp.zeros((T, 1), F32)
    for j in range(2):
        first = (row * COLS + chip * 2 + j) * VOCAB
        ids = first + lax.broadcasted_iota(jnp.int32, (T, VOCAB), 1)
        picked = picked + jnp.sum(jnp.where(ids == target, both[j], 0.0), axis=1, keepdims=True)
    lane = lax.broadcasted_iota(jnp.int32, (T, HEAD), 1)
    packed = jnp.where(lane == 0, top, jnp.where(lane == 1, exponential, picked))
    stat_recv[0] = jnp.transpose(packed)[0:8, :]

    def st_copy(d):
        return remote(stat_recv.at[0], stat_recv.at[d], st_s.at[d], st_r.at[d], row, chip_at(d) * 2 + core)

    start(1, CHIPS, st_copy)
    arrive(1, CHIPS, st_copy)

    def merge(blocks):
        top = jnp.max(blocks[:, 0:1, :], axis=0)
        exponential = jnp.sum(blocks[:, 1:2, :] * jnp.exp(blocks[:, 0:1, :] - top[None]), axis=0)
        return top, exponential, jnp.sum(blocks[:, 2:3, :], axis=0)

    top, exponential, picked = merge(stat_recv[...])
    line = lax.broadcasted_iota(jnp.int32, (8, T), 0)
    stat_send[...] = jnp.where(line == 0, top, jnp.where(line == 1, exponential, picked))
    own_stat = stat2_recv.at[core, row]
    stat2_recv[core, row] = stat_send[...]

    def st2_copy(d):
        return remote(stat_send, own_stat, st2_s.at[d], st2_r.at[d], row_at(d), col)

    def st2_cross(d):
        return remote(stat_send, own_stat, st2_s.at[ROWS + d], st2_r.at[ROWS + d], row_at(d), sib)

    start(1, ROWS, st2_copy)
    start(0, ROWS, st2_cross)
    arrive(1, ROWS, st2_copy)
    arrive(0, ROWS, st2_cross)
    logprob = []
    for m in range(2):
        top, exponential, picked = merge(stat2_recv[m])
        logprob.append(picked - (top + jnp.log(exponential)))
    difference = logprob[0] - logprob[1]
    hit = line == k_segment
    sums = jnp.sum(jnp.where(hit, difference, 0.0), axis=1, keepdims=True)
    length = jnp.sum(jnp.where(hit, 1.0, 0.0), axis=1, keepdims=True)
    square8 = lax.broadcasted_iota(jnp.int32, (8, 8), 0) == lax.broadcasted_iota(jnp.int32, (8, 8), 1)
    out[...] = jnp.sum(jnp.where(square8, sums / length, 0.0), axis=0, keepdims=True)

    flush()


def per_device(
    residual, attn_gain, w_query, w_key, w_value, w_out, mlp_gain, w_gate, w_up, w_down, final_gain, w_head,
    seq_lengths, targets,
):
    anywhere = pl.BlockSpec(memory_space=pl.ANY)
    vmem = pl.BlockSpec(memory_space=pltpu.VMEM)
    smem = pl.BlockSpec(memory_space=pltpu.SMEM)
    dma = pltpu.SemaphoreType.DMA
    result = pl.pallas_call(
        kernel,
        out_shape=jax.ShapeDtypeStruct((1, SEQS), F32),
        in_specs=[anywhere] * 12 + [smem, vmem],
        out_specs=vmem,
        scratch_shapes=[
            pltpu.VMEM((2, 32, FEAT), BF16),
            pltpu.VMEM((COLS, 8, HEAD), F32),
            pltpu.VMEM((ROWS, 32, FEAT), BF16),
            pltpu.VMEM((FEAT, QKV), BF16),
            pltpu.VMEM((CHIP, QW), BF16),
            pltpu.VMEM((CHIP, FF), BF16),
            pltpu.VMEM((CHIP, FF), BF16),
            pltpu.VMEM((CHIP, FF), BF16),
            pltpu.VMEM((2, D, VOCAB), BF16),
            pltpu.VMEM((FEAT,), F32),
            pltpu.VMEM((FEAT,), F32),
            pltpu.VMEM((FEAT,), F32),
            pltpu.VMEM((2, 1, FEAT), F32),
            pltpu.VMEM((2, 1, FEAT), F32),
            pltpu.VMEM((CHIPS, 2, 16, QKV), F32),
            pltpu.VMEM((CHIPS, 16, QKV), F32),
            pltpu.VMEM((CHIPS, 16, QKV), F32),
            pltpu.VMEM((CHIPS, 16, QKV), F32),
            pltpu.VMEM((CHIPS, 2, 16, QKV), BF16),
            pltpu.VMEM((T // 2, QW), BF16),
            pltpu.VMEM((ROWS, 16, CHIP), F32),
            pltpu.VMEM((ROWS, 16, CHIP), F32),
            pltpu.VMEM((ROWS, 2, 16, CHIP), BF16),
            pltpu.VMEM((CHIPS, 32, FFP), BF16),
            pltpu.VMEM((CHIPS, 32, FFP), BF16),
            pltpu.VMEM((CHIPS, 32, FFP), BF16),
            pltpu.VMEM((CHIPS, 32, FFP), BF16),
            pltpu.VMEM((CHIPS, 32, FF), BF16),
            pltpu.VMEM((ROWS, 32, CHIP), F32),
            pltpu.VMEM((ROWS, 32, CHIP), F32),
            pltpu.VMEM((4, 2, 4, 2, 32, 256), BF16),
            pltpu.VMEM((4, 2, 4, 2, 32, 256), BF16),
            pltpu.VMEM((4, 2, 4, 2, 32, 256), BF16),
            pltpu.VMEM((2, T, VOCAB), F32),
            pltpu.VMEM((8, T), F32),
            pltpu.VMEM((CHIPS, 8, T), F32),
            pltpu.VMEM((2, ROWS, 8, T), F32),
            dma((12,)), dma((8,)), dma((8,)),
            dma((COLS,)), dma((COLS,)),
            dma((ROWS,)), dma((ROWS,)),
            dma, dma,
            dma((CHIPS,)), dma((CHIPS,)),
            dma((COLS,)), dma((COLS,)),
            dma((ROWS,)), dma((ROWS,)),
            dma((2 * ROWS,)), dma((2 * ROWS,)),
            dma((2, CHIPS)), dma((2, CHIPS)),
            dma((CHIPS,)), dma((CHIPS,)),
            dma((ROWS,)), dma((ROWS,)),
            dma((27,)), dma((27,)),
            dma((CHIPS,)), dma((CHIPS,)),
            dma((2 * ROWS,)), dma((2 * ROWS,)),
        ],
        compiler_params=pltpu.CompilerParams(
            collective_id=0, has_side_effects=True, vmem_limit_bytes=60 * 1024 * 1024
        ),
    )(
        residual, attn_gain, w_query, w_key, w_value, w_out.T, mlp_gain, w_gate, w_up,
        jnp.swapaxes(w_down, 1, 2), final_gain, w_head, seq_lengths, targets.reshape(1, T),
    )
    return result.reshape(SEQS)


def solution(mesh):
    placed = (
        P("row", "col"), P("col"), P("col", "row"), P("col", "row"), P("col", "row"), P("row", "col"), P("col"),
        P(None, "col", "row"), P(None, "col", "row"), P(None, "row", "col"), P("col"), P(None, ("row", "col")), P(), P(),
    )
    return jax.shard_map(per_device, mesh=mesh, in_specs=placed, out_specs=P(), check_vma=False)
```

```python
import math

import jax
import jax.numpy as jnp
from jax import lax
from jax.experimental import pallas as pl
from jax.experimental.pallas import tpu as pltpu
from jax.sharding import PartitionSpec as P

T = 256
D = 5120
HEAD = 128
Q_HEADS = 5
QW = Q_HEADS * HEAD
QKV = QW + 2 * HEAD
SEQS = 8
FEAT = 320
CHIP = 2 * FEAT
FF = 1728
FFP = 1792
HALF = FFP // 2
CHUNKS = ((HALF, FF - HALF), (0, HALF))
VOCAB = 640
ROWS = 8
COLS = 16
CHIPS = 8
EPSILON = 1e-06
ROPE_BASE = 1000000.0
MASKED = -1e30
MESH = pl.DeviceIdType.MESH
F32 = jnp.float32
BF16 = jnp.bfloat16


def remote(src, dst, send, recv, row, col):
    return pltpu.make_async_remote_copy(
        src_ref=src, dst_ref=dst, send_sem=send, recv_sem=recv,
        device_id={"row": row, "col": col}, device_id_type=MESH,
    )


def each(start, stop, body):
    def step(i, carry):
        body(i)
        return carry

    lax.fori_loop(start, stop, step, 0)


def dot_nt(a, b):
    return lax.dot_general(a, b, (((1,), (1,)), ((), ())), preferred_element_type=F32)


def split_sum(total, width):
    high = total.astype(BF16)
    low = (total - high.astype(F32)).astype(BF16)
    shape = (total.shape[0], width)
    return (
        jnp.broadcast_to(high.astype(F32), shape).astype(BF16),
        jnp.broadcast_to(low.astype(F32), shape).astype(BF16),
    )


def inverse_rms(total):
    return lax.rsqrt(total / D + EPSILON)


def layout_of(lens_ref, token):
    segment = jnp.zeros_like(token)
    start = jnp.zeros_like(token)
    end = jnp.int32(0)
    for s in range(SEQS):
        length = lens_ref[s]
        end = end + length
        before = end <= token
        segment = segment + jnp.where(before, 1, 0)
        start = start + jnp.where(before, length, 0)
    return segment, token - start


def kernel(
    res, attn_gain, w_query, w_key, w_value, w_out, mlp_gain, w_gate, w_up, w_down, final_gain, w_head, lens, targets,
    out,
    target_row, res_chip, square_all, x_all, wqkv, wo, wg, wu, wd, wh, gain_a, gain_m, gain_f, mg, fg,
    part_own, part_pair, part_send, part_recv, qkv_all, attended, proj_send, proj_recv, stream_all,
    gu_send, gu_recv, hidden_all, down_send, down_recv,
    fin_a, fin_b, fin_c, logits, stat_send, stat_recv, stat2_recv,
    local_sem, swap_send, swap_recv, sq_s, sq_r, x_s, x_r, pair_s, pair_r, part_s, part_r, qkv_s, qkv_r, proj_s, proj_r,
    stream_s, stream_r, gu_s, gu_r, hid_s, hid_r, down_s, down_r, fin_s, fin_r, st_s, st_r, st2_s, st2_r,
):
    row, col = lax.axis_index("row"), lax.axis_index("col")
    core = lax.rem(col, 2)
    other = 1 - core
    chip = lax.div(col, 2)
    cx, zh = lax.div(row, 2), lax.rem(row, 2)
    cy, zl = lax.div(chip, 2), lax.rem(chip, 2)
    cz = zh * 2 + zl
    sib = chip * 2 + other

    def row_at(d):
        return lax.rem(row + d, ROWS)

    def chip_at(d):
        return lax.rem(chip + d, CHIPS)

    def col_at(d):
        return lax.rem(col + d, COLS)

    def at_xyz(x, y, z):
        return x * 2 + lax.div(z, 2), (y * 2 + lax.rem(z, 2)) * 2 + core

    mine = pl.ds(pl.multiple_of(core * FEAT, 64), FEAT)
    waits, pending, numbers = {}, [], {"own": 0, "pair": 0}

    def own(name, src, dst):
        copy = pltpu.make_async_copy(src, dst, local_sem.at[numbers["own"]])
        numbers["own"] += 1
        copy.start()
        waits.setdefault(name, []).append(copy.wait)

    def swap(name, src, dst):
        i = numbers["pair"]
        numbers["pair"] += 1
        copy = remote(src, dst, swap_send.at[i], swap_recv.at[i], row, sib)
        copy.start()
        waits.setdefault(name, []).append(copy.wait_recv)
        pending.append(copy.wait_send)

    def ready(*names):
        for name in names:
            for wait in waits.pop(name):
                wait()

    def start(first, stop, copy):
        each(first, stop, lambda d: copy(d).start())
        pending.append(lambda: each(first, stop, lambda d: copy(d).wait_send()))

    def arrive(first, stop, copy):
        each(first, stop, lambda d: copy(d).wait_recv())

    def flush():
        for finish in pending:
            finish()
        pending.clear()

    own("residual", res, res_chip.at[core])
    own("targets", targets, target_row)
    own("gains", attn_gain, gain_a)
    own("gains", mlp_gain, gain_m)
    own("gains", final_gain, gain_f)
    own("wqkv", w_query, wqkv.at[:, 0:QW])
    own("wqkv", w_key, wqkv.at[:, QW:QW + HEAD])
    own("wqkv", w_value, wqkv.at[:, QW + HEAD:QKV])

    barrier = pltpu.get_barrier_semaphore()

    def greet(r, c):
        pl.semaphore_signal(barrier, inc=1, device_id={"row": r, "col": c}, device_id_type=MESH)

    each(1, ROWS, lambda d: greet(row_at(d), col))
    each(1, ROWS, lambda d: greet(row_at(d), sib))
    each(1, COLS, lambda d: greet(row, col_at(d)))
    cross_z = lax.rem(cz + 1 + 2 * (1 - zl), 4)
    cross_row, cross_col = at_xyz(cx, cy, cross_z)
    greet(cross_row, cross_col)
    pl.semaphore_wait(barrier, 2 * (ROWS - 1) + (COLS - 1) + 1)

    ready("residual", "gains")
    x = res_chip[core].astype(F32)
    eye = lax.broadcasted_iota(jnp.int32, (32, HEAD), 0) == lax.broadcasted_iota(jnp.int32, (32, HEAD), 1)
    square = jnp.sum(jnp.where(eye, jnp.sum(x * x, axis=1, keepdims=True), 0.0), axis=0, keepdims=True)
    square_all[0] = jnp.broadcast_to(square, (8, HEAD))

    def sq_copy(d):
        return remote(square_all.at[0], square_all.at[d], sq_s.at[d], sq_r.at[d], row, col_at(d))

    start(1, COLS, sq_copy)
    mg[core] = gain_m[...].reshape(1, FEAT)
    fg[core] = gain_f[...].reshape(1, FEAT)

    own_token = COLS * col + lax.broadcasted_iota(jnp.int32, (16, HEAD), 0)
    position = layout_of(lens, own_token)[1].astype(F32)
    lane = lax.broadcasted_iota(jnp.int32, (16, HEAD), 1)
    low_half = lane < HEAD // 2
    frequency = jnp.exp(jnp.where(low_half, lane, lane - HEAD // 2).astype(F32) * (-2.0 * math.log(ROPE_BASE) / HEAD))
    angle = position * frequency
    cosine = jnp.cos(angle)
    sine = jnp.where(low_half, -jnp.sin(angle), jnp.sin(angle))

    arrive(1, COLS, sq_copy)
    square = jnp.sum(square_all[...], axis=0)[0:1]
    square = jnp.sum(jnp.where(eye, square, 0.0), axis=1, keepdims=True)
    x_all[row] = (x * inverse_rms(square) * gain_a[...].reshape(1, FEAT)).astype(BF16)

    def x_copy(d):
        return remote(x_all.at[row], x_all.at[row], x_s.at[d], x_r.at[d], row_at(d), col)

    start(1, ROWS, x_copy)
    swap("residual_pair", res_chip.at[core], res_chip.at[core])
    swap("gains_pair", mg.at[core], mg.at[core])
    swap("gains_pair", fg.at[core], fg.at[core])
    own("wo", w_out, wo.at[mine])
    swap("wo", w_out, wo.at[mine])
    ready("wqkv")
    arrive(1, ROWS, x_copy)

    part = jnp.dot(x_all[...].reshape(T, FEAT), wqkv[...], preferred_element_type=F32)
    part_own[...] = part.reshape(CHIPS, 2, 16, QKV)
    pair = remote(part_own.at[:, other], part_pair, pair_s, pair_r, row, sib)
    pair.start()
    pending.append(pair.wait_send)
    pair.wait_recv()
    part_send[...] = part_own[:, core] + part_pair[...]

    def part_copy(d):
        c = chip_at(d)
        return remote(part_send.at[c], part_recv.at[d], part_s.at[d], part_r.at[d], row, c * 2 + core)

    start(1, CHIPS, part_copy)
    own("wg", w_gate.at[core], wg.at[mine])
    own("wu", w_up.at[core], wu.at[mine])
    swap("wg", w_gate.at[other], wg.at[mine])
    swap("wu", w_up.at[other], wu.at[mine])
    part_recv[0] = part_send[chip]
    arrive(1, CHIPS, part_copy)

    total = jnp.sum(part_recv[...], axis=0)
    for h in range(Q_HEADS + 1):
        head = total[:, h * HEAD:(h + 1) * HEAD]
        turned = head * cosine + pltpu.roll(head, HEAD // 2, 1) * sine
        qkv_all[chip, core, :, h * HEAD:(h + 1) * HEAD] = turned.astype(BF16)
    qkv_all[chip, core, :, QW + HEAD:QKV] = total[:, QW + HEAD:QKV].astype(BF16)

    own_qkv = qkv_all.at[chip, core]
    own_kv = qkv_all.at[chip, core, :, QW:QKV]

    def qkv_copy(d):
        return remote(own_qkv, own_qkv, qkv_s.at[d], qkv_r.at[d], row, chip_at(d) * 2 + core)

    def kv_copy(d):
        return remote(own_kv, own_kv, qkv_s.at[CHIPS + d], qkv_r.at[CHIPS + d], row, chip_at(d) * 2 + other)

    start(1, CHIPS, qkv_copy)
    start(0, CHIPS, kv_copy)
    own("wd", w_down.at[core], wd.at[mine])
    swap("wd", w_down.at[other], wd.at[mine])

    row_i = lax.broadcasted_iota(jnp.int32, (T // 2, 1), 0)
    q_token = lax.div(row_i, 16) * 32 + core * 16 + lax.rem(row_i, 16)
    k_token = lax.broadcasted_iota(jnp.int32, (1, T), 1)
    q_segment = layout_of(lens, q_token)[0]
    k_segment = layout_of(lens, k_token)[0]
    allowed = (q_segment == k_segment) & (k_token <= q_token)

    arrive(1, CHIPS, qkv_copy)
    arrive(0, CHIPS, kv_copy)

    keys = qkv_all[:, :, :, QW:QW + HEAD].reshape(T, HEAD)
    values = qkv_all[:, :, :, QW + HEAD:QKV].reshape(T, HEAD)
    for h in range(Q_HEADS):
        query = qkv_all[:, core, :, h * HEAD:(h + 1) * HEAD].reshape(T // 2, HEAD)
        scores = dot_nt(query, keys)
        scores = jnp.where(allowed, scores * HEAD ** (-0.5), MASKED)
        weights = jnp.exp(scores - jnp.max(scores, axis=1, keepdims=True))
        weights = (weights / jnp.sum(weights, axis=1, keepdims=True)).astype(BF16)
        result = jnp.dot(weights, values, preferred_element_type=F32)
        attended[:, h * HEAD:(h + 1) * HEAD] = result.astype(BF16)

    ready("wo", "residual_pair")
    proj_send[...] = dot_nt(attended[...], wo[...]).reshape(ROWS, 16, CHIP)

    def proj_copy(d):
        r = row_at(d)
        return remote(proj_send.at[r], proj_recv.at[d], proj_s.at[d], proj_r.at[d], r, col)

    start(1, ROWS, proj_copy)
    proj_recv[0] = proj_send[row]
    arrive(1, ROWS, proj_copy)
    half_rows = pl.ds(pl.multiple_of(core * 16, 16), 16)
    residual = jnp.concatenate([res_chip[0, half_rows, :], res_chip[1, half_rows, :]], axis=1).astype(F32)
    stream_all[row, core] = (residual + jnp.sum(proj_recv[...], axis=0)).astype(BF16)

    own_stream = stream_all.at[row, core]

    def stream_copy(d):
        return remote(own_stream, own_stream, stream_s.at[d], stream_r.at[d], row_at(d), col)

    def stream_cross(d):
        return remote(own_stream, own_stream, stream_s.at[ROWS + d], stream_r.at[ROWS + d], row_at(d), sib)

    start(1, ROWS, stream_copy)
    start(0, ROWS, stream_cross)
    own("wh", w_head, wh.at[core])
    swap("wh", w_head, wh.at[core])
    wh_at = len(pending) - 1
    ready("wg", "wu", "gains_pair")
    arrive(1, ROWS, stream_copy)
    arrive(0, ROWS, stream_cross)

    stream = stream_all[...].reshape(T, CHIP).astype(F32)
    square_hi, square_lo = split_sum(jnp.sum(stream * stream, axis=1, keepdims=True), HALF - CHUNKS[0][1])
    gain = jnp.concatenate([mg[0], mg[1]], axis=1)
    xg = (stream * gain).astype(BF16)

    def gu_copy(i):
        def copy(d):
            c = chip_at(d)
            return remote(gu_send.at[i, c], gu_recv.at[i, d], gu_s.at[i, d], gu_r.at[i, d], row, c * 2 + core)

        return copy

    for i, (low, width) in enumerate(CHUNKS):
        for half, weight in enumerate((wg, wu)):
            product = jnp.dot(xg, weight[:, low:low + width], preferred_element_type=F32)
            gu_send[i, :, :, half * HALF:half * HALF + width] = product.astype(BF16).reshape(CHIPS, 32, width)
        if i == 0:
            gu_send[0, :, :, width:HALF] = square_hi.reshape(CHIPS, 32, HALF - width)
            gu_send[0, :, :, HALF + width:FFP] = square_lo.reshape(CHIPS, 32, HALF - width)
        start(1, CHIPS, gu_copy(i))
        gu_recv[i, 0] = gu_send[i, chip]
    held = pending[-2:]
    del pending[-2:]
    wh_swap = pending.pop(wh_at)
    flush()
    pending.extend([wh_swap] + held)

    def hid_copy(i):
        own_hidden = hidden_all.at[chip, :, CHUNKS[i][0]:CHUNKS[i][0] + HALF]

        def copy(d):
            return remote(own_hidden, own_hidden, hid_s.at[i, d], hid_r.at[i, d], row, chip_at(d) * 2 + core)

        return copy

    hidden_all[chip, :, FF:FFP] = jnp.zeros((32, FFP - FF), BF16)
    for i, (low, width) in enumerate(CHUNKS):
        arrive(1, CHIPS, gu_copy(i))
        total = jnp.sum(gu_recv[i].astype(F32), axis=0)
        if i == 0:
            scale = inverse_rms(total[:, width:width + 1] + total[:, HALF + width:HALF + width + 1])
        gate = total[:, 0:width] * scale
        hidden = gate / (1.0 + jnp.exp(-gate)) * (total[:, HALF:HALF + width] * scale)
        hidden_all[chip, :, low:low + width] = hidden.astype(BF16)
        start(1, CHIPS, hid_copy(i))
    ready("wd")

    product = jnp.zeros((T, CHIP), F32)
    for i, (low, width) in enumerate(CHUNKS):
        arrive(1, CHIPS, hid_copy(i))
        hidden = hidden_all[:, :, low:low + width].reshape(T, width)
        product += dot_nt(hidden, wd[:, low:low + width])
    down_send[...] = product.reshape(ROWS, 32, CHIP)

    def down_copy(d):
        r = row_at(d)
        return remote(down_send.at[r], down_recv.at[d], down_s.at[d], down_r.at[d], r, col)

    start(1, ROWS, down_copy)
    down_recv[0] = down_send[row]
    arrive(1, ROWS, down_copy)
    final = stream_all[row].reshape(32, CHIP).astype(F32) + jnp.sum(down_recv[...], axis=0)
    square_hi, square_lo = split_sum(jnp.sum(final * final, axis=1, keepdims=True), 64)
    final = (final * jnp.concatenate([fg[0], fg[1]], axis=1)).astype(BF16)

    fin_a[cy, zl, cx, zh] = final[:, 0:256]
    fin_b[cy, zl, cx, zh] = final[:, 256:512]
    fin_c[cy, zl, cx, zh, :, 0:128] = final[:, 512:640]
    fin_c[cy, zl, cx, zh, :, 128:192] = square_hi
    fin_c[cy, zl, cx, zh, :, 192:256] = square_lo

    parts = (fin_a, fin_b, fin_c)
    orders = ("zyx", "xzy", "yxz")

    def axis_copies(p, stage):
        order = orders[p % 3]
        axis, done = order[stage], order[:stage]
        one = {"y": pl.ds(cy, 1), "x": pl.ds(cx, 1), "zl": pl.ds(zl, 1), "zh": pl.ds(zh, 1)}
        full = {"y": pl.ds(0, 4), "x": pl.ds(0, 4), "zl": pl.ds(0, 2), "zh": pl.ds(0, 2)}
        pick = {k: full[k] if k[0] in done else one[k] for k in one}
        ref = parts[p % 3].at[pick["y"], pick["zl"], pick["x"], pick["zh"], pl.ds(p // 3 * 16, 16)]
        copies = []
        for d in (2, 1, 3):
            x = lax.rem(cx + d, 4) if axis == "x" else cx
            y = lax.rem(cy + d, 4) if axis == "y" else cy
            z = lax.rem(cz + d, 4) if axis == "z" else cz
            r, c = at_xyz(x, y, z)
            i = (p * 3 + stage) * 3 + d - 1
            copies.append(remote(ref, ref, fin_s.at[i], fin_r.at[i], r, c))
        return copies

    gathers = [[axis_copies(p, stage) for p in range(6)] for stage in range(3)]
    for stage in range(3):
        for p in range(6):
            if stage:
                for copy in gathers[stage - 1][p]:
                    copy.wait_recv()
            for copy in gathers[stage][p]:
                copy.start()
                pending.append(copy.wait_send)
    last = pending[-18:]
    del pending[-18:]
    flush()
    pending.extend(last)
    ready("wh")
    ready("targets")
    diagonal = lax.broadcasted_iota(jnp.int32, (T, T), 0) == lax.broadcasted_iota(jnp.int32, (T, T), 1)
    target = jnp.sum(jnp.where(diagonal, target_row[...].astype(F32), 0.0), axis=1, keepdims=True).astype(jnp.int32)
    for p in range(6):
        for copy in gathers[2][p]:
            copy.wait_recv()

    square = jnp.zeros((T, 1), F32)
    for y in range(4):
        pieces = []
        for z in range(2):
            c = fin_c[y, z].reshape(T, 256)
            square = square + c[:, 128:129].astype(F32) + c[:, 192:193].astype(F32)
            pieces += [fin_a[y, z].reshape(T, 256), fin_b[y, z].reshape(T, 256), c[:, 0:128]]
        states = jnp.concatenate(pieces, axis=1)
        for j in range(2):
            product = jnp.dot(states, wh[j, y * 2 * CHIP:(y + 1) * 2 * CHIP], preferred_element_type=F32)
            logits[j] = product if y == 0 else logits[j] + product
    scale = inverse_rms(square)
    both = [logits[j] * scale for j in range(2)]
    top = jnp.maximum(*[jnp.max(l, axis=1, keepdims=True) for l in both])
    exponential = sum(jnp.sum(jnp.exp(l - top), axis=1, keepdims=True) for l in both)
    picked = jnp.zeros((T, 1), F32)
    for j in range(2):
        first = (row * COLS + chip * 2 + j) * VOCAB
        ids = first + lax.broadcasted_iota(jnp.int32, (T, VOCAB), 1)
        picked = picked + jnp.sum(jnp.where(ids == target, both[j], 0.0), axis=1, keepdims=True)
    lane = lax.broadcasted_iota(jnp.int32, (T, HEAD), 1)
    packed = jnp.where(lane == 0, top, jnp.where(lane == 1, exponential, picked))
    stat_recv[0] = jnp.transpose(packed)[0:8, :]

    def st_copy(d):
        return remote(stat_recv.at[0], stat_recv.at[d], st_s.at[d], st_r.at[d], row, chip_at(d) * 2 + core)

    start(1, CHIPS, st_copy)
    arrive(1, CHIPS, st_copy)

    def merge(blocks):
        top = jnp.max(blocks[:, 0:1, :], axis=0)
        exponential = jnp.sum(blocks[:, 1:2, :] * jnp.exp(blocks[:, 0:1, :] - top[None]), axis=0)
        return top, exponential, jnp.sum(blocks[:, 2:3, :], axis=0)

    top, exponential, picked = merge(stat_recv[...])
    line = lax.broadcasted_iota(jnp.int32, (8, T), 0)
    stat_send[...] = jnp.where(line == 0, top, jnp.where(line == 1, exponential, picked))
    own_stat = stat2_recv.at[core, row]
    stat2_recv[core, row] = stat_send[...]

    def st2_copy(d):
        return remote(stat_send, own_stat, st2_s.at[d], st2_r.at[d], row_at(d), col)

    def st2_cross(d):
        return remote(stat_send, own_stat, st2_s.at[ROWS + d], st2_r.at[ROWS + d], row_at(d), sib)

    start(1, ROWS, st2_copy)
    start(0, ROWS, st2_cross)
    arrive(1, ROWS, st2_copy)
    arrive(0, ROWS, st2_cross)
    logprob = []
    for m in range(2):
        top, exponential, picked = merge(stat2_recv[m])
        logprob.append(picked - (top + jnp.log(exponential)))
    difference = logprob[0] - logprob[1]
    hit = line == k_segment
    sums = jnp.sum(jnp.where(hit, difference, 0.0), axis=1, keepdims=True)
    length = jnp.sum(jnp.where(hit, 1.0, 0.0), axis=1, keepdims=True)
    square8 = lax.broadcasted_iota(jnp.int32, (8, 8), 0) == lax.broadcasted_iota(jnp.int32, (8, 8), 1)
    out[...] = jnp.sum(jnp.where(square8, sums / length, 0.0), axis=0, keepdims=True)

    flush()


def per_device(
    residual, attn_gain, w_query, w_key, w_value, w_out, mlp_gain, w_gate, w_up, w_down, final_gain, w_head,
    seq_lengths, targets,
):
    anywhere = pl.BlockSpec(memory_space=pl.ANY)
    vmem = pl.BlockSpec(memory_space=pltpu.VMEM)
    smem = pl.BlockSpec(memory_space=pltpu.SMEM)
    dma = pltpu.SemaphoreType.DMA
    result = pl.pallas_call(
        kernel,
        out_shape=jax.ShapeDtypeStruct((1, SEQS), F32),
        in_specs=[anywhere] * 12 + [smem, anywhere],
        out_specs=vmem,
        scratch_shapes=[
            pltpu.VMEM((1, T), jnp.int32),
            pltpu.VMEM((2, 32, FEAT), BF16),
            pltpu.VMEM((COLS, 8, HEAD), F32),
            pltpu.VMEM((ROWS, 32, FEAT), BF16),
            pltpu.VMEM((FEAT, QKV), BF16),
            pltpu.VMEM((CHIP, QW), BF16),
            pltpu.VMEM((CHIP, FF), BF16),
            pltpu.VMEM((CHIP, FF), BF16),
            pltpu.VMEM((CHIP, FF), BF16),
            pltpu.VMEM((2, D, VOCAB), BF16),
            pltpu.VMEM((FEAT,), F32),
            pltpu.VMEM((FEAT,), F32),
            pltpu.VMEM((FEAT,), F32),
            pltpu.VMEM((2, 1, FEAT), F32),
            pltpu.VMEM((2, 1, FEAT), F32),
            pltpu.VMEM((CHIPS, 2, 16, QKV), F32),
            pltpu.VMEM((CHIPS, 16, QKV), F32),
            pltpu.VMEM((CHIPS, 16, QKV), F32),
            pltpu.VMEM((CHIPS, 16, QKV), F32),
            pltpu.VMEM((CHIPS, 2, 16, QKV), BF16),
            pltpu.VMEM((T // 2, QW), BF16),
            pltpu.VMEM((ROWS, 16, CHIP), F32),
            pltpu.VMEM((ROWS, 16, CHIP), F32),
            pltpu.VMEM((ROWS, 2, 16, CHIP), BF16),
            pltpu.VMEM((2, CHIPS, 32, FFP), BF16),
            pltpu.VMEM((2, CHIPS, 32, FFP), BF16),
            pltpu.VMEM((CHIPS, 32, FFP), BF16),
            pltpu.VMEM((ROWS, 32, CHIP), F32),
            pltpu.VMEM((ROWS, 32, CHIP), F32),
            pltpu.VMEM((4, 2, 4, 2, 32, 256), BF16),
            pltpu.VMEM((4, 2, 4, 2, 32, 256), BF16),
            pltpu.VMEM((4, 2, 4, 2, 32, 256), BF16),
            pltpu.VMEM((2, T, VOCAB), F32),
            pltpu.VMEM((8, T), F32),
            pltpu.VMEM((CHIPS, 8, T), F32),
            pltpu.VMEM((2, ROWS, 8, T), F32),
            dma((13,)), dma((8,)), dma((8,)),
            dma((COLS,)), dma((COLS,)),
            dma((ROWS,)), dma((ROWS,)),
            dma, dma,
            dma((CHIPS,)), dma((CHIPS,)),
            dma((COLS,)), dma((COLS,)),
            dma((ROWS,)), dma((ROWS,)),
            dma((2 * ROWS,)), dma((2 * ROWS,)),
            dma((2, CHIPS)), dma((2, CHIPS)),
            dma((2, CHIPS)), dma((2, CHIPS)),
            dma((ROWS,)), dma((ROWS,)),
            dma((54,)), dma((54,)),
            dma((CHIPS,)), dma((CHIPS,)),
            dma((2 * ROWS,)), dma((2 * ROWS,)),
        ],
        compiler_params=pltpu.CompilerParams(
            collective_id=0, has_side_effects=True, vmem_limit_bytes=60 * 1024 * 1024
        ),
    )(
        residual, attn_gain, w_query, w_key, w_value, w_out.T, mlp_gain, w_gate, w_up,
        jnp.swapaxes(w_down, 1, 2), final_gain, w_head, seq_lengths, targets.reshape(1, T),
    )
    return result.reshape(SEQS)


def solution(mesh):
    placed = (
        P("row", "col"), P("col"), P("col", "row"), P("col", "row"), P("col", "row"), P("row", "col"), P("col"),
        P(None, "col", "row"), P(None, "col", "row"), P(None, "row", "col"), P("col"), P(None, ("row", "col")), P(), P(),
    )
    return jax.shard_map(per_device, mesh=mesh, in_specs=placed, out_specs=P(), check_vma=False)
```

```python
import math

import jax
import jax.numpy as jnp
from jax import lax
from jax.experimental import pallas as pl
from jax.experimental.pallas import tpu as pltpu
from jax.sharding import PartitionSpec as P

T = 256
D = 5120
HEAD = 128
Q_HEADS = 5
QW = Q_HEADS * HEAD
QKV = QW + 2 * HEAD
SEQS = 8
FEAT = 320
CHIP = 2 * FEAT
FF = 1728
FFP = 1792
HALF = FFP // 2
CHUNKS = ((HALF, FF - HALF), (0, HALF))
VOCAB = 640
ROWS = 8
COLS = 16
CHIPS = 8
EPSILON = 1e-06
ROPE_BASE = 1000000.0
MASKED = -1e30
MESH = pl.DeviceIdType.MESH
F32 = jnp.float32
BF16 = jnp.bfloat16


def remote(src, dst, send, recv, row, col):
    return pltpu.make_async_remote_copy(
        src_ref=src, dst_ref=dst, send_sem=send, recv_sem=recv,
        device_id={"row": row, "col": col}, device_id_type=MESH,
    )


def each(start, stop, body):
    def step(i, carry):
        body(i)
        return carry

    lax.fori_loop(start, stop, step, 0)


def dot_nt(a, b):
    return lax.dot_general(a, b, (((1,), (1,)), ((), ())), preferred_element_type=F32)


def diagonal_of(count):
    return lax.broadcasted_iota(jnp.int32, (count, HEAD), 0) == lax.broadcasted_iota(jnp.int32, (count, HEAD), 1)


def to_row(column):
    row = jnp.sum(jnp.where(diagonal_of(column.shape[0]), column, 0.0), axis=0, keepdims=True)
    return jnp.broadcast_to(row, (8, HEAD))


def to_column(rows, count):
    return jnp.sum(jnp.where(diagonal_of(count), rows[0:1], 0.0), axis=1, keepdims=True)


def inverse_rms(total):
    return lax.rsqrt(total / D + EPSILON)


def layout_of(lens_ref, token):
    segment = jnp.zeros_like(token)
    start = jnp.zeros_like(token)
    end = jnp.int32(0)
    for s in range(SEQS):
        length = lens_ref[s]
        end = end + length
        before = end <= token
        segment = segment + jnp.where(before, 1, 0)
        start = start + jnp.where(before, length, 0)
    return segment, token - start


def kernel(
    res, attn_gain, w_query, w_key, w_value, w_out, mlp_gain, w_gate, w_up, w_down, final_gain, w_head, lens, targets,
    out,
    target_row, res_chip, square_all, x_all, wqkv, wo, wg, wu, wd, wh, gain_a, gain_m, gain_f, mg, fg,
    part_own, part_pair, part_send, part_recv, qkv_all, attended, proj_send, proj_recv, stream_chip, norm_all, mlp_all,
    gu_own, gu_send, gu_z0, gu_y0, gu_z1, gu_y1, mid_own, mid_send, mid2_own, mid2_send, hidden_all, down_send, down_recv,
    fin_a, fin_b, fin_c, logits, stat_send, stat_recv, stat2_recv,
    local_sem, swap_send, swap_recv, sq_s, sq_r, x_s, x_r, pair_s, pair_r, part_s, part_r, qkv_s, qkv_r, proj_s, proj_r,
    norm_s, norm_r, stream_s, stream_r, y_s, y_r, z_s, z_r, down_s, down_r, fin_s, fin_r, st_s, st_r, st2_s, st2_r,
):
    row, col = lax.axis_index("row"), lax.axis_index("col")
    core = lax.rem(col, 2)
    other = 1 - core
    chip = lax.div(col, 2)
    cx, zh = lax.div(row, 2), lax.rem(row, 2)
    cy, zl = lax.div(chip, 2), lax.rem(chip, 2)
    cz = zh * 2 + zl
    sib = chip * 2 + other

    def row_at(d):
        return lax.rem(row + d, ROWS)

    def chip_at(d):
        return lax.rem(chip + d, CHIPS)

    def col_at(d):
        return lax.rem(col + d, COLS)

    def at_xyz(x, y, z):
        return x * 2 + lax.div(z, 2), (y * 2 + lax.rem(z, 2)) * 2 + core

    mine = pl.ds(pl.multiple_of(core * FEAT, 64), FEAT)
    waits, pending, numbers = {}, [], {"own": 0, "pair": 0}

    def own(name, src, dst):
        copy = pltpu.make_async_copy(src, dst, local_sem.at[numbers["own"]])
        numbers["own"] += 1
        copy.start()
        waits.setdefault(name, []).append(copy.wait)

    def swap(name, src, dst):
        i = numbers["pair"]
        numbers["pair"] += 1
        copy = remote(src, dst, swap_send.at[i], swap_recv.at[i], row, sib)
        copy.start()
        waits.setdefault(name, []).append(copy.wait_recv)
        pending.append(copy.wait_send)

    def ready(*names):
        for name in names:
            for wait in waits.pop(name):
                wait()

    def start(first, stop, copy):
        each(first, stop, lambda d: copy(d).start())
        pending.append(lambda: each(first, stop, lambda d: copy(d).wait_send()))

    def arrive(first, stop, copy):
        each(first, stop, lambda d: copy(d).wait_recv())

    def flush():
        for finish in pending:
            finish()
        pending.clear()

    own("residual", res, res_chip.at[core])
    own("targets", targets, target_row)
    own("gains", attn_gain, gain_a)
    own("gains", mlp_gain, gain_m)
    own("gains", final_gain, gain_f)
    own("wqkv", w_query, wqkv.at[:, 0:QW])
    own("wqkv", w_key, wqkv.at[:, QW:QW + HEAD])
    own("wqkv", w_value, wqkv.at[:, QW + HEAD:QKV])

    barrier = pltpu.get_barrier_semaphore()

    def greet(r, c):
        pl.semaphore_signal(barrier, inc=1, device_id={"row": r, "col": c}, device_id_type=MESH)

    each(1, ROWS, lambda d: greet(row_at(d), col))
    each(1, ROWS, lambda d: greet(row_at(d), sib))
    each(1, COLS, lambda d: greet(row, col_at(d)))
    cross_z = lax.rem(cz + 1 + 2 * (1 - zl), 4)
    cross_row, cross_col = at_xyz(cx, cy, cross_z)
    greet(cross_row, cross_col)
    pl.semaphore_wait(barrier, 2 * (ROWS - 1) + (COLS - 1) + 1)

    ready("residual", "gains")
    x = res_chip[core].astype(F32)
    square_all[0] = to_row(jnp.sum(x * x, axis=1, keepdims=True))

    def sq_copy(d):
        return remote(square_all.at[0], square_all.at[d], sq_s.at[d], sq_r.at[d], row, col_at(d))

    start(1, COLS, sq_copy)
    mg[core] = gain_m[...].reshape(1, FEAT)
    fg[core] = gain_f[...].reshape(1, FEAT)

    own_token = COLS * col + lax.broadcasted_iota(jnp.int32, (16, HEAD), 0)
    position = layout_of(lens, own_token)[1].astype(F32)
    lane = lax.broadcasted_iota(jnp.int32, (16, HEAD), 1)
    low_half = lane < HEAD // 2
    frequency = jnp.exp(jnp.where(low_half, lane, lane - HEAD // 2).astype(F32) * (-2.0 * math.log(ROPE_BASE) / HEAD))
    angle = position * frequency
    cosine = jnp.cos(angle)
    sine = jnp.where(low_half, -jnp.sin(angle), jnp.sin(angle))

    arrive(1, COLS, sq_copy)
    square = to_column(jnp.sum(square_all[...], axis=0), 32)
    x_all[row] = (x * inverse_rms(square) * gain_a[...].reshape(1, FEAT)).astype(BF16)

    def x_copy(d):
        return remote(x_all.at[row], x_all.at[row], x_s.at[d], x_r.at[d], row_at(d), col)

    start(1, ROWS, x_copy)
    swap("residual_pair", res_chip.at[core], res_chip.at[core])
    swap("gains_pair", mg.at[core], mg.at[core])
    swap("gains_pair", fg.at[core], fg.at[core])
    own("wo", w_out, wo.at[mine])
    swap("wo", w_out, wo.at[mine])
    ready("wqkv")
    arrive(1, ROWS, x_copy)

    part = jnp.dot(x_all[...].reshape(T, FEAT), wqkv[...], preferred_element_type=F32)
    part_own[...] = part.reshape(CHIPS, 2, 16, QKV)
    pair = remote(part_own.at[:, other], part_pair, pair_s, pair_r, row, sib)
    pair.start()
    pending.append(pair.wait_send)
    pair.wait_recv()
    part_send[...] = part_own[:, core] + part_pair[...]

    def part_copy(d):
        c = chip_at(d)
        return remote(part_send.at[c], part_recv.at[d], part_s.at[d], part_r.at[d], row, c * 2 + core)

    start(1, CHIPS, part_copy)
    own("wg", w_gate.at[core], wg.at[mine])
    own("wu", w_up.at[core], wu.at[mine])
    swap("wg", w_gate.at[other], wg.at[mine])
    swap("wu", w_up.at[other], wu.at[mine])
    part_recv[0] = part_send[chip]
    arrive(1, CHIPS, part_copy)

    total = jnp.sum(part_recv[...], axis=0)
    for h in range(Q_HEADS + 1):
        head = total[:, h * HEAD:(h + 1) * HEAD]
        turned = head * cosine + pltpu.roll(head, HEAD // 2, 1) * sine
        qkv_all[chip, core, :, h * HEAD:(h + 1) * HEAD] = turned.astype(BF16)
    qkv_all[chip, core, :, QW + HEAD:QKV] = total[:, QW + HEAD:QKV].astype(BF16)

    own_qkv = qkv_all.at[chip, core]
    own_kv = qkv_all.at[chip, core, :, QW:QKV]

    def qkv_copy(d):
        return remote(own_qkv, own_qkv, qkv_s.at[d], qkv_r.at[d], row, chip_at(d) * 2 + core)

    def kv_copy(d):
        return remote(own_kv, own_kv, qkv_s.at[CHIPS + d], qkv_r.at[CHIPS + d], row, chip_at(d) * 2 + other)

    start(1, CHIPS, qkv_copy)
    start(0, CHIPS, kv_copy)
    own("wd", w_down.at[core], wd.at[mine])
    swap("wd", w_down.at[other], wd.at[mine])

    row_i = lax.broadcasted_iota(jnp.int32, (T // 2, 1), 0)
    q_token = lax.div(row_i, 16) * 32 + core * 16 + lax.rem(row_i, 16)
    k_token = lax.broadcasted_iota(jnp.int32, (1, T), 1)
    q_segment = layout_of(lens, q_token)[0]
    k_segment = layout_of(lens, k_token)[0]
    allowed = (q_segment == k_segment) & (k_token <= q_token)

    arrive(1, CHIPS, qkv_copy)
    arrive(0, CHIPS, kv_copy)

    keys = qkv_all[:, :, :, QW:QW + HEAD].reshape(T, HEAD)
    values = qkv_all[:, :, :, QW + HEAD:QKV].reshape(T, HEAD)
    for h in range(Q_HEADS):
        query = qkv_all[:, core, :, h * HEAD:(h + 1) * HEAD].reshape(T // 2, HEAD)
        scores = dot_nt(query, keys)
        scores = jnp.where(allowed, scores * HEAD ** (-0.5), MASKED)
        weights = jnp.exp(scores - jnp.max(scores, axis=1, keepdims=True))
        weights = (weights / jnp.sum(weights, axis=1, keepdims=True)).astype(BF16)
        result = jnp.dot(weights, values, preferred_element_type=F32)
        attended[:, h * HEAD:(h + 1) * HEAD] = result.astype(BF16)

    ready("wo", "residual_pair")
    proj_send[...] = dot_nt(attended[...], wo[...]).reshape(ROWS, 16, CHIP)

    def proj_copy(d):
        r = row_at(d)
        return remote(proj_send.at[r], proj_recv.at[d], proj_s.at[d], proj_r.at[d], r, col)

    start(1, ROWS, proj_copy)
    proj_recv[0] = proj_send[row]
    arrive(1, ROWS, proj_copy)
    half_rows = pl.ds(pl.multiple_of(core * 16, 16), 16)
    residual = jnp.concatenate([res_chip[0, half_rows, :], res_chip[1, half_rows, :]], axis=1).astype(F32)
    stream = (residual + jnp.sum(proj_recv[...], axis=0)).astype(BF16)
    stream_chip[core] = stream
    stream = stream.astype(F32)

    def norm(i, value, gain):
        count = value.shape[0]
        norm_all[i, 0] = to_row(jnp.sum(value * value, axis=1, keepdims=True))

        def copy(d):
            return remote(
                norm_all.at[i, 0], norm_all.at[i, d], norm_s.at[i, d], norm_r.at[i, d], row, chip_at(d) * 2 + core
            )

        start(1, CHIPS, copy)
        arrive(1, CHIPS, copy)
        square = to_column(jnp.sum(norm_all[i], axis=0), count)
        gain = jnp.concatenate([gain[0], gain[1]], axis=1)
        return (value * inverse_rms(square) * gain).astype(BF16)

    ready("gains_pair")
    mlp_all[row, core] = norm(0, stream, mg)

    own_stream = mlp_all.at[row, core]

    def stream_copy(d):
        return remote(own_stream, own_stream, stream_s.at[d], stream_r.at[d], row_at(d), col)

    def stream_cross(d):
        return remote(own_stream, own_stream, stream_s.at[ROWS + d], stream_r.at[ROWS + d], row_at(d), sib)

    start(1, ROWS, stream_copy)
    start(0, ROWS, stream_cross)
    swap("stream_pair", stream_chip.at[core], stream_chip.at[core])
    own("wh", w_head, wh.at[core])
    swap("wh", w_head, wh.at[core])
    wh_at = len(pending) - 1
    ready("wg", "wu")
    arrive(1, ROWS, stream_copy)
    arrive(0, ROWS, stream_cross)

    mlp_in = mlp_all[...].reshape(T, CHIP)

    def y_peer(d):
        return (lax.rem(cy + d, 4) * 2 + zl) * 2 + core

    z_peer = (cy * 2 + 1 - zl) * 2 + core

    def to_y(src, dst, i):
        def copy(d):
            return remote(src(lax.rem(cy + d, 4)), dst(d), y_s.at[i, d], y_r.at[i, d], row, y_peer(d))

        return copy

    def to_z(src, dst, i):
        return lambda d: remote(src, dst, z_s.at[i], z_r.at[i], row, z_peer)

    def gate_up(i):
        low, width = CHUNKS[i]
        for half, weight in enumerate((wg, wu)):
            product = jnp.dot(mlp_in, weight[:, low:low + width], preferred_element_type=F32)
            product = product.reshape(4, 2, 32, width)
            gu_own[i, :, :, :, half * HALF:half * HALF + width] = product
            gu_send[i, :, :, :, half * HALF:half * HALF + width] = product.astype(BF16)
            if width < HALF:
                rest = jnp.zeros((4, 2, 32, HALF - width), F32)
                gu_own[i, :, :, :, half * HALF + width:(half + 1) * HALF] = rest
                gu_send[i, :, :, :, half * HALF + width:(half + 1) * HALF] = rest.astype(BF16)

    gate_up(0)
    sum_z0 = to_z(gu_send.at[0, :, 1 - zl], gu_z0, 0)
    start(0, 1, sum_z0)
    gate_up(1)
    sum_y1 = to_y(lambda y: gu_send.at[1, y], lambda d: gu_y1.at[d], 0)
    start(1, 4, sum_y1)
    held = pending[-2:]
    del pending[-2:]
    wh_swap = pending.pop(wh_at)
    flush()
    pending.extend([wh_swap] + held)

    arrive(0, 1, sum_z0)
    mid_own[...] = gu_own[0, :, zl] + gu_z0[...].astype(F32)
    mid_send[...] = mid_own[...].astype(BF16)
    sum_y0 = to_y(lambda y: mid_send.at[y], lambda d: gu_y0.at[d], 1)
    start(1, 4, sum_y0)
    arrive(1, 4, sum_y1)
    gu_y1[0] = jnp.zeros((2, 32, FFP), BF16)
    mid2_own[...] = gu_own[1, cy] + jnp.sum(gu_y1[...].astype(F32), axis=0)
    mid2_send[...] = mid2_own[1 - zl].astype(BF16)
    sum_z1 = to_z(mid2_send, gu_z1, 1)
    start(0, 1, sum_z1)

    def activate(i, total):
        low, width = CHUNKS[i]
        gate = total[:, 0:width]
        hidden = gate / (1.0 + jnp.exp(-gate)) * total[:, HALF:HALF + width]
        hidden_all[cy, zl, :, low:low + width] = hidden.astype(BF16)

    def lanes(i):
        return pl.ds(CHUNKS[i][0], HALF)

    hidden_all[cy, zl, :, FF:FFP] = jnp.zeros((32, FFP - FF), BF16)
    arrive(1, 4, sum_y0)
    gu_y0[0] = jnp.zeros((32, FFP), BF16)
    activate(0, mid_own[cy] + jnp.sum(gu_y0[...].astype(F32), axis=0))
    own0 = hidden_all.at[cy, zl, :, lanes(0)]
    hid_z0 = to_z(own0, own0, 2)
    start(0, 1, hid_z0)
    arrive(0, 1, sum_z1)
    activate(1, mid2_own[zl] + gu_z1[...].astype(F32))
    own1 = hidden_all.at[cy, zl, :, lanes(1)]
    hid_y1 = to_y(lambda y: own1, lambda d: own1, 2)
    start(1, 4, hid_y1)
    arrive(0, 1, hid_z0)
    both0 = hidden_all.at[cy, :, :, lanes(0)]
    hid_y0 = to_y(lambda y: both0, lambda d: both0, 3)
    start(1, 4, hid_y0)
    arrive(1, 4, hid_y1)
    four1 = hidden_all.at[:, zl, :, lanes(1)]
    hid_z1 = to_z(four1, four1, 3)
    start(0, 1, hid_z1)
    ready("wd")

    product = jnp.zeros((T, CHIP), F32)
    for i, (low, width) in enumerate(CHUNKS):
        arrive(*((1, 4, hid_y0) if i == 0 else (0, 1, hid_z1)))
        hidden = hidden_all[:, :, :, low:low + width].reshape(T, width)
        product += dot_nt(hidden, wd[:, low:low + width])
    down_send[...] = product.reshape(ROWS, 32, CHIP)

    def down_copy(d):
        r = row_at(d)
        return remote(down_send.at[r], down_recv.at[d], down_s.at[d], down_r.at[d], r, col)

    start(1, ROWS, down_copy)
    down_recv[0] = down_send[row]
    arrive(1, ROWS, down_copy)
    ready("stream_pair")
    final = stream_chip[...].reshape(32, CHIP).astype(F32) + jnp.sum(down_recv[...], axis=0)
    final = norm(1, final, fg)

    fin_a[cy, zl, cx, zh] = final[:, 0:256]
    fin_b[cy, zl, cx, zh] = final[:, 256:512]
    fin_c[cy, zl, cx, zh] = final[:, 512:640]

    parts = (fin_a, fin_b, fin_c)
    orders = ("zyx", "xzy", "yxz")

    def axis_copies(p, stage):
        order = orders[p % 3]
        axis, done = order[stage], order[:stage]
        one = {"y": pl.ds(cy, 1), "x": pl.ds(cx, 1), "zl": pl.ds(zl, 1), "zh": pl.ds(zh, 1)}
        full = {"y": pl.ds(0, 4), "x": pl.ds(0, 4), "zl": pl.ds(0, 2), "zh": pl.ds(0, 2)}
        pick = {k: full[k] if k[0] in done else one[k] for k in one}
        ref = parts[p % 3].at[pick["y"], pick["zl"], pick["x"], pick["zh"], pl.ds(p // 3 * 16, 16)]
        copies = []
        for d in (2, 1, 3):
            x = lax.rem(cx + d, 4) if axis == "x" else cx
            y = lax.rem(cy + d, 4) if axis == "y" else cy
            z = lax.rem(cz + d, 4) if axis == "z" else cz
            r, c = at_xyz(x, y, z)
            i = (p * 3 + stage) * 3 + d - 1
            copies.append(remote(ref, ref, fin_s.at[i], fin_r.at[i], r, c))
        return copies

    gathers = [[axis_copies(p, stage) for p in range(6)] for stage in range(3)]
    for stage in range(3):
        for p in range(6):
            if stage:
                for copy in gathers[stage - 1][p]:
                    copy.wait_recv()
            for copy in gathers[stage][p]:
                copy.start()
                pending.append(copy.wait_send)
    last = pending[-18:]
    del pending[-18:]
    flush()
    pending.extend(last)
    ready("wh")
    ready("targets")
    diagonal = lax.broadcasted_iota(jnp.int32, (T, T), 0) == lax.broadcasted_iota(jnp.int32, (T, T), 1)
    target = jnp.sum(jnp.where(diagonal, target_row[...].astype(F32), 0.0), axis=1, keepdims=True).astype(jnp.int32)
    for p in range(6):
        for copy in gathers[2][p]:
            copy.wait_recv()

    for y in range(4):
        pieces = []
        for z in range(2):
            pieces += [fin_a[y, z].reshape(T, 256), fin_b[y, z].reshape(T, 256), fin_c[y, z].reshape(T, HEAD)]
        states = jnp.concatenate(pieces, axis=1)
        for j in range(2):
            product = jnp.dot(states, wh[j, y * 2 * CHIP:(y + 1) * 2 * CHIP], preferred_element_type=F32)
            logits[j] = product if y == 0 else logits[j] + product
    both = [logits[j] for j in range(2)]
    top = jnp.maximum(*[jnp.max(l, axis=1, keepdims=True) for l in both])
    exponential = sum(jnp.sum(jnp.exp(l - top), axis=1, keepdims=True) for l in both)
    picked = jnp.zeros((T, 1), F32)
    for j in range(2):
        first = (row * COLS + chip * 2 + j) * VOCAB
        ids = first + lax.broadcasted_iota(jnp.int32, (T, VOCAB), 1)
        picked = picked + jnp.sum(jnp.where(ids == target, both[j], 0.0), axis=1, keepdims=True)
    lane = lax.broadcasted_iota(jnp.int32, (T, HEAD), 1)
    packed = jnp.where(lane == 0, top, jnp.where(lane == 1, exponential, picked))
    stat_recv[0, 0] = jnp.transpose(packed)[0:8, :]

    def merge(blocks):
        top = jnp.max(blocks[:, 0:1, :], axis=0)
        exponential = jnp.sum(blocks[:, 1:2, :] * jnp.exp(blocks[:, 0:1, :] - top[None]), axis=0)
        return top, exponential, jnp.sum(blocks[:, 2:3, :], axis=0)

    line = lax.broadcasted_iota(jnp.int32, (8, T), 0)

    def packed_merge(blocks):
        top, exponential, picked = merge(blocks)
        return jnp.where(line == 0, top, jnp.where(line == 1, exponential, picked))

    for stage in range(2):
        def st_copy(d):
            if stage == 0:
                r, c = at_xyz(cx, cy, lax.rem(cz + d, 4))
            else:
                r, c = at_xyz(cx, lax.rem(cy + d, 4), cz)
            return remote(stat_recv.at[stage, 0], stat_recv.at[stage, d], st_s.at[stage, d], st_r.at[stage, d], r, c)

        each(1, 4, lambda d: st_copy(d).start())
        arrive(1, 4, st_copy)
        each(1, 4, lambda d: st_copy(d).wait_send())
        merged = packed_merge(stat_recv[stage])
        if stage == 0:
            stat_recv[1, 0] = merged
        else:
            stat_send[...] = merged
            stat2_recv[core, cx] = merged
    own_stat = stat2_recv.at[core, cx]

    def st2_copy(d):
        return remote(stat_send, own_stat, st2_s.at[d], st2_r.at[d], lax.rem(cx + d, 4) * 2 + zh, col)

    def st2_cross(d):
        return remote(stat_send, own_stat, st2_s.at[4 + d], st2_r.at[4 + d], lax.rem(cx + d, 4) * 2 + zh, sib)

    start(1, 4, st2_copy)
    start(0, 4, st2_cross)
    arrive(1, 4, st2_copy)
    arrive(0, 4, st2_cross)
    logprob = []
    for m in range(2):
        top, exponential, picked = merge(stat2_recv[m])
        logprob.append(picked - (top + jnp.log(exponential)))
    difference = logprob[0] - logprob[1]
    hit = line == k_segment
    sums = jnp.sum(jnp.where(hit, difference, 0.0), axis=1, keepdims=True)
    length = jnp.sum(jnp.where(hit, 1.0, 0.0), axis=1, keepdims=True)
    square8 = lax.broadcasted_iota(jnp.int32, (8, 8), 0) == lax.broadcasted_iota(jnp.int32, (8, 8), 1)
    out[...] = jnp.sum(jnp.where(square8, sums / length, 0.0), axis=0, keepdims=True)

    flush()


def per_device(
    residual, attn_gain, w_query, w_key, w_value, w_out, mlp_gain, w_gate, w_up, w_down, final_gain, w_head,
    seq_lengths, targets,
):
    anywhere = pl.BlockSpec(memory_space=pl.ANY)
    vmem = pl.BlockSpec(memory_space=pltpu.VMEM)
    smem = pl.BlockSpec(memory_space=pltpu.SMEM)
    dma = pltpu.SemaphoreType.DMA
    result = pl.pallas_call(
        kernel,
        out_shape=jax.ShapeDtypeStruct((1, SEQS), F32),
        in_specs=[anywhere] * 12 + [smem, anywhere],
        out_specs=vmem,
        scratch_shapes=[
            pltpu.VMEM((1, T), jnp.int32),
            pltpu.VMEM((2, 32, FEAT), BF16),
            pltpu.VMEM((COLS, 8, HEAD), F32),
            pltpu.VMEM((ROWS, 32, FEAT), BF16),
            pltpu.VMEM((FEAT, QKV), BF16),
            pltpu.VMEM((CHIP, QW), BF16),
            pltpu.VMEM((CHIP, FF), BF16),
            pltpu.VMEM((CHIP, FF), BF16),
            pltpu.VMEM((CHIP, FF), BF16),
            pltpu.VMEM((2, D, VOCAB), BF16),
            pltpu.VMEM((FEAT,), F32),
            pltpu.VMEM((FEAT,), F32),
            pltpu.VMEM((FEAT,), F32),
            pltpu.VMEM((2, 1, FEAT), F32),
            pltpu.VMEM((2, 1, FEAT), F32),
            pltpu.VMEM((CHIPS, 2, 16, QKV), F32),
            pltpu.VMEM((CHIPS, 16, QKV), F32),
            pltpu.VMEM((CHIPS, 16, QKV), F32),
            pltpu.VMEM((CHIPS, 16, QKV), F32),
            pltpu.VMEM((CHIPS, 2, 16, QKV), BF16),
            pltpu.VMEM((T // 2, QW), BF16),
            pltpu.VMEM((ROWS, 16, CHIP), F32),
            pltpu.VMEM((ROWS, 16, CHIP), F32),
            pltpu.VMEM((2, 16, CHIP), BF16),
            pltpu.VMEM((2, CHIPS, 8, HEAD), F32),
            pltpu.VMEM((ROWS, 2, 16, CHIP), BF16),
            pltpu.VMEM((2, 4, 2, 32, FFP), F32),
            pltpu.VMEM((2, 4, 2, 32, FFP), BF16),
            pltpu.VMEM((4, 32, FFP), BF16),
            pltpu.VMEM((4, 32, FFP), BF16),
            pltpu.VMEM((32, FFP), BF16),
            pltpu.VMEM((4, 2, 32, FFP), BF16),
            pltpu.VMEM((4, 32, FFP), F32),
            pltpu.VMEM((4, 32, FFP), BF16),
            pltpu.VMEM((2, 32, FFP), F32),
            pltpu.VMEM((32, FFP), BF16),
            pltpu.VMEM((4, 2, 32, FFP), BF16),
            pltpu.VMEM((ROWS, 32, CHIP), F32),
            pltpu.VMEM((ROWS, 32, CHIP), F32),
            pltpu.VMEM((4, 2, 4, 2, 32, 256), BF16),
            pltpu.VMEM((4, 2, 4, 2, 32, 256), BF16),
            pltpu.VMEM((4, 2, 4, 2, 32, HEAD), BF16),
            pltpu.VMEM((2, T, VOCAB), F32),
            pltpu.VMEM((8, T), F32),
            pltpu.VMEM((2, 4, 8, T), F32),
            pltpu.VMEM((2, 4, 8, T), F32),
            dma((13,)), dma((9,)), dma((9,)),
            dma((COLS,)), dma((COLS,)),
            dma((ROWS,)), dma((ROWS,)),
            dma, dma,
            dma((CHIPS,)), dma((CHIPS,)),
            dma((COLS,)), dma((COLS,)),
            dma((ROWS,)), dma((ROWS,)),
            dma((2, CHIPS)), dma((2, CHIPS)),
            dma((2 * ROWS,)), dma((2 * ROWS,)),
            dma((4, 4)), dma((4, 4)),
            dma((4,)), dma((4,)),
            dma((ROWS,)), dma((ROWS,)),
            dma((54,)), dma((54,)),
            dma((2, 4)), dma((2, 4)),
            dma((CHIPS,)), dma((CHIPS,)),
        ],
        compiler_params=pltpu.CompilerParams(
            collective_id=0, has_side_effects=True, vmem_limit_bytes=60 * 1024 * 1024
        ),
    )(
        residual, attn_gain, w_query, w_key, w_value, w_out.T, mlp_gain, w_gate, w_up,
        jnp.swapaxes(w_down, 1, 2), final_gain, w_head, seq_lengths, targets.reshape(1, T),
    )
    return result.reshape(SEQS)


def solution(mesh):
    placed = (
        P("row", "col"), P("col"), P("col", "row"), P("col", "row"), P("col", "row"), P("row", "col"), P("col"),
        P(None, "col", "row"), P(None, "col", "row"), P(None, "row", "col"), P("col"), P(None, ("row", "col")), P(), P(),
    )
    return jax.shard_map(per_device, mesh=mesh, in_specs=placed, out_specs=P(), check_vma=False)
```

```python
import math

import jax
import jax.numpy as jnp
from jax import lax
from jax.experimental import pallas as pl
from jax.experimental.pallas import tpu as pltpu
from jax.sharding import PartitionSpec as P

T = 256
D = 5120
HEAD = 128
Q_HEADS = 5
QW = Q_HEADS * HEAD
QKV = QW + 2 * HEAD
SEQS = 8
FEAT = 320
CHIP = 2 * FEAT
FF = 1728
FFP = 1792
HALF = FFP // 2
CHUNKS = ((HALF, FF - HALF), (0, HALF))
VOCAB = 640
ROWS = 8
COLS = 16
CHIPS = 8
EPSILON = 1e-06
ROPE_BASE = 1000000.0
MASKED = -1e30
MESH = pl.DeviceIdType.MESH
F32 = jnp.float32
BF16 = jnp.bfloat16


def remote(src, dst, send, recv, row, col):
    return pltpu.make_async_remote_copy(
        src_ref=src, dst_ref=dst, send_sem=send, recv_sem=recv,
        device_id={"row": row, "col": col}, device_id_type=MESH,
    )


def dot_nt(a, b):
    return lax.dot_general(a, b, (((1,), (1,)), ((), ())), preferred_element_type=F32)


def diagonal_of(count):
    return lax.broadcasted_iota(jnp.int32, (count, HEAD), 0) == lax.broadcasted_iota(jnp.int32, (count, HEAD), 1)


def to_row(column):
    row = jnp.sum(jnp.where(diagonal_of(column.shape[0]), column, 0.0), axis=0, keepdims=True)
    return jnp.broadcast_to(row, (8, HEAD))


def to_column(rows, count):
    return jnp.sum(jnp.where(diagonal_of(count), rows[0:1], 0.0), axis=1, keepdims=True)


def inverse_rms(total):
    return lax.rsqrt(total / D + EPSILON)


def layout_of(lens_ref, token):
    segment = jnp.zeros_like(token)
    start = jnp.zeros_like(token)
    end = jnp.int32(0)
    for s in range(SEQS):
        length = lens_ref[s]
        end = end + length
        before = end <= token
        segment = segment + jnp.where(before, 1, 0)
        start = start + jnp.where(before, length, 0)
    return segment, token - start


def kernel(
    res, attn_gain, w_query, w_key, w_value, w_out, mlp_gain, w_gate, w_up, w_down, final_gain, w_head, lens, targets,
    out,
    target_row, res_chip, tiny, x_all, wqkv, wo, wg, wu, wd, wh, gain_a, gain_m, gain_f, mg, fg,
    part_own, part_pair, part_send, part_r1, part_mid, part_r2, qkv_all, attended,
    proj_send, proj_r1, proj_mid, proj_r2, stream_chip, mlp_all,
    gu_own, gu_send, gu_z0, gu_y0, gu_z1, gu_y1, mid_own, mid_send, mid2_own, mid2_send, hidden_all,
    down_send, down_r1, down_mid, down_r2, fin_a, fin_b, fin_c, logits, stat_recv, stat_all,
    local_sem, send_sem, recv_sem,
):
    row, col = lax.axis_index("row"), lax.axis_index("col")
    core = lax.rem(col, 2)
    other = 1 - core
    chip = lax.div(col, 2)
    cx, zh = lax.div(row, 2), lax.rem(row, 2)
    cy, zl = lax.div(chip, 2), lax.rem(chip, 2)
    cz = zh * 2 + zl
    sib = chip * 2 + other

    place = {"x": cx, "y": cy, "z": cz, "zl": zl, "zh": zh, "core": core}
    size = {"x": 4, "y": 4, "z": 4, "zl": 2, "zh": 2, "core": 2}

    def peer(axis, d):
        at = dict(place)
        at[axis] = lax.rem(at[axis] + d, size[axis])
        z = at["z"] if axis == "z" else at["zh"] * 2 + at["zl"]
        device = at["x"] * 2 + lax.div(z, 2), (at["y"] * 2 + lax.rem(z, 2)) * 2 + at["core"]
        return at[axis], device

    mine = pl.ds(pl.multiple_of(core * FEAT, 64), FEAT)
    waits, pending, numbers = {}, [], {"own": 0, "sent": 0}

    def own(name, src, dst):
        copy = pltpu.make_async_copy(src, dst, local_sem.at[numbers["own"]])
        numbers["own"] += 1
        copy.start()
        waits.setdefault(name, []).append(copy.wait)

    def one(axis, d, src, dst):
        i = numbers["sent"]
        numbers["sent"] += 1
        copy = remote(src, dst, send_sem.at[i], recv_sem.at[i], *peer(axis, d)[1])
        copy.start()
        pending.append(copy.wait_send)
        return copy

    def send(axis, src, dst):
        return [one(axis, d, src(peer(axis, d)[0]), dst(d)) for d in range(1, size[axis])]

    def spread(axis, ref):
        return send(axis, lambda at: ref, lambda d: ref)

    def arrive(copies):
        for copy in copies:
            copy.wait_recv()

    def swap(name, src, dst):
        waits.setdefault(name, []).append(one("core", 1, src, dst).wait_recv)

    def ready(*names):
        for name in names:
            for wait in waits.pop(name):
                wait()

    def flush(count):
        for finish in pending[:count]:
            finish()
        del pending[:count]

    def reduce(blocks, first, second, arrived, middle, last):
        copies = send(first, lambda at: blocks.at[at], lambda d: arrived.at[d])
        arrived[0] = blocks[place[first]]
        arrive(copies)
        middle[...] = jnp.sum(arrived[...], axis=0)
        arrive(send(second, lambda at: middle.at[at], lambda d: last))
        return middle[place[second]] + last[...]

    def column_sum(i, column, axes):
        value = to_row(column)
        for axis in axes:
            tiny[i, 0] = value
            arrive(send(axis, lambda at: tiny.at[i, 0], lambda d: tiny.at[i, d]))
            value = jnp.sum(tiny[i, 0:size[axis]], axis=0)
            i += 1
        return to_column(value, column.shape[0])

    own("residual", res, res_chip.at[core])
    own("targets", targets, target_row)
    own("gains", attn_gain, gain_a)
    own("gains", mlp_gain, gain_m)
    own("gains", final_gain, gain_f)
    own("wqkv", w_query, wqkv.at[:, 0:QW])
    own("wqkv", w_key, wqkv.at[:, QW:QW + HEAD])
    own("wqkv", w_value, wqkv.at[:, QW + HEAD:QKV])

    barrier = pltpu.get_barrier_semaphore()

    greeted = [("core", 1)] + [(axis, d) for axis in "xyz" for d in (1, 2, 3)]
    for axis, d in greeted:
        r, c = peer(axis, d)[1]
        pl.semaphore_signal(barrier, inc=1, device_id={"row": r, "col": c}, device_id_type=MESH)
    pl.semaphore_wait(barrier, len(greeted))

    ready("residual", "gains")
    x = res_chip[core].astype(F32)
    mg[core] = gain_m[...].reshape(1, FEAT)
    fg[core] = gain_f[...].reshape(1, FEAT)
    square = column_sum(0, jnp.sum(x * x, axis=1, keepdims=True), ("core", "y", "zl"))
    x_all[cx, zh] = (x * inverse_rms(square) * gain_a[...].reshape(1, FEAT)).astype(BF16)
    first = spread("zh", x_all.at[cx, zh])
    swap("residual_pair", res_chip.at[core], res_chip.at[core])
    swap("gains_pair", mg.at[core], mg.at[core])
    swap("gains_pair", fg.at[core], fg.at[core])
    own("wo", w_out, wo.at[mine])
    swap("wo", w_out, wo.at[mine])
    arrive(first)
    second = spread("x", x_all.at[cx])

    own_token = COLS * col + lax.broadcasted_iota(jnp.int32, (16, HEAD), 0)
    position = layout_of(lens, own_token)[1].astype(F32)
    lane = lax.broadcasted_iota(jnp.int32, (16, HEAD), 1)
    low_half = lane < HEAD // 2
    frequency = jnp.exp(jnp.where(low_half, lane, lane - HEAD // 2).astype(F32) * (-2.0 * math.log(ROPE_BASE) / HEAD))
    angle = position * frequency
    cosine = jnp.cos(angle)
    sine = jnp.where(low_half, -jnp.sin(angle), jnp.sin(angle))

    ready("wqkv")
    arrive(second)

    part = jnp.dot(x_all[...].reshape(T, FEAT), wqkv[...], preferred_element_type=F32)
    part_own[...] = part.reshape(4, 2, 2, 16, QKV)
    arrive([one("core", 1, part_own.at[:, :, other], part_pair)])
    part_send[...] = part_own[:, :, core] + part_pair[...]
    own("wg", w_gate.at[core], wg.at[mine])
    own("wu", w_up.at[core], wu.at[mine])
    swap("wg", w_gate.at[other], wg.at[mine])
    swap("wu", w_up.at[other], wu.at[mine])
    total = reduce(part_send, "y", "zl", part_r1, part_mid, part_r2)
    for h in range(Q_HEADS + 1):
        head = total[:, h * HEAD:(h + 1) * HEAD]
        turned = head * cosine + pltpu.roll(head, HEAD // 2, 1) * sine
        qkv_all[cy, zl, core, :, h * HEAD:(h + 1) * HEAD] = turned.astype(BF16)
    qkv_all[cy, zl, core, :, QW + HEAD:QKV] = total[:, QW + HEAD:QKV].astype(BF16)

    first = spread("zl", qkv_all.at[cy, zl, core])
    own("wd", w_down.at[core], wd.at[mine])
    swap("wd", w_down.at[other], wd.at[mine])
    arrive(first)
    second = spread("y", qkv_all.at[cy, :, core])

    row_i = lax.broadcasted_iota(jnp.int32, (T // 2, 1), 0)
    q_token = lax.div(row_i, 16) * 32 + core * 16 + lax.rem(row_i, 16)
    k_token = lax.broadcasted_iota(jnp.int32, (1, T), 1)
    q_segment = layout_of(lens, q_token)[0]
    k_segment = layout_of(lens, k_token)[0]
    allowed = (q_segment == k_segment) & (k_token <= q_token)

    arrive(second)
    pairs = qkv_all.at[:, :, core, :, QW:QKV]
    arrive(spread("core", pairs))

    keys = qkv_all[:, :, :, :, QW:QW + HEAD].reshape(T, HEAD)
    values = qkv_all[:, :, :, :, QW + HEAD:QKV].reshape(T, HEAD)
    for h in range(Q_HEADS):
        query = qkv_all[:, :, core, :, h * HEAD:(h + 1) * HEAD].reshape(T // 2, HEAD)
        scores = dot_nt(query, keys)
        scores = jnp.where(allowed, scores * HEAD ** (-0.5), MASKED)
        weights = jnp.exp(scores - jnp.max(scores, axis=1, keepdims=True))
        weights = (weights / jnp.sum(weights, axis=1, keepdims=True)).astype(BF16)
        result = jnp.dot(weights, values, preferred_element_type=F32)
        attended[:, h * HEAD:(h + 1) * HEAD] = result.astype(BF16)

    ready("wo", "residual_pair")
    proj_send[...] = dot_nt(attended[...], wo[...]).reshape(4, 2, 16, CHIP)

    projected = reduce(proj_send, "x", "zh", proj_r1, proj_mid, proj_r2)
    half_rows = pl.ds(pl.multiple_of(core * 16, 16), 16)
    residual = jnp.concatenate([res_chip[0, half_rows, :], res_chip[1, half_rows, :]], axis=1).astype(F32)
    stream = (residual + projected).astype(BF16)
    stream_chip[core] = stream
    stream = stream.astype(F32)

    def norm(i, value, gain):
        square = column_sum(i, jnp.sum(value * value, axis=1, keepdims=True), ("y", "zl"))
        gain = jnp.concatenate([gain[0], gain[1]], axis=1)
        return (value * inverse_rms(square) * gain).astype(BF16)

    ready("gains_pair")
    mlp_all[cx, zh, core] = norm(3, stream, mg)

    first = spread("zh", mlp_all.at[cx, zh, core])
    swap("stream_pair", stream_chip.at[core], stream_chip.at[core])
    own("wh", w_head, wh.at[core])
    swap("wh", w_head, wh.at[core])
    wh_at = len(pending) - 1
    arrive(first)
    arrive(spread("x", mlp_all.at[cx, :, core]))
    arrive(spread("core", mlp_all.at[:, :, core]))
    ready("wg", "wu")

    mlp_in = mlp_all[...].reshape(T, CHIP)

    def gate_up(i):
        low, width = CHUNKS[i]
        for half, weight in enumerate((wg, wu)):
            product = jnp.dot(mlp_in, weight[:, low:low + width], preferred_element_type=F32)
            product = product.reshape(4, 2, 32, width)
            gu_own[i, :, :, :, half * HALF:half * HALF + width] = product
            gu_send[i, :, :, :, half * HALF:half * HALF + width] = product.astype(BF16)
            if width < HALF:
                rest = jnp.zeros((4, 2, 32, HALF - width), F32)
                gu_own[i, :, :, :, half * HALF + width:(half + 1) * HALF] = rest
                gu_send[i, :, :, :, half * HALF + width:(half + 1) * HALF] = rest.astype(BF16)

    gate_up(0)
    sum_z0 = send("zl", lambda at: gu_send.at[0, :, at], lambda d: gu_z0)
    gate_up(1)
    sum_y1 = send("y", lambda at: gu_send.at[1, at], lambda d: gu_y1.at[d])
    flush(wh_at)

    arrive(sum_z0)
    mid_own[...] = gu_own[0, :, zl] + gu_z0[...].astype(F32)
    mid_send[...] = mid_own[...].astype(BF16)
    sum_y0 = send("y", lambda at: mid_send.at[at], lambda d: gu_y0.at[d])
    arrive(sum_y1)
    gu_y1[0] = jnp.zeros((2, 32, FFP), BF16)
    mid2_own[...] = gu_own[1, cy] + jnp.sum(gu_y1[...].astype(F32), axis=0)
    mid2_send[...] = mid2_own[1 - zl].astype(BF16)
    sum_z1 = send("zl", lambda at: mid2_send, lambda d: gu_z1)

    def activate(i, total):
        low, width = CHUNKS[i]
        gate = total[:, 0:width]
        hidden = gate / (1.0 + jnp.exp(-gate)) * total[:, HALF:HALF + width]
        hidden_all[cy, zl, :, low:low + width] = hidden.astype(BF16)

    def lanes(i):
        return pl.ds(CHUNKS[i][0], HALF)

    hidden_all[cy, zl, :, FF:FFP] = jnp.zeros((32, FFP - FF), BF16)
    arrive(sum_y0)
    gu_y0[0] = jnp.zeros((32, FFP), BF16)
    activate(0, mid_own[cy] + jnp.sum(gu_y0[...].astype(F32), axis=0))
    hid_z0 = spread("zl", hidden_all.at[cy, zl, :, lanes(0)])
    arrive(sum_z1)
    activate(1, mid2_own[zl] + gu_z1[...].astype(F32))
    hid_y1 = spread("y", hidden_all.at[cy, zl, :, lanes(1)])
    arrive(hid_z0)
    hid_y0 = spread("y", hidden_all.at[cy, :, :, lanes(0)])
    arrive(hid_y1)
    hid_z1 = spread("zl", hidden_all.at[:, zl, :, lanes(1)])
    ready("wd")

    product = jnp.zeros((T, CHIP), F32)
    for i, (low, width) in enumerate(CHUNKS):
        arrive(hid_y0 if i == 0 else hid_z1)
        hidden = hidden_all[:, :, :, low:low + width].reshape(T, width)
        product += dot_nt(hidden, wd[:, low:low + width])
    down_send[...] = product.reshape(4, 2, 32, CHIP)
    summed = reduce(down_send, "x", "zh", down_r1, down_mid, down_r2)
    ready("stream_pair")
    final = stream_chip[...].reshape(32, CHIP).astype(F32) + summed
    final = norm(5, final, fg)

    fin_a[cy, zl, cx, zh] = final[:, 0:256]
    fin_b[cy, zl, cx, zh] = final[:, 256:512]
    fin_c[cy, zl, cx, zh] = final[:, 512:640]

    parts = (fin_a, fin_b, fin_c)
    orders = ("zyx", "xzy", "yxz")

    def slab(p, stage):
        done = orders[p % 3][:stage]
        alone = {"y": pl.ds(cy, 1), "zl": pl.ds(zl, 1), "x": pl.ds(cx, 1), "zh": pl.ds(zh, 1)}
        pick = [pl.ds(0, size[k]) if k[0] in done else alone[k] for k in alone]
        return parts[p % 3].at[(*pick, pl.ds(p // 3 * 16, 16))]

    before = len(pending)
    gathers = [None] * 6
    for stage in range(3):
        for p in range(6):
            if stage:
                arrive(gathers[p])
            gathers[p] = spread(orders[p % 3][stage], slab(p, stage))
    flush(before)
    ready("wh")
    ready("targets")
    diagonal = lax.broadcasted_iota(jnp.int32, (T, T), 0) == lax.broadcasted_iota(jnp.int32, (T, T), 1)
    target = jnp.sum(jnp.where(diagonal, target_row[...].astype(F32), 0.0), axis=1, keepdims=True).astype(jnp.int32)
    for copies in gathers:
        arrive(copies)

    for y in range(4):
        pieces = []
        for z in range(2):
            pieces += [fin_a[y, z].reshape(T, 256), fin_b[y, z].reshape(T, 256), fin_c[y, z].reshape(T, HEAD)]
        states = jnp.concatenate(pieces, axis=1)
        for j in range(2):
            product = jnp.dot(states, wh[j, y * 2 * CHIP:(y + 1) * 2 * CHIP], preferred_element_type=F32)
            logits[j] = product if y == 0 else logits[j] + product
    both = [logits[j] for j in range(2)]
    top = jnp.maximum(*[jnp.max(l, axis=1, keepdims=True) for l in both])
    exponential = sum(jnp.sum(jnp.exp(l - top), axis=1, keepdims=True) for l in both)
    picked = jnp.zeros((T, 1), F32)
    for j in range(2):
        first = (row * COLS + chip * 2 + j) * VOCAB
        ids = first + lax.broadcasted_iota(jnp.int32, (T, VOCAB), 1)
        picked = picked + jnp.sum(jnp.where(ids == target, both[j], 0.0), axis=1, keepdims=True)
    lane = lax.broadcasted_iota(jnp.int32, (T, HEAD), 1)
    packed = jnp.where(lane == 0, top, jnp.where(lane == 1, exponential, picked))
    stat_recv[0, 0] = jnp.transpose(packed)[0:8, :]

    def merge(blocks):
        top = jnp.max(blocks[:, 0:1, :], axis=0)
        exponential = jnp.sum(blocks[:, 1:2, :] * jnp.exp(blocks[:, 0:1, :] - top[None]), axis=0)
        return top, exponential, jnp.sum(blocks[:, 2:3, :], axis=0)

    line = lax.broadcasted_iota(jnp.int32, (8, T), 0)

    def packed_merge(blocks):
        top, exponential, picked = merge(blocks)
        return jnp.where(line == 0, top, jnp.where(line == 1, exponential, picked))

    for stage, axis in enumerate("zyx"):
        arrive(send(axis, lambda at: stat_recv.at[stage, 0], lambda d: stat_recv.at[stage, d]))
        merged = packed_merge(stat_recv[stage])
        if stage < 2:
            stat_recv[stage + 1, 0] = merged
    stat_all[core] = merged
    arrive(spread("core", stat_all.at[core]))
    logprob = []
    for m in range(2):
        top, exponential, picked = stat_all[m, 0:1], stat_all[m, 1:2], stat_all[m, 2:3]
        logprob.append(picked - (top + jnp.log(exponential)))
    difference = logprob[0] - logprob[1]
    hit = line == k_segment
    sums = jnp.sum(jnp.where(hit, difference, 0.0), axis=1, keepdims=True)
    length = jnp.sum(jnp.where(hit, 1.0, 0.0), axis=1, keepdims=True)
    square8 = lax.broadcasted_iota(jnp.int32, (8, 8), 0) == lax.broadcasted_iota(jnp.int32, (8, 8), 1)
    out[...] = jnp.sum(jnp.where(square8, sums / length, 0.0), axis=0, keepdims=True)

    flush(len(pending))


def per_device(
    residual, attn_gain, w_query, w_key, w_value, w_out, mlp_gain, w_gate, w_up, w_down, final_gain, w_head,
    seq_lengths, targets,
):
    anywhere = pl.BlockSpec(memory_space=pl.ANY)
    vmem = pl.BlockSpec(memory_space=pltpu.VMEM)
    smem = pl.BlockSpec(memory_space=pltpu.SMEM)
    dma = pltpu.SemaphoreType.DMA
    result = pl.pallas_call(
        kernel,
        out_shape=jax.ShapeDtypeStruct((1, SEQS), F32),
        in_specs=[anywhere] * 12 + [smem, anywhere],
        out_specs=vmem,
        scratch_shapes=[
            pltpu.VMEM((1, T), jnp.int32),
            pltpu.VMEM((2, 32, FEAT), BF16),
            pltpu.VMEM((7, 4, 8, HEAD), F32),
            pltpu.VMEM((4, 2, 32, FEAT), BF16),
            pltpu.VMEM((FEAT, QKV), BF16),
            pltpu.VMEM((CHIP, QW), BF16),
            pltpu.VMEM((CHIP, FF), BF16),
            pltpu.VMEM((CHIP, FF), BF16),
            pltpu.VMEM((CHIP, FF), BF16),
            pltpu.VMEM((2, D, VOCAB), BF16),
            pltpu.VMEM((FEAT,), F32),
            pltpu.VMEM((FEAT,), F32),
            pltpu.VMEM((FEAT,), F32),
            pltpu.VMEM((2, 1, FEAT), F32),
            pltpu.VMEM((2, 1, FEAT), F32),
            pltpu.VMEM((4, 2, 2, 16, QKV), F32),
            pltpu.VMEM((4, 2, 16, QKV), F32),
            pltpu.VMEM((4, 2, 16, QKV), F32),
            pltpu.VMEM((4, 2, 16, QKV), F32),
            pltpu.VMEM((2, 16, QKV), F32),
            pltpu.VMEM((16, QKV), F32),
            pltpu.VMEM((4, 2, 2, 16, QKV), BF16),
            pltpu.VMEM((T // 2, QW), BF16),
            pltpu.VMEM((4, 2, 16, CHIP), F32),
            pltpu.VMEM((4, 2, 16, CHIP), F32),
            pltpu.VMEM((2, 16, CHIP), F32),
            pltpu.VMEM((16, CHIP), F32),
            pltpu.VMEM((2, 16, CHIP), BF16),
            pltpu.VMEM((4, 2, 2, 16, CHIP), BF16),
            pltpu.VMEM((2, 4, 2, 32, FFP), F32),
            pltpu.VMEM((2, 4, 2, 32, FFP), BF16),
            pltpu.VMEM((4, 32, FFP), BF16),
            pltpu.VMEM((4, 32, FFP), BF16),
            pltpu.VMEM((32, FFP), BF16),
            pltpu.VMEM((4, 2, 32, FFP), BF16),
            pltpu.VMEM((4, 32, FFP), F32),
            pltpu.VMEM((4, 32, FFP), BF16),
            pltpu.VMEM((2, 32, FFP), F32),
            pltpu.VMEM((32, FFP), BF16),
            pltpu.VMEM((4, 2, 32, FFP), BF16),
            pltpu.VMEM((4, 2, 32, CHIP), F32),
            pltpu.VMEM((4, 2, 32, CHIP), F32),
            pltpu.VMEM((2, 32, CHIP), F32),
            pltpu.VMEM((32, CHIP), F32),
            pltpu.VMEM((4, 2, 4, 2, 32, 256), BF16),
            pltpu.VMEM((4, 2, 4, 2, 32, 256), BF16),
            pltpu.VMEM((4, 2, 4, 2, 32, HEAD), BF16),
            pltpu.VMEM((2, T, VOCAB), F32),
            pltpu.VMEM((3, 4, 8, T), F32),
            pltpu.VMEM((2, 8, T), F32),
            dma((13,)), dma((160,)), dma((160,)),
        ],
        compiler_params=pltpu.CompilerParams(
            collective_id=0, has_side_effects=True, vmem_limit_bytes=60 * 1024 * 1024
        ),
    )(
        residual, attn_gain, w_query, w_key, w_value, w_out.T, mlp_gain, w_gate, w_up,
        jnp.swapaxes(w_down, 1, 2), final_gain, w_head, seq_lengths, targets.reshape(1, T),
    )
    return result.reshape(SEQS)


def solution(mesh):
    placed = (
        P("row", "col"), P("col"), P("col", "row"), P("col", "row"), P("col", "row"), P("row", "col"), P("col"),
        P(None, "col", "row"), P(None, "col", "row"), P(None, "row", "col"), P("col"), P(None, ("row", "col")), P(), P(),
    )
    return jax.shard_map(per_device, mesh=mesh, in_specs=placed, out_specs=P(), check_vma=False)
```

```python
import math

import jax
import jax.numpy as jnp
from jax import lax
from jax.experimental import pallas as pl
from jax.experimental.pallas import tpu as pltpu
from jax.sharding import PartitionSpec as P

T = 256
D = 5120
HEAD = 128
Q_HEADS = 5
QW = Q_HEADS * HEAD
QKV = QW + 2 * HEAD
SEQS = 8
FEAT = 320
CHIP = 2 * FEAT
FF = 1728
FFP = 1792
HALF = FFP // 2
CHUNKS = ((HALF, FF - HALF), (0, HALF))
VOCAB = 640
ROWS = 8
COLS = 16
CHIPS = 8
EPSILON = 1e-06
ROPE_BASE = 1000000.0
MASKED = -1e30
MESH = pl.DeviceIdType.MESH
F32 = jnp.float32
BF16 = jnp.bfloat16


def remote(src, dst, send, recv, row, col):
    return pltpu.make_async_remote_copy(
        src_ref=src, dst_ref=dst, send_sem=send, recv_sem=recv,
        device_id={"row": row, "col": col}, device_id_type=MESH,
    )


def each(start, stop, body):
    def step(i, carry):
        body(i)
        return carry

    lax.fori_loop(start, stop, step, 0)


def dot_nt(a, b):
    return lax.dot_general(a, b, (((1,), (1,)), ((), ())), preferred_element_type=F32)


def diagonal_of(count):
    return lax.broadcasted_iota(jnp.int32, (count, HEAD), 0) == lax.broadcasted_iota(jnp.int32, (count, HEAD), 1)


def to_row(column):
    row = jnp.sum(jnp.where(diagonal_of(column.shape[0]), column, 0.0), axis=0, keepdims=True)
    return jnp.broadcast_to(row, (8, HEAD))


def to_column(rows, count):
    return jnp.sum(jnp.where(diagonal_of(count), rows[0:1], 0.0), axis=1, keepdims=True)


def split_sum(total, width):
    high = total.astype(BF16)
    low = (total - high.astype(F32)).astype(BF16)
    shape = (total.shape[0], width)
    return (
        jnp.broadcast_to(high.astype(F32), shape).astype(BF16),
        jnp.broadcast_to(low.astype(F32), shape).astype(BF16),
    )


def inverse_rms(total):
    return lax.rsqrt(total / D + EPSILON)


def layout_of(lens_ref, token):
    segment = jnp.zeros_like(token)
    start = jnp.zeros_like(token)
    end = jnp.int32(0)
    for s in range(SEQS):
        length = lens_ref[s]
        end = end + length
        before = end <= token
        segment = segment + jnp.where(before, 1, 0)
        start = start + jnp.where(before, length, 0)
    return segment, token - start


def kernel(
    res, attn_gain, w_query, w_key, w_value, w_out, mlp_gain, w_gate, w_up, w_down, final_gain, w_head, lengths, targets,
    out,
    lens, target_row, res_chip, square_all, x_all, wqkv, wo, wg, wu, wd, wh, gain_a, gain_m, gain_f, mg, fg,
    part_own, part_pair, part_send, part_recv, qkv_all, attended, proj_send, proj_recv, stream_chip, norm_all, mlp_all,
    gu_own, gu_send, gu_z0, gu_y0, gu_z1, gu_y1, mid_own, mid_send, mid2_own, hidden_all, down_send, down_recv,
    fin_a, fin_b, fin_c, logits, stat_send, stat_recv, stat2_recv,
    local_sem, swap_send, swap_recv, sq_s, sq_r, x_s, x_r, pair_s, pair_r, part_s, part_r, qkv_s, qkv_r, proj_s, proj_r,
    norm_s, norm_r, stream_s, stream_r, y_s, y_r, z_s, z_r, down_s, down_r, fin_s, fin_r, st_s, st_r, st2_s, st2_r,
):
    row, col = lax.axis_index("row"), lax.axis_index("col")
    core = lax.rem(col, 2)
    other = 1 - core
    chip = lax.div(col, 2)
    cx, zh = lax.div(row, 2), lax.rem(row, 2)
    cy, zl = lax.div(chip, 2), lax.rem(chip, 2)
    cz = zh * 2 + zl
    sib = chip * 2 + other

    def row_at(d):
        return lax.rem(row + d, ROWS)

    def chip_at(d):
        return lax.rem(chip + d, CHIPS)

    def col_at(d):
        return lax.rem(col + d, COLS)

    def at_xyz(x, y, z):
        return x * 2 + lax.div(z, 2), (y * 2 + lax.rem(z, 2)) * 2 + core

    mine = pl.ds(pl.multiple_of(core * FEAT, 64), FEAT)
    waits, pending, numbers = {}, [], {"own": 0, "pair": 0}

    def own(name, src, dst):
        copy = pltpu.make_async_copy(src, dst, local_sem.at[numbers["own"]])
        numbers["own"] += 1
        copy.start()
        waits.setdefault(name, []).append(copy.wait)

    def swap(name, src, dst):
        i = numbers["pair"]
        numbers["pair"] += 1
        copy = remote(src, dst, swap_send.at[i], swap_recv.at[i], row, sib)
        copy.start()
        waits.setdefault(name, []).append(copy.wait_recv)
        pending.append(copy.wait_send)

    def ready(*names):
        for name in names:
            for wait in waits.pop(name):
                wait()

    def start(first, stop, copy):
        each(first, stop, lambda d: copy(d).start())
        pending.append(lambda: each(first, stop, lambda d: copy(d).wait_send()))

    def arrive(first, stop, copy):
        each(first, stop, lambda d: copy(d).wait_recv())

    def flush():
        for finish in pending:
            finish()
        pending.clear()

    own("residual", res, res_chip.at[core])
    own("targets", targets, target_row)
    own("lens", lengths, lens)
    own("gains", attn_gain, gain_a)
    own("gains", mlp_gain, gain_m)
    own("gains", final_gain, gain_f)
    own("wqkv", w_query, wqkv.at[:, 0:QW])
    own("wqkv", w_key, wqkv.at[:, QW:QW + HEAD])
    own("wqkv", w_value, wqkv.at[:, QW + HEAD:QKV])

    barrier = pltpu.get_barrier_semaphore()

    def greet(r, c):
        pl.semaphore_signal(barrier, inc=1, device_id={"row": r, "col": c}, device_id_type=MESH)

    each(1, ROWS, lambda d: greet(row_at(d), col))
    each(1, ROWS, lambda d: greet(row_at(d), sib))
    each(1, COLS, lambda d: greet(row, col_at(d)))
    cross_z = lax.rem(cz + 1 + 2 * (1 - zl), 4)
    cross_row, cross_col = at_xyz(cx, cy, cross_z)
    greet(cross_row, cross_col)
    ready("residual", "gains")
    x = res_chip[core].astype(F32)
    square_all[0] = to_row(jnp.sum(x * x, axis=1, keepdims=True))
    pl.semaphore_wait(barrier, 2 * (ROWS - 1) + (COLS - 1) + 1)

    def sq_copy(d):
        return remote(square_all.at[0], square_all.at[d], sq_s.at[d], sq_r.at[d], row, col_at(d))

    start(1, COLS, sq_copy)
    mg[core] = gain_m[...].reshape(1, FEAT)
    fg[core] = gain_f[...].reshape(1, FEAT)

    ready("lens")
    own_token = COLS * col + lax.broadcasted_iota(jnp.int32, (16, HEAD), 0)
    position = layout_of(lens, own_token)[1].astype(F32)
    lane = lax.broadcasted_iota(jnp.int32, (16, HEAD), 1)
    low_half = lane < HEAD // 2
    frequency = jnp.exp(jnp.where(low_half, lane, lane - HEAD // 2).astype(F32) * (-2.0 * math.log(ROPE_BASE) / HEAD))
    angle = position * frequency
    cosine = jnp.cos(angle)
    sine = jnp.where(low_half, -jnp.sin(angle), jnp.sin(angle))

    arrive(1, COLS, sq_copy)
    square = to_column(jnp.sum(square_all[...], axis=0), 32)
    x_all[row] = (x * inverse_rms(square) * gain_a[...].reshape(1, FEAT)).astype(BF16)

    def x_copy(d):
        return remote(x_all.at[row], x_all.at[row], x_s.at[d], x_r.at[d], row_at(d), col)

    start(1, ROWS, x_copy)
    swap("residual_pair", res_chip.at[core], res_chip.at[core])
    swap("gains_pair", mg.at[core], mg.at[core])
    swap("gains_pair", fg.at[core], fg.at[core])
    own("wo", w_out, wo.at[mine])
    swap("wo", w_out, wo.at[mine])
    ready("wqkv")
    arrive(1, ROWS, x_copy)

    part = jnp.dot(x_all[...].reshape(T, FEAT), wqkv[...], preferred_element_type=F32)
    part_own[...] = part.reshape(CHIPS, 2, 16, QKV)
    pair = remote(part_own.at[:, other], part_pair, pair_s, pair_r, row, sib)
    pair.start()
    pending.append(pair.wait_send)
    pair.wait_recv()
    part_send[...] = part_own[:, core] + part_pair[...]

    def part_copy(d):
        c = chip_at(d)
        return remote(part_send.at[c], part_recv.at[d], part_s.at[d], part_r.at[d], row, c * 2 + core)

    start(1, CHIPS, part_copy)
    own("wg", w_gate.at[core], wg.at[mine])
    own("wu", w_up.at[core], wu.at[mine])
    swap("wg", w_gate.at[other], wg.at[mine])
    swap("wu", w_up.at[other], wu.at[mine])
    part_recv[0] = part_send[chip]
    arrive(1, CHIPS, part_copy)

    total = jnp.sum(part_recv[...], axis=0)
    for h in range(Q_HEADS + 1):
        head = total[:, h * HEAD:(h + 1) * HEAD]
        turned = head * cosine + pltpu.roll(head, HEAD // 2, 1) * sine
        qkv_all[chip, core, :, h * HEAD:(h + 1) * HEAD] = turned.astype(BF16)
    qkv_all[chip, core, :, QW + HEAD:QKV] = total[:, QW + HEAD:QKV].astype(BF16)

    own_qkv = qkv_all.at[chip, core]
    own_kv = qkv_all.at[chip, core, :, QW:QKV]

    def qkv_copy(d):
        return remote(own_qkv, own_qkv, qkv_s.at[d], qkv_r.at[d], row, chip_at(d) * 2 + core)

    def kv_copy(d):
        return remote(own_kv, own_kv, qkv_s.at[CHIPS + d], qkv_r.at[CHIPS + d], row, chip_at(d) * 2 + other)

    start(1, CHIPS, qkv_copy)
    start(0, CHIPS, kv_copy)
    own("wd", w_down.at[core], wd.at[mine])
    swap("wd", w_down.at[other], wd.at[mine])

    row_i = lax.broadcasted_iota(jnp.int32, (T // 2, 1), 0)
    q_token = lax.div(row_i, 16) * 32 + core * 16 + lax.rem(row_i, 16)
    k_token = lax.broadcasted_iota(jnp.int32, (1, T), 1)
    q_segment = layout_of(lens, q_token)[0]
    k_segment = layout_of(lens, k_token)[0]
    allowed = (q_segment == k_segment) & (k_token <= q_token)

    arrive(1, CHIPS, qkv_copy)
    arrive(0, CHIPS, kv_copy)

    keys = qkv_all[:, :, :, QW:QW + HEAD].reshape(T, HEAD)
    values = qkv_all[:, :, :, QW + HEAD:QKV].reshape(T, HEAD)
    for h in range(Q_HEADS):
        query = qkv_all[:, core, :, h * HEAD:(h + 1) * HEAD].reshape(T // 2, HEAD)
        scores = dot_nt(query, keys)
        scores = jnp.where(allowed, scores * HEAD ** (-0.5), MASKED)
        weights = jnp.exp(scores - jnp.max(scores, axis=1, keepdims=True))
        weights = (weights / jnp.sum(weights, axis=1, keepdims=True)).astype(BF16)
        result = jnp.dot(weights, values, preferred_element_type=F32)
        attended[:, h * HEAD:(h + 1) * HEAD] = result.astype(BF16)

    ready("wo", "residual_pair")
    proj_send[...] = dot_nt(attended[...], wo[...]).reshape(ROWS, 16, CHIP)

    def proj_copy(d):
        r = row_at(d)
        return remote(proj_send.at[r], proj_recv.at[d], proj_s.at[d], proj_r.at[d], r, col)

    start(1, ROWS, proj_copy)
    proj_recv[0] = proj_send[row]
    arrive(1, ROWS, proj_copy)
    half_rows = pl.ds(pl.multiple_of(core * 16, 16), 16)
    residual = jnp.concatenate([res_chip[0, half_rows, :], res_chip[1, half_rows, :]], axis=1).astype(F32)
    stream = (residual + jnp.sum(proj_recv[...], axis=0)).astype(BF16)
    stream_chip[core] = stream
    stream = stream.astype(F32)

    def norm(value, gain):
        count = value.shape[0]
        norm_all[0] = to_row(jnp.sum(value * value, axis=1, keepdims=True))

        def copy(d):
            return remote(
                norm_all.at[0], norm_all.at[d], norm_s.at[d], norm_r.at[d], row, chip_at(d) * 2 + core
            )

        start(1, CHIPS, copy)
        arrive(1, CHIPS, copy)
        square = to_column(jnp.sum(norm_all[...], axis=0), count)
        gain = jnp.concatenate([gain[0], gain[1]], axis=1)
        return (value * inverse_rms(square) * gain).astype(BF16)

    ready("gains_pair")
    mlp_all[row, core] = norm(stream, mg)

    own_stream = mlp_all.at[row, core]

    def stream_copy(d):
        return remote(own_stream, own_stream, stream_s.at[d], stream_r.at[d], row_at(d), col)

    def stream_cross(d):
        return remote(own_stream, own_stream, stream_s.at[ROWS + d], stream_r.at[ROWS + d], row_at(d), sib)

    start(1, ROWS, stream_copy)
    start(0, ROWS, stream_cross)
    swap("stream_pair", stream_chip.at[core], stream_chip.at[core])
    own("wh", w_head, wh.at[core])
    swap("wh", w_head, wh.at[core])
    wh_at = len(pending) - 1
    ready("wg", "wu")
    arrive(1, ROWS, stream_copy)
    arrive(0, ROWS, stream_cross)

    mlp_in = mlp_all[...].reshape(T, CHIP)

    def y_peer(d):
        return (lax.rem(cy + d, 4) * 2 + zl) * 2 + core

    z_peer = (cy * 2 + 1 - zl) * 2 + core

    def to_y(src, dst, i):
        def copy(d):
            return remote(src(lax.rem(cy + d, 4)), dst(d), y_s.at[i, d], y_r.at[i, d], row, y_peer(d))

        return copy

    def to_z(src, dst, i):
        return lambda d: remote(src, dst, z_s.at[i], z_r.at[i], row, z_peer)

    def gate_up(i):
        low, width = CHUNKS[i]
        for half, weight in enumerate((wg, wu)):
            product = jnp.dot(mlp_in, weight[:, low:low + width], preferred_element_type=F32)
            product = product.reshape(4, 2, 32, width)
            gu_own[i, :, :, :, half * HALF:half * HALF + width] = product
            gu_send[i, :, :, :, half * HALF:half * HALF + width] = product.astype(BF16)
            if width < HALF:
                rest = jnp.zeros((4, 2, 32, HALF - width), F32)
                gu_own[i, :, :, :, half * HALF + width:(half + 1) * HALF] = rest
                gu_send[i, :, :, :, half * HALF + width:(half + 1) * HALF] = rest.astype(BF16)

    gate_up(0)
    sum_z0 = to_z(gu_send.at[0, :, 1 - zl], gu_z0, 0)
    start(0, 1, sum_z0)
    gate_up(1)
    sum_y1 = to_y(lambda y: gu_send.at[1, y], lambda d: gu_y1.at[d], 0)
    start(1, 4, sum_y1)
    held = pending[-2:]
    del pending[-2:]
    wh_swap = pending.pop(wh_at)
    flush()
    pending.extend([wh_swap] + held)

    arrive(0, 1, sum_z0)
    mid_own[...] = gu_own[0, :, zl] + gu_z0[...].astype(F32)
    mid_send[...] = mid_own[...].astype(BF16)
    sum_y0 = to_y(lambda y: mid_send.at[y], lambda d: gu_y0.at[d], 1)
    start(1, 4, sum_y0)
    arrive(1, 4, sum_y1)
    gu_y1[0] = jnp.zeros((2, 32, FFP), BF16)
    mid2_own[...] = gu_own[1, cy] + jnp.sum(gu_y1[...].astype(F32), axis=0)
    sum_z1 = to_z(mid2_own.at[1 - zl], gu_z1, 1)
    start(0, 1, sum_z1)

    def activate(i, total):
        low, width = CHUNKS[i]
        gate = total[:, 0:width]
        hidden = gate / (1.0 + jnp.exp(-gate)) * total[:, HALF:HALF + width]
        hidden_all[cy, zl, :, low:low + width] = hidden.astype(BF16)

    def lanes(i):
        return pl.ds(CHUNKS[i][0], HALF)

    hidden_all[cy, zl, :, FF:FFP] = jnp.zeros((32, FFP - FF), BF16)
    arrive(1, 4, sum_y0)
    gu_y0[0] = jnp.zeros((32, FFP), BF16)
    activate(0, mid_own[cy] + jnp.sum(gu_y0[...].astype(F32), axis=0))
    own0 = hidden_all.at[cy, zl, :, lanes(0)]
    hid_z0 = to_z(own0, own0, 2)
    start(0, 1, hid_z0)
    arrive(0, 1, sum_z1)
    activate(1, mid2_own[zl] + gu_z1[...])
    own1 = hidden_all.at[cy, zl, :, lanes(1)]
    hid_y1 = to_y(lambda y: own1, lambda d: own1, 2)
    start(1, 4, hid_y1)
    arrive(0, 1, hid_z0)
    both0 = hidden_all.at[cy, :, :, lanes(0)]
    hid_y0 = to_y(lambda y: both0, lambda d: both0, 3)
    start(1, 4, hid_y0)
    arrive(1, 4, hid_y1)
    four1 = hidden_all.at[:, zl, :, lanes(1)]
    hid_z1 = to_z(four1, four1, 3)
    start(0, 1, hid_z1)
    ready("wd")

    product = jnp.zeros((T, CHIP), F32)
    for i, (low, width) in enumerate(CHUNKS):
        arrive(*((1, 4, hid_y0) if i == 0 else (0, 1, hid_z1)))
        hidden = hidden_all[:, :, :, low:low + width].reshape(T, width)
        product += dot_nt(hidden, wd[:, low:low + width])
    down_send[...] = product.reshape(ROWS, 32, CHIP)

    def down_copy(d):
        r = row_at(d)
        return remote(down_send.at[r], down_recv.at[d], down_s.at[d], down_r.at[d], r, col)

    start(1, ROWS, down_copy)
    down_recv[0] = down_send[row]
    arrive(1, ROWS, down_copy)
    ready("stream_pair")
    final = stream_chip[...].reshape(32, CHIP).astype(F32) + jnp.sum(down_recv[...], axis=0)
    square_hi, square_lo = split_sum(jnp.sum(final * final, axis=1, keepdims=True), 64)
    final = (final * jnp.concatenate([fg[0], fg[1]], axis=1)).astype(BF16)

    fin_a[cy, zl, cx, zh] = final[:, 0:256]
    fin_b[cy, zl, cx, zh] = final[:, 256:512]
    fin_c[cy, zl, cx, zh, :, 0:128] = final[:, 512:640]
    fin_c[cy, zl, cx, zh, :, 128:192] = square_hi
    fin_c[cy, zl, cx, zh, :, 192:256] = square_lo

    parts = (fin_a, fin_b, fin_c)
    orders = ("zyx", "xzy", "yxz")

    def axis_copies(p, stage):
        order = orders[p % 3]
        axis, done = order[stage], order[:stage]
        one = {"y": pl.ds(cy, 1), "x": pl.ds(cx, 1), "zl": pl.ds(zl, 1), "zh": pl.ds(zh, 1)}
        full = {"y": pl.ds(0, 4), "x": pl.ds(0, 4), "zl": pl.ds(0, 2), "zh": pl.ds(0, 2)}
        pick = {k: full[k] if k[0] in done else one[k] for k in one}
        ref = parts[p % 3].at[pick["y"], pick["zl"], pick["x"], pick["zh"], pl.ds(p // 3 * 16, 16)]
        copies = []
        for d in (2, 1, 3):
            x = lax.rem(cx + d, 4) if axis == "x" else cx
            y = lax.rem(cy + d, 4) if axis == "y" else cy
            z = lax.rem(cz + d, 4) if axis == "z" else cz
            r, c = at_xyz(x, y, z)
            i = (p * 3 + stage) * 3 + d - 1
            copies.append(remote(ref, ref, fin_s.at[i], fin_r.at[i], r, c))
        return copies

    gathers = [[axis_copies(p, stage) for p in range(6)] for stage in range(3)]
    for stage in range(3):
        for p in range(6):
            if stage:
                for copy in gathers[stage - 1][p]:
                    copy.wait_recv()
            for copy in gathers[stage][p]:
                copy.start()
                pending.append(copy.wait_send)
    last = pending[-18:]
    del pending[-18:]
    flush()
    pending.extend(last)
    ready("wh")
    ready("targets")
    diagonal = lax.broadcasted_iota(jnp.int32, (T, T), 0) == lax.broadcasted_iota(jnp.int32, (T, T), 1)
    target = jnp.sum(jnp.where(diagonal, target_row[...].astype(F32), 0.0), axis=1, keepdims=True).astype(jnp.int32)
    for p in range(6):
        for copy in gathers[2][p]:
            copy.wait_recv()

    square = jnp.zeros((T, 1), F32)
    for y in range(4):
        pieces = []
        for z in range(2):
            c = fin_c[y, z].reshape(T, 256)
            square = square + c[:, 128:129].astype(F32) + c[:, 192:193].astype(F32)
            pieces += [fin_a[y, z].reshape(T, 256), fin_b[y, z].reshape(T, 256), c[:, 0:128]]
        states = jnp.concatenate(pieces, axis=1)
        for j in range(2):
            product = jnp.dot(states, wh[j, y * 2 * CHIP:(y + 1) * 2 * CHIP], preferred_element_type=F32)
            logits[j] = product if y == 0 else logits[j] + product
    scale = inverse_rms(square)
    both = [logits[j] * scale for j in range(2)]
    top = jnp.maximum(*[jnp.max(l, axis=1, keepdims=True) for l in both])
    exponential = sum(jnp.sum(jnp.exp(l - top), axis=1, keepdims=True) for l in both)
    picked = jnp.zeros((T, 1), F32)
    for j in range(2):
        first = (row * COLS + chip * 2 + j) * VOCAB
        ids = first + lax.broadcasted_iota(jnp.int32, (T, VOCAB), 1)
        picked = picked + jnp.sum(jnp.where(ids == target, both[j], 0.0), axis=1, keepdims=True)
    lane = lax.broadcasted_iota(jnp.int32, (T, HEAD), 1)
    packed = jnp.where(lane == 0, top, jnp.where(lane == 1, exponential, picked))
    stat_recv[0, 0] = jnp.transpose(packed)[0:8, :]

    def merge(blocks):
        top = jnp.max(blocks[:, 0:1, :], axis=0)
        exponential = jnp.sum(blocks[:, 1:2, :] * jnp.exp(blocks[:, 0:1, :] - top[None]), axis=0)
        return top, exponential, jnp.sum(blocks[:, 2:3, :], axis=0)

    line = lax.broadcasted_iota(jnp.int32, (8, T), 0)

    def packed_merge(blocks):
        top, exponential, picked = merge(blocks)
        return jnp.where(line == 0, top, jnp.where(line == 1, exponential, picked))

    for stage in range(2):
        def st_copy(d):
            if stage == 0:
                r, c = at_xyz(cx, cy, lax.rem(cz + d, 4))
            else:
                r, c = at_xyz(cx, lax.rem(cy + d, 4), cz)
            return remote(stat_recv.at[stage, 0], stat_recv.at[stage, d], st_s.at[stage, d], st_r.at[stage, d], r, c)

        each(1, 4, lambda d: st_copy(d).start())
        arrive(1, 4, st_copy)
        each(1, 4, lambda d: st_copy(d).wait_send())
        merged = packed_merge(stat_recv[stage])
        if stage == 0:
            stat_recv[1, 0] = merged
        else:
            stat_send[...] = merged
            stat2_recv[core, cx] = merged
    own_stat = stat2_recv.at[core, cx]

    def st2_copy(d):
        return remote(stat_send, own_stat, st2_s.at[d], st2_r.at[d], lax.rem(cx + d, 4) * 2 + zh, col)

    def st2_cross(d):
        return remote(stat_send, own_stat, st2_s.at[4 + d], st2_r.at[4 + d], lax.rem(cx + d, 4) * 2 + zh, sib)

    start(1, 4, st2_copy)
    start(0, 4, st2_cross)
    arrive(1, 4, st2_copy)
    arrive(0, 4, st2_cross)
    logprob = []
    for m in range(2):
        top, exponential, picked = merge(stat2_recv[m])
        logprob.append(picked - (top + jnp.log(exponential)))
    difference = logprob[0] - logprob[1]
    hit = line == k_segment
    sums = jnp.sum(jnp.where(hit, difference, 0.0), axis=1, keepdims=True)
    length = jnp.sum(jnp.where(hit, 1.0, 0.0), axis=1, keepdims=True)
    square8 = lax.broadcasted_iota(jnp.int32, (8, 8), 0) == lax.broadcasted_iota(jnp.int32, (8, 8), 1)
    out[...] = jnp.sum(jnp.where(square8, sums / length, 0.0), axis=0, keepdims=True)

    flush()


def per_device(
    residual, attn_gain, w_query, w_key, w_value, w_out, mlp_gain, w_gate, w_up, w_down, final_gain, w_head,
    seq_lengths, targets,
):
    anywhere = pl.BlockSpec(memory_space=pl.ANY)
    vmem = pl.BlockSpec(memory_space=pltpu.VMEM)
    dma = pltpu.SemaphoreType.DMA
    result = pl.pallas_call(
        kernel,
        out_shape=jax.ShapeDtypeStruct((1, SEQS), F32),
        in_specs=[anywhere] * 12 + [anywhere, anywhere],
        out_specs=vmem,
        scratch_shapes=[
            pltpu.SMEM((SEQS,), jnp.int32),
            pltpu.VMEM((1, T), jnp.int32),
            pltpu.VMEM((2, 32, FEAT), BF16),
            pltpu.VMEM((COLS, 8, HEAD), F32),
            pltpu.VMEM((ROWS, 32, FEAT), BF16),
            pltpu.VMEM((FEAT, QKV), BF16),
            pltpu.VMEM((CHIP, QW), BF16),
            pltpu.VMEM((CHIP, FF), BF16),
            pltpu.VMEM((CHIP, FF), BF16),
            pltpu.VMEM((CHIP, FF), BF16),
            pltpu.VMEM((2, D, VOCAB), BF16),
            pltpu.VMEM((FEAT,), F32),
            pltpu.VMEM((FEAT,), F32),
            pltpu.VMEM((FEAT,), F32),
            pltpu.VMEM((2, 1, FEAT), F32),
            pltpu.VMEM((2, 1, FEAT), F32),
            pltpu.VMEM((CHIPS, 2, 16, QKV), F32),
            pltpu.VMEM((CHIPS, 16, QKV), F32),
            pltpu.VMEM((CHIPS, 16, QKV), F32),
            pltpu.VMEM((CHIPS, 16, QKV), F32),
            pltpu.VMEM((CHIPS, 2, 16, QKV), BF16),
            pltpu.VMEM((T // 2, QW), BF16),
            pltpu.VMEM((ROWS, 16, CHIP), F32),
            pltpu.VMEM((ROWS, 16, CHIP), F32),
            pltpu.VMEM((2, 16, CHIP), BF16),
            pltpu.VMEM((CHIPS, 8, HEAD), F32),
            pltpu.VMEM((ROWS, 2, 16, CHIP), BF16),
            pltpu.VMEM((2, 4, 2, 32, FFP), F32),
            pltpu.VMEM((2, 4, 2, 32, FFP), BF16),
            pltpu.VMEM((4, 32, FFP), BF16),
            pltpu.VMEM((4, 32, FFP), BF16),
            pltpu.VMEM((32, FFP), F32),
            pltpu.VMEM((4, 2, 32, FFP), BF16),
            pltpu.VMEM((4, 32, FFP), F32),
            pltpu.VMEM((4, 32, FFP), BF16),
            pltpu.VMEM((2, 32, FFP), F32),
            pltpu.VMEM((4, 2, 32, FFP), BF16),
            pltpu.VMEM((ROWS, 32, CHIP), F32),
            pltpu.VMEM((ROWS, 32, CHIP), F32),
            pltpu.VMEM((4, 2, 4, 2, 32, 256), BF16),
            pltpu.VMEM((4, 2, 4, 2, 32, 256), BF16),
            pltpu.VMEM((4, 2, 4, 2, 32, 256), BF16),
            pltpu.VMEM((2, T, VOCAB), F32),
            pltpu.VMEM((8, T), F32),
            pltpu.VMEM((2, 4, 8, T), F32),
            pltpu.VMEM((2, 4, 8, T), F32),
            dma((14,)), dma((9,)), dma((9,)),
            dma((COLS,)), dma((COLS,)),
            dma((ROWS,)), dma((ROWS,)),
            dma, dma,
            dma((CHIPS,)), dma((CHIPS,)),
            dma((COLS,)), dma((COLS,)),
            dma((ROWS,)), dma((ROWS,)),
            dma((CHIPS,)), dma((CHIPS,)),
            dma((2 * ROWS,)), dma((2 * ROWS,)),
            dma((4, 4)), dma((4, 4)),
            dma((4,)), dma((4,)),
            dma((ROWS,)), dma((ROWS,)),
            dma((54,)), dma((54,)),
            dma((2, 4)), dma((2, 4)),
            dma((CHIPS,)), dma((CHIPS,)),
        ],
        compiler_params=pltpu.CompilerParams(
            collective_id=0, has_side_effects=True, vmem_limit_bytes=60 * 1024 * 1024
        ),
    )(
        residual, attn_gain, w_query, w_key, w_value, w_out.T, mlp_gain, w_gate, w_up,
        jnp.swapaxes(w_down, 1, 2), final_gain, w_head, seq_lengths, targets.reshape(1, T),
    )
    return result.reshape(SEQS)


def solution(mesh):
    placed = (
        P("row", "col"), P("col"), P("col", "row"), P("col", "row"), P("col", "row"), P("row", "col"), P("col"),
        P(None, "col", "row"), P(None, "col", "row"), P(None, "row", "col"), P("col"), P(None, ("row", "col")), P(), P(),
    )
    return jax.shard_map(per_device, mesh=mesh, in_specs=placed, out_specs=P(), check_vma=False)
```

```python
import math

import jax
import jax.numpy as jnp
from jax import lax
from jax.experimental import pallas as pl
from jax.experimental.pallas import tpu as pltpu
from jax.sharding import PartitionSpec as P

T = 256
D = 5120
HEAD = 128
Q_HEADS = 5
QW = Q_HEADS * HEAD
QKV = QW + 2 * HEAD
SEQS = 8
FEAT = 320
CHIP = 2 * FEAT
FF = 1728
FFP = 1792
HALF = FFP // 2
CHUNKS = ((HALF, FF - HALF), (0, HALF))
VOCAB = 640
ROWS = 8
COLS = 16
CHIPS = 8
EPSILON = 1e-06
ROPE_BASE = 1000000.0
MASKED = -1e30
MESH = pl.DeviceIdType.MESH
F32 = jnp.float32
BF16 = jnp.bfloat16


def remote(src, dst, send, recv, row, col):
    return pltpu.make_async_remote_copy(
        src_ref=src, dst_ref=dst, send_sem=send, recv_sem=recv,
        device_id={"row": row, "col": col}, device_id_type=MESH,
    )


def each(start, stop, body):
    def step(i, carry):
        body(i)
        return carry

    lax.fori_loop(start, stop, step, 0)


def dot_nt(a, b):
    return lax.dot_general(a, b, (((1,), (1,)), ((), ())), preferred_element_type=F32)


def diagonal_of(count):
    return lax.broadcasted_iota(jnp.int32, (count, HEAD), 0) == lax.broadcasted_iota(jnp.int32, (count, HEAD), 1)


def to_row(column):
    row = jnp.sum(jnp.where(diagonal_of(column.shape[0]), column, 0.0), axis=0, keepdims=True)
    return jnp.broadcast_to(row, (8, HEAD))


def to_column(rows, count):
    return jnp.sum(jnp.where(diagonal_of(count), rows[0:1], 0.0), axis=1, keepdims=True)


def split_sum(total, width):
    high = total.astype(BF16)
    low = (total - high.astype(F32)).astype(BF16)
    shape = (total.shape[0], width)
    return (
        jnp.broadcast_to(high.astype(F32), shape).astype(BF16),
        jnp.broadcast_to(low.astype(F32), shape).astype(BF16),
    )


def inverse_rms(total):
    return lax.rsqrt(total / D + EPSILON)


def layout_of(lens_ref, token):
    segment = jnp.zeros_like(token)
    start = jnp.zeros_like(token)
    end = jnp.int32(0)
    for s in range(SEQS):
        length = lens_ref[s]
        end = end + length
        before = end <= token
        segment = segment + jnp.where(before, 1, 0)
        start = start + jnp.where(before, length, 0)
    return segment, token - start


def kernel(
    res, attn_gain, w_query, w_key, w_value, w_out, mlp_gain, w_gate, w_up, w_down, final_gain, w_head, lengths, targets,
    out,
    lens, target_row, res_chip, square_all, x_all, wqkv, wo, wg, wu, wd, wh, gain_a, gain_m, gain_f, mg, fg,
    part_own, part_pair, part_send, part_recv, qkv_all, attended, proj_send, proj_recv, stream_all,
    gu_own, gu_send, gu_z0, gu_y0, gu_z1, gu_y1, mid_own, mid_send, mid2_own, hidden_all, down_send, down_recv,
    fin_a, fin_b, fin_c, logits, stat_send, stat_recv, stat2_recv,
    local_sem, swap_send, swap_recv, sq_s, sq_r, x_s, x_r, pair_s, pair_r, part_s, part_r, qkv_s, qkv_r, proj_s, proj_r,
    stream_s, stream_r, y_s, y_r, z_s, z_r, down_s, down_r, fin_s, fin_r, st_s, st_r, st2_s, st2_r,
):
    row, col = lax.axis_index("row"), lax.axis_index("col")
    core = lax.rem(col, 2)
    other = 1 - core
    chip = lax.div(col, 2)
    cx, zh = lax.div(row, 2), lax.rem(row, 2)
    cy, zl = lax.div(chip, 2), lax.rem(chip, 2)
    cz = zh * 2 + zl
    sib = chip * 2 + other

    def row_at(d):
        return lax.rem(row + d, ROWS)

    def chip_at(d):
        return lax.rem(chip + d, CHIPS)

    def col_at(d):
        return lax.rem(col + d, COLS)

    def at_xyz(x, y, z):
        return x * 2 + lax.div(z, 2), (y * 2 + lax.rem(z, 2)) * 2 + core

    mine = pl.ds(pl.multiple_of(core * FEAT, 64), FEAT)
    waits, pending, numbers = {}, [], {"own": 0, "pair": 0}

    def own(name, src, dst):
        copy = pltpu.make_async_copy(src, dst, local_sem.at[numbers["own"]])
        numbers["own"] += 1
        copy.start()
        waits.setdefault(name, []).append(copy.wait)

    def swap(name, src, dst):
        i = numbers["pair"]
        numbers["pair"] += 1
        copy = remote(src, dst, swap_send.at[i], swap_recv.at[i], row, sib)
        copy.start()
        waits.setdefault(name, []).append(copy.wait_recv)
        pending.append(copy.wait_send)

    def ready(*names):
        for name in names:
            for wait in waits.pop(name):
                wait()

    def start(first, stop, copy):
        each(first, stop, lambda d: copy(d).start())
        pending.append(lambda: each(first, stop, lambda d: copy(d).wait_send()))

    def arrive(first, stop, copy):
        each(first, stop, lambda d: copy(d).wait_recv())

    def flush():
        for finish in pending:
            finish()
        pending.clear()

    own("residual", res, res_chip.at[core])
    own("targets", targets, target_row)
    own("lens", lengths, lens)
    own("gains", attn_gain, gain_a)
    own("gains", mlp_gain, gain_m)
    own("gains", final_gain, gain_f)
    own("wqkv", w_query, wqkv.at[:, 0:QW])
    own("wqkv", w_key, wqkv.at[:, QW:QW + HEAD])
    own("wqkv", w_value, wqkv.at[:, QW + HEAD:QKV])

    barrier = pltpu.get_barrier_semaphore()

    def greet(r, c):
        pl.semaphore_signal(barrier, inc=1, device_id={"row": r, "col": c}, device_id_type=MESH)

    each(1, ROWS, lambda d: greet(row_at(d), col))
    each(1, ROWS, lambda d: greet(row_at(d), sib))
    each(1, COLS, lambda d: greet(row, col_at(d)))
    cross_z = lax.rem(cz + 1 + 2 * (1 - zl), 4)
    cross_row, cross_col = at_xyz(cx, cy, cross_z)
    greet(cross_row, cross_col)
    ready("residual", "gains")
    x = res_chip[core].astype(F32)
    square_all[0] = to_row(jnp.sum(x * x, axis=1, keepdims=True))
    pl.semaphore_wait(barrier, 2 * (ROWS - 1) + (COLS - 1) + 1)

    def sq_copy(d):
        return remote(square_all.at[0], square_all.at[d], sq_s.at[d], sq_r.at[d], row, col_at(d))

    start(1, COLS, sq_copy)
    mg[core] = gain_m[...].reshape(1, FEAT)
    fg[core] = gain_f[...].reshape(1, FEAT)

    ready("lens")
    own_token = COLS * col + lax.broadcasted_iota(jnp.int32, (16, HEAD), 0)
    position = layout_of(lens, own_token)[1].astype(F32)
    lane = lax.broadcasted_iota(jnp.int32, (16, HEAD), 1)
    low_half = lane < HEAD // 2
    frequency = jnp.exp(jnp.where(low_half, lane, lane - HEAD // 2).astype(F32) * (-2.0 * math.log(ROPE_BASE) / HEAD))
    angle = position * frequency
    cosine = jnp.cos(angle)
    sine = jnp.where(low_half, -jnp.sin(angle), jnp.sin(angle))

    arrive(1, COLS, sq_copy)
    square = to_column(jnp.sum(square_all[...], axis=0), 32)
    x_all[row] = (x * inverse_rms(square) * gain_a[...].reshape(1, FEAT)).astype(BF16)

    def x_copy(d):
        return remote(x_all.at[row], x_all.at[row], x_s.at[d], x_r.at[d], row_at(d), col)

    start(1, ROWS, x_copy)
    swap("residual_pair", res_chip.at[core], res_chip.at[core])
    swap("gains_pair", mg.at[core], mg.at[core])
    swap("gains_pair", fg.at[core], fg.at[core])
    own("wo", w_out, wo.at[mine])
    swap("wo", w_out, wo.at[mine])
    ready("wqkv")
    arrive(1, ROWS, x_copy)

    part = jnp.dot(x_all[...].reshape(T, FEAT), wqkv[...], preferred_element_type=F32)
    part_own[...] = part.reshape(CHIPS, 2, 16, QKV)
    pair = remote(part_own.at[:, other], part_pair, pair_s, pair_r, row, sib)
    pair.start()
    pending.append(pair.wait_send)
    pair.wait_recv()
    part_send[...] = part_own[:, core] + part_pair[...]

    def part_copy(d):
        c = chip_at(d)
        return remote(part_send.at[c], part_recv.at[d], part_s.at[d], part_r.at[d], row, c * 2 + core)

    start(1, CHIPS, part_copy)
    own("wg", w_gate.at[core], wg.at[mine])
    own("wu", w_up.at[core], wu.at[mine])
    swap("wg", w_gate.at[other], wg.at[mine])
    swap("wu", w_up.at[other], wu.at[mine])
    part_recv[0] = part_send[chip]
    arrive(1, CHIPS, part_copy)

    total = jnp.sum(part_recv[...], axis=0)
    for h in range(Q_HEADS + 1):
        head = total[:, h * HEAD:(h + 1) * HEAD]
        turned = head * cosine + pltpu.roll(head, HEAD // 2, 1) * sine
        qkv_all[chip, core, :, h * HEAD:(h + 1) * HEAD] = turned.astype(BF16)
    qkv_all[chip, core, :, QW + HEAD:QKV] = total[:, QW + HEAD:QKV].astype(BF16)

    own_qkv = qkv_all.at[chip, core]
    own_kv = qkv_all.at[chip, core, :, QW:QKV]

    def qkv_copy(d):
        return remote(own_qkv, own_qkv, qkv_s.at[d], qkv_r.at[d], row, chip_at(d) * 2 + core)

    def kv_copy(d):
        return remote(own_kv, own_kv, qkv_s.at[CHIPS + d], qkv_r.at[CHIPS + d], row, chip_at(d) * 2 + other)

    start(1, CHIPS, qkv_copy)
    start(0, CHIPS, kv_copy)
    own("wd", w_down.at[core], wd.at[mine])
    swap("wd", w_down.at[other], wd.at[mine])

    row_i = lax.broadcasted_iota(jnp.int32, (T // 2, 1), 0)
    q_token = lax.div(row_i, 16) * 32 + core * 16 + lax.rem(row_i, 16)
    k_token = lax.broadcasted_iota(jnp.int32, (1, T), 1)
    q_segment = layout_of(lens, q_token)[0]
    k_segment = layout_of(lens, k_token)[0]
    allowed = (q_segment == k_segment) & (k_token <= q_token)

    arrive(1, CHIPS, qkv_copy)
    arrive(0, CHIPS, kv_copy)

    keys = qkv_all[:, :, :, QW:QW + HEAD].reshape(T, HEAD)
    values = qkv_all[:, :, :, QW + HEAD:QKV].reshape(T, HEAD)
    for h in range(Q_HEADS):
        query = qkv_all[:, core, :, h * HEAD:(h + 1) * HEAD].reshape(T // 2, HEAD)
        scores = dot_nt(query, keys)
        scores = jnp.where(allowed, scores * HEAD ** (-0.5), MASKED)
        weights = jnp.exp(scores - jnp.max(scores, axis=1, keepdims=True))
        weights = (weights / jnp.sum(weights, axis=1, keepdims=True)).astype(BF16)
        result = jnp.dot(weights, values, preferred_element_type=F32)
        attended[:, h * HEAD:(h + 1) * HEAD] = result.astype(BF16)

    ready("wo", "residual_pair")
    proj_send[...] = dot_nt(attended[...], wo[...]).reshape(ROWS, 16, CHIP)

    def proj_copy(d):
        r = row_at(d)
        return remote(proj_send.at[r], proj_recv.at[d], proj_s.at[d], proj_r.at[d], r, col)

    start(1, ROWS, proj_copy)
    proj_recv[0] = proj_send[row]
    arrive(1, ROWS, proj_copy)
    half_rows = pl.ds(pl.multiple_of(core * 16, 16), 16)
    residual = jnp.concatenate([res_chip[0, half_rows, :], res_chip[1, half_rows, :]], axis=1).astype(F32)
    stream_all[row, core] = (residual + jnp.sum(proj_recv[...], axis=0)).astype(BF16)

    own_stream = stream_all.at[row, core]

    def stream_copy(d):
        return remote(own_stream, own_stream, stream_s.at[d], stream_r.at[d], row_at(d), col)

    def stream_cross(d):
        return remote(own_stream, own_stream, stream_s.at[ROWS + d], stream_r.at[ROWS + d], row_at(d), sib)

    start(1, ROWS, stream_copy)
    start(0, ROWS, stream_cross)
    own("wh", w_head, wh.at[core])
    swap("wh", w_head, wh.at[core])
    wh_at = len(pending) - 1
    ready("wg", "wu", "gains_pair")
    arrive(1, ROWS, stream_copy)
    arrive(0, ROWS, stream_cross)

    stream = stream_all[...].reshape(T, CHIP).astype(F32)
    square_hi, square_lo = split_sum(jnp.sum(stream * stream, axis=1, keepdims=True), HALF - CHUNKS[0][1])
    stream = stream * jnp.concatenate([mg[0], mg[1]], axis=1)
    mlp_hi = stream.astype(BF16)
    mlp_lo = (stream - mlp_hi.astype(F32)).astype(BF16)

    def y_peer(d):
        return (lax.rem(cy + d, 4) * 2 + zl) * 2 + core

    z_peer = (cy * 2 + 1 - zl) * 2 + core

    def to_y(src, dst, i):
        def copy(d):
            return remote(src(lax.rem(cy + d, 4)), dst(d), y_s.at[i, d], y_r.at[i, d], row, y_peer(d))

        return copy

    def to_z(src, dst, i):
        return lambda d: remote(src, dst, z_s.at[i], z_r.at[i], row, z_peer)

    def gate_up(i):
        low, width = CHUNKS[i]
        for half, weight in enumerate((wg, wu)):
            product = jnp.dot(mlp_hi, weight[:, low:low + width], preferred_element_type=F32)
            product += jnp.dot(mlp_lo, weight[:, low:low + width], preferred_element_type=F32)
            product = product.reshape(4, 2, 32, width)
            gu_own[i, :, :, :, half * HALF:half * HALF + width] = product
            gu_send[i, :, :, :, half * HALF:half * HALF + width] = product.astype(BF16)
            if width < HALF:
                rest = (square_hi, square_lo)[half].reshape(4, 2, 32, HALF - width)
                gu_own[i, :, :, :, half * HALF + width:(half + 1) * HALF] = rest.astype(F32)
                gu_send[i, :, :, :, half * HALF + width:(half + 1) * HALF] = rest

    gate_up(0)
    sum_z0 = to_z(gu_send.at[0, :, 1 - zl], gu_z0, 0)
    start(0, 1, sum_z0)
    gate_up(1)
    sum_y1 = to_y(lambda y: gu_send.at[1, y], lambda d: gu_y1.at[d], 0)
    start(1, 4, sum_y1)
    held = pending[-2:]
    del pending[-2:]
    wh_swap = pending.pop(wh_at)
    flush()
    pending.extend([wh_swap] + held)

    arrive(0, 1, sum_z0)
    middle = gu_own[0, :, zl] + gu_z0[...].astype(F32)
    mid_own[...] = middle
    mid_send[...] = middle.astype(BF16)
    width = CHUNKS[0][1]
    square = middle[:, :, width:width + 1] + middle[:, :, HALF + width:HALF + width + 1]
    for half, rest in enumerate(split_sum(square.reshape(HEAD, 1), HALF - width)):
        rest = rest.reshape(4, 32, HALF - width)
        mid_own[:, :, half * HALF + width:(half + 1) * HALF] = rest.astype(F32)
        mid_send[:, :, half * HALF + width:(half + 1) * HALF] = rest
    sum_y0 = to_y(lambda y: mid_send.at[y], lambda d: gu_y0.at[d], 1)
    start(1, 4, sum_y0)
    arrive(1, 4, sum_y1)
    gu_y1[0] = jnp.zeros((2, 32, FFP), BF16)
    mid2_own[...] = gu_own[1, cy] + jnp.sum(gu_y1[...].astype(F32), axis=0)
    sum_z1 = to_z(mid2_own.at[1 - zl], gu_z1, 1)
    start(0, 1, sum_z1)

    def activate(i, total, scale):
        low, width = CHUNKS[i]
        gate = total[:, 0:width] * scale
        hidden = gate / (1.0 + jnp.exp(-gate)) * (total[:, HALF:HALF + width] * scale)
        hidden_all[cy, zl, :, low:low + width] = hidden.astype(BF16)

    def lanes(i):
        return pl.ds(CHUNKS[i][0], HALF)

    hidden_all[cy, zl, :, FF:FFP] = jnp.zeros((32, FFP - FF), BF16)
    arrive(1, 4, sum_y0)
    gu_y0[0] = jnp.zeros((32, FFP), BF16)
    total = mid_own[cy] + jnp.sum(gu_y0[...].astype(F32), axis=0)
    scale = inverse_rms(total[:, width:width + 1] + total[:, HALF + width:HALF + width + 1])
    activate(0, total, scale)
    own0 = hidden_all.at[cy, zl, :, lanes(0)]
    hid_z0 = to_z(own0, own0, 2)
    start(0, 1, hid_z0)
    arrive(0, 1, sum_z1)
    activate(1, mid2_own[zl] + gu_z1[...], scale)
    own1 = hidden_all.at[cy, zl, :, lanes(1)]
    hid_y1 = to_y(lambda y: own1, lambda d: own1, 2)
    start(1, 4, hid_y1)
    arrive(0, 1, hid_z0)
    both0 = hidden_all.at[cy, :, :, lanes(0)]
    hid_y0 = to_y(lambda y: both0, lambda d: both0, 3)
    start(1, 4, hid_y0)
    arrive(1, 4, hid_y1)
    four1 = hidden_all.at[:, zl, :, lanes(1)]
    hid_z1 = to_z(four1, four1, 3)
    start(0, 1, hid_z1)
    ready("wd")

    product = jnp.zeros((T, CHIP), F32)
    for i, (low, width) in enumerate(CHUNKS):
        arrive(*((1, 4, hid_y0) if i == 0 else (0, 1, hid_z1)))
        hidden = hidden_all[:, :, :, low:low + width].reshape(T, width)
        product += dot_nt(hidden, wd[:, low:low + width])
    down_send[...] = product.reshape(ROWS, 32, CHIP)

    def down_copy(d):
        r = row_at(d)
        return remote(down_send.at[r], down_recv.at[d], down_s.at[d], down_r.at[d], r, col)

    start(1, ROWS, down_copy)
    down_recv[0] = down_send[row]
    arrive(1, ROWS, down_copy)
    final = stream_all[row].reshape(32, CHIP).astype(F32) + jnp.sum(down_recv[...], axis=0)
    square_hi, square_lo = split_sum(jnp.sum(final * final, axis=1, keepdims=True), 64)
    final = (final * jnp.concatenate([fg[0], fg[1]], axis=1)).astype(BF16)

    fin_a[cy, zl, cx, zh] = final[:, 0:256]
    fin_b[cy, zl, cx, zh] = final[:, 256:512]
    fin_c[cy, zl, cx, zh, :, 0:128] = final[:, 512:640]
    fin_c[cy, zl, cx, zh, :, 128:192] = square_hi
    fin_c[cy, zl, cx, zh, :, 192:256] = square_lo

    parts = (fin_a, fin_b, fin_c)
    orders = ("zyx", "xzy", "yxz")

    def axis_copies(p, stage):
        order = orders[p % 3]
        axis, done = order[stage], order[:stage]
        one = {"y": pl.ds(cy, 1), "x": pl.ds(cx, 1), "zl": pl.ds(zl, 1), "zh": pl.ds(zh, 1)}
        full = {"y": pl.ds(0, 4), "x": pl.ds(0, 4), "zl": pl.ds(0, 2), "zh": pl.ds(0, 2)}
        pick = {k: full[k] if k[0] in done else one[k] for k in one}
        ref = parts[p % 3].at[pick["y"], pick["zl"], pick["x"], pick["zh"], pl.ds(p // 3 * 16, 16)]
        copies = []
        for d in (2, 1, 3):
            x = lax.rem(cx + d, 4) if axis == "x" else cx
            y = lax.rem(cy + d, 4) if axis == "y" else cy
            z = lax.rem(cz + d, 4) if axis == "z" else cz
            r, c = at_xyz(x, y, z)
            i = (p * 3 + stage) * 3 + d - 1
            copies.append(remote(ref, ref, fin_s.at[i], fin_r.at[i], r, c))
        return copies

    gathers = [[axis_copies(p, stage) for p in range(6)] for stage in range(3)]
    for stage in range(3):
        for p in range(6):
            if stage:
                for copy in gathers[stage - 1][p]:
                    copy.wait_recv()
            for copy in gathers[stage][p]:
                copy.start()
                pending.append(copy.wait_send)
    last = pending[-18:]
    del pending[-18:]
    flush()
    pending.extend(last)
    ready("wh")
    ready("targets")
    diagonal = lax.broadcasted_iota(jnp.int32, (T, T), 0) == lax.broadcasted_iota(jnp.int32, (T, T), 1)
    target = jnp.sum(jnp.where(diagonal, target_row[...].astype(F32), 0.0), axis=1, keepdims=True).astype(jnp.int32)
    for p in range(6):
        for copy in gathers[2][p]:
            copy.wait_recv()

    square = jnp.zeros((T, 1), F32)
    for y in range(4):
        pieces = []
        for z in range(2):
            c = fin_c[y, z].reshape(T, 256)
            square = square + c[:, 128:129].astype(F32) + c[:, 192:193].astype(F32)
            pieces += [fin_a[y, z].reshape(T, 256), fin_b[y, z].reshape(T, 256), c[:, 0:128]]
        states = jnp.concatenate(pieces, axis=1)
        for j in range(2):
            product = jnp.dot(states, wh[j, y * 2 * CHIP:(y + 1) * 2 * CHIP], preferred_element_type=F32)
            logits[j] = product if y == 0 else logits[j] + product
    scale = inverse_rms(square)
    both = [logits[j] * scale for j in range(2)]
    top = jnp.maximum(*[jnp.max(l, axis=1, keepdims=True) for l in both])
    exponential = sum(jnp.sum(jnp.exp(l - top), axis=1, keepdims=True) for l in both)
    picked = jnp.zeros((T, 1), F32)
    for j in range(2):
        first = (row * COLS + chip * 2 + j) * VOCAB
        ids = first + lax.broadcasted_iota(jnp.int32, (T, VOCAB), 1)
        picked = picked + jnp.sum(jnp.where(ids == target, both[j], 0.0), axis=1, keepdims=True)
    lane = lax.broadcasted_iota(jnp.int32, (T, HEAD), 1)
    packed = jnp.where(lane == 0, top, jnp.where(lane == 1, exponential, picked))
    stat_recv[0, 0] = jnp.transpose(packed)[0:8, :]

    def merge(blocks):
        top = jnp.max(blocks[:, 0:1, :], axis=0)
        exponential = jnp.sum(blocks[:, 1:2, :] * jnp.exp(blocks[:, 0:1, :] - top[None]), axis=0)
        return top, exponential, jnp.sum(blocks[:, 2:3, :], axis=0)

    line = lax.broadcasted_iota(jnp.int32, (8, T), 0)

    def packed_merge(blocks):
        top, exponential, picked = merge(blocks)
        return jnp.where(line == 0, top, jnp.where(line == 1, exponential, picked))

    for stage in range(2):
        def st_copy(d):
            if stage == 0:
                r, c = at_xyz(cx, cy, lax.rem(cz + d, 4))
            else:
                r, c = at_xyz(cx, lax.rem(cy + d, 4), cz)
            return remote(stat_recv.at[stage, 0], stat_recv.at[stage, d], st_s.at[stage, d], st_r.at[stage, d], r, c)

        each(1, 4, lambda d: st_copy(d).start())
        arrive(1, 4, st_copy)
        each(1, 4, lambda d: st_copy(d).wait_send())
        merged = packed_merge(stat_recv[stage])
        if stage == 0:
            stat_recv[1, 0] = merged
        else:
            stat_send[...] = merged
            stat2_recv[core, cx] = merged
    own_stat = stat2_recv.at[core, cx]

    def st2_copy(d):
        return remote(stat_send, own_stat, st2_s.at[d], st2_r.at[d], lax.rem(cx + d, 4) * 2 + zh, col)

    def st2_cross(d):
        return remote(stat_send, own_stat, st2_s.at[4 + d], st2_r.at[4 + d], lax.rem(cx + d, 4) * 2 + zh, sib)

    start(1, 4, st2_copy)
    start(0, 4, st2_cross)
    arrive(1, 4, st2_copy)
    arrive(0, 4, st2_cross)
    logprob = []
    for m in range(2):
        top, exponential, picked = merge(stat2_recv[m])
        logprob.append(picked - (top + jnp.log(exponential)))
    difference = logprob[0] - logprob[1]
    hit = line == k_segment
    sums = jnp.sum(jnp.where(hit, difference, 0.0), axis=1, keepdims=True)
    length = jnp.sum(jnp.where(hit, 1.0, 0.0), axis=1, keepdims=True)
    square8 = lax.broadcasted_iota(jnp.int32, (8, 8), 0) == lax.broadcasted_iota(jnp.int32, (8, 8), 1)
    out[...] = jnp.sum(jnp.where(square8, sums / length, 0.0), axis=0, keepdims=True)

    flush()


def per_device(
    residual, attn_gain, w_query, w_key, w_value, w_out, mlp_gain, w_gate, w_up, w_down, final_gain, w_head,
    seq_lengths, targets,
):
    anywhere = pl.BlockSpec(memory_space=pl.ANY)
    vmem = pl.BlockSpec(memory_space=pltpu.VMEM)
    dma = pltpu.SemaphoreType.DMA
    result = pl.pallas_call(
        kernel,
        out_shape=jax.ShapeDtypeStruct((1, SEQS), F32),
        in_specs=[anywhere] * 12 + [anywhere, anywhere],
        out_specs=vmem,
        scratch_shapes=[
            pltpu.SMEM((SEQS,), jnp.int32),
            pltpu.VMEM((1, T), jnp.int32),
            pltpu.VMEM((2, 32, FEAT), BF16),
            pltpu.VMEM((COLS, 8, HEAD), F32),
            pltpu.VMEM((ROWS, 32, FEAT), BF16),
            pltpu.VMEM((FEAT, QKV), BF16),
            pltpu.VMEM((CHIP, QW), BF16),
            pltpu.VMEM((CHIP, FF), BF16),
            pltpu.VMEM((CHIP, FF), BF16),
            pltpu.VMEM((CHIP, FF), BF16),
            pltpu.VMEM((2, D, VOCAB), BF16),
            pltpu.VMEM((FEAT,), F32),
            pltpu.VMEM((FEAT,), F32),
            pltpu.VMEM((FEAT,), F32),
            pltpu.VMEM((2, 1, FEAT), F32),
            pltpu.VMEM((2, 1, FEAT), F32),
            pltpu.VMEM((CHIPS, 2, 16, QKV), F32),
            pltpu.VMEM((CHIPS, 16, QKV), F32),
            pltpu.VMEM((CHIPS, 16, QKV), F32),
            pltpu.VMEM((CHIPS, 16, QKV), F32),
            pltpu.VMEM((CHIPS, 2, 16, QKV), BF16),
            pltpu.VMEM((T // 2, QW), BF16),
            pltpu.VMEM((ROWS, 16, CHIP), F32),
            pltpu.VMEM((ROWS, 16, CHIP), F32),
            pltpu.VMEM((ROWS, 2, 16, CHIP), BF16),
            pltpu.VMEM((2, 4, 2, 32, FFP), F32),
            pltpu.VMEM((2, 4, 2, 32, FFP), BF16),
            pltpu.VMEM((4, 32, FFP), BF16),
            pltpu.VMEM((4, 32, FFP), BF16),
            pltpu.VMEM((32, FFP), F32),
            pltpu.VMEM((4, 2, 32, FFP), BF16),
            pltpu.VMEM((4, 32, FFP), F32),
            pltpu.VMEM((4, 32, FFP), BF16),
            pltpu.VMEM((2, 32, FFP), F32),
            pltpu.VMEM((4, 2, 32, FFP), BF16),
            pltpu.VMEM((ROWS, 32, CHIP), F32),
            pltpu.VMEM((ROWS, 32, CHIP), F32),
            pltpu.VMEM((4, 2, 4, 2, 32, 256), BF16),
            pltpu.VMEM((4, 2, 4, 2, 32, 256), BF16),
            pltpu.VMEM((4, 2, 4, 2, 32, 256), BF16),
            pltpu.VMEM((2, T, VOCAB), F32),
            pltpu.VMEM((8, T), F32),
            pltpu.VMEM((2, 4, 8, T), F32),
            pltpu.VMEM((2, 4, 8, T), F32),
            dma((14,)), dma((8,)), dma((8,)),
            dma((COLS,)), dma((COLS,)),
            dma((ROWS,)), dma((ROWS,)),
            dma, dma,
            dma((CHIPS,)), dma((CHIPS,)),
            dma((COLS,)), dma((COLS,)),
            dma((ROWS,)), dma((ROWS,)),
            dma((2 * ROWS,)), dma((2 * ROWS,)),
            dma((4, 4)), dma((4, 4)),
            dma((4,)), dma((4,)),
            dma((ROWS,)), dma((ROWS,)),
            dma((54,)), dma((54,)),
            dma((2, 4)), dma((2, 4)),
            dma((CHIPS,)), dma((CHIPS,)),
        ],
        compiler_params=pltpu.CompilerParams(
            collective_id=0, has_side_effects=True, vmem_limit_bytes=60 * 1024 * 1024
        ),
    )(
        residual, attn_gain, w_query, w_key, w_value, w_out.T, mlp_gain, w_gate, w_up,
        jnp.swapaxes(w_down, 1, 2), final_gain, w_head, seq_lengths, targets.reshape(1, T),
    )
    return result.reshape(SEQS)


def solution(mesh):
    placed = (
        P("row", "col"), P("col"), P("col", "row"), P("col", "row"), P("col", "row"), P("row", "col"), P("col"),
        P(None, "col", "row"), P(None, "col", "row"), P(None, "row", "col"), P("col"), P(None, ("row", "col")), P(), P(),
    )
    return jax.shard_map(per_device, mesh=mesh, in_specs=placed, out_specs=P(), check_vma=False)
```

```python
import math

import jax
import jax.numpy as jnp
from jax import lax
from jax.experimental import pallas as pl
from jax.experimental.pallas import tpu as pltpu
from jax.sharding import PartitionSpec as P

T = 256
D = 5120
HEAD = 128
Q_HEADS = 5
QW = Q_HEADS * HEAD
QKV = QW + 2 * HEAD
SEQS = 8
FEAT = 320
CHIP = 2 * FEAT
FF = 1728
FFP = 1792
HALF = FFP // 2
CHUNKS = ((HALF, FF - HALF), (0, HALF))
VOCAB = 640
ROWS = 8
COLS = 16
CHIPS = 8
EPSILON = 1e-06
ROPE_BASE = 1000000.0
MASKED = -1e30
MESH = pl.DeviceIdType.MESH
F32 = jnp.float32
BF16 = jnp.bfloat16


def remote(src, dst, send, recv, row, col):
    return pltpu.make_async_remote_copy(
        src_ref=src, dst_ref=dst, send_sem=send, recv_sem=recv,
        device_id={"row": row, "col": col}, device_id_type=MESH,
    )


def each(start, stop, body):
    def step(i, carry):
        body(i)
        return carry

    lax.fori_loop(start, stop, step, 0)


def dot_nt(a, b):
    return lax.dot_general(a, b, (((1,), (1,)), ((), ())), preferred_element_type=F32)


def diagonal_of(count):
    return lax.broadcasted_iota(jnp.int32, (count, HEAD), 0) == lax.broadcasted_iota(jnp.int32, (count, HEAD), 1)


def to_row(column):
    row = jnp.sum(jnp.where(diagonal_of(column.shape[0]), column, 0.0), axis=0, keepdims=True)
    return jnp.broadcast_to(row, (8, HEAD))


def to_column(rows, count):
    return jnp.sum(jnp.where(diagonal_of(count), rows[0:1], 0.0), axis=1, keepdims=True)


def split_sum(total, width):
    high = total.astype(BF16)
    low = (total - high.astype(F32)).astype(BF16)
    shape = (total.shape[0], width)
    return (
        jnp.broadcast_to(high.astype(F32), shape).astype(BF16),
        jnp.broadcast_to(low.astype(F32), shape).astype(BF16),
    )


def inverse_rms(total):
    return lax.rsqrt(total / D + EPSILON)


def layout_of(lens_ref, token):
    segment = jnp.zeros_like(token)
    start = jnp.zeros_like(token)
    end = jnp.int32(0)
    for s in range(SEQS):
        length = lens_ref[s]
        end = end + length
        before = end <= token
        segment = segment + jnp.where(before, 1, 0)
        start = start + jnp.where(before, length, 0)
    return segment, token - start


def kernel(
    res, attn_gain, w_query, w_key, w_value, w_out, mlp_gain, w_gate, w_up, w_down, final_gain, w_head, lengths, targets,
    out,
    lens, target_row, res_chip, square_all, x_all, wqkv, wo, wg, wu, wd, wh, gain_a, gain_m, gain_f, mg, fg,
    part_own, part_pair, part_send, part_recv, qkv_all, attended, proj_send, proj_recv, stream_all,
    gu_own, gu_send, gu_z0, gu_y0, gu_z1, gu_y1, mid_own, mid_send, mid2_own, hidden_all, down_send, down_recv,
    fin_a, fin_b, fin_c, logits, stat_send, stat_recv, stat2_recv,
    local_sem, swap_send, swap_recv, sq_s, sq_r, x_s, x_r, pair_s, pair_r, part_s, part_r, qkv_s, qkv_r, proj_s, proj_r,
    stream_s, stream_r, y_s, y_r, z_s, z_r, down_s, down_r, fin_s, fin_r, st_s, st_r, st2_s, st2_r,
):
    row, col = lax.axis_index("row"), lax.axis_index("col")
    core = lax.rem(col, 2)
    other = 1 - core
    chip = lax.div(col, 2)
    cx, zh = lax.div(row, 2), lax.rem(row, 2)
    cy, zl = lax.div(chip, 2), lax.rem(chip, 2)
    cz = zh * 2 + zl
    sib = chip * 2 + other

    def row_at(d):
        return lax.rem(row + d, ROWS)

    def chip_at(d):
        return lax.rem(chip + d, CHIPS)

    def col_at(d):
        return lax.rem(col + d, COLS)

    def at_xyz(x, y, z):
        return x * 2 + lax.div(z, 2), (y * 2 + lax.rem(z, 2)) * 2 + core

    mine = pl.ds(pl.multiple_of(core * FEAT, 64), FEAT)
    waits, pending, numbers = {}, [], {"own": 0, "pair": 0}

    def own(name, src, dst):
        copy = pltpu.make_async_copy(src, dst, local_sem.at[numbers["own"]])
        numbers["own"] += 1
        copy.start()
        waits.setdefault(name, []).append(copy.wait)

    def swap(name, src, dst):
        i = numbers["pair"]
        numbers["pair"] += 1
        copy = remote(src, dst, swap_send.at[i], swap_recv.at[i], row, sib)
        copy.start()
        waits.setdefault(name, []).append(copy.wait_recv)
        pending.append(copy.wait_send)

    def ready(*names):
        for name in names:
            for wait in waits.pop(name):
                wait()

    def start(first, stop, copy):
        each(first, stop, lambda d: copy(d).start())
        pending.append(lambda: each(first, stop, lambda d: copy(d).wait_send()))

    def arrive(first, stop, copy):
        each(first, stop, lambda d: copy(d).wait_recv())

    def flush():
        for finish in pending:
            finish()
        pending.clear()

    own("residual", res, res_chip.at[core])
    own("targets", targets, target_row)
    own("lens", lengths, lens)
    own("gains", attn_gain, gain_a)
    own("gains", mlp_gain, gain_m)
    own("gains", final_gain, gain_f)
    own("wqkv", w_query, wqkv.at[:, 0:QW])
    own("wqkv", w_key, wqkv.at[:, QW:QW + HEAD])
    own("wqkv", w_value, wqkv.at[:, QW + HEAD:QKV])

    barrier = pltpu.get_barrier_semaphore()

    def greet(r, c):
        pl.semaphore_signal(barrier, inc=1, device_id={"row": r, "col": c}, device_id_type=MESH)

    each(1, ROWS, lambda d: greet(row_at(d), col))
    each(1, ROWS, lambda d: greet(row_at(d), sib))
    each(1, COLS, lambda d: greet(row, col_at(d)))
    cross_z = lax.rem(cz + 1 + 2 * (1 - zl), 4)
    cross_row, cross_col = at_xyz(cx, cy, cross_z)
    greet(cross_row, cross_col)
    ready("residual", "gains")
    x = res_chip[core].astype(F32)
    square_all[0] = to_row(jnp.sum(x * x, axis=1, keepdims=True))
    pl.semaphore_wait(barrier, 2 * (ROWS - 1) + (COLS - 1) + 1)

    def sq_copy(d):
        return remote(square_all.at[0], square_all.at[d], sq_s.at[d], sq_r.at[d], row, col_at(d))

    start(1, COLS, sq_copy)
    mg[core] = gain_m[...].reshape(1, FEAT)
    fg[core] = gain_f[...].reshape(1, FEAT)

    ready("lens")
    own_token = COLS * col + lax.broadcasted_iota(jnp.int32, (16, HEAD), 0)
    position = layout_of(lens, own_token)[1].astype(F32)
    lane = lax.broadcasted_iota(jnp.int32, (16, HEAD), 1)
    low_half = lane < HEAD // 2
    frequency = jnp.exp(jnp.where(low_half, lane, lane - HEAD // 2).astype(F32) * (-2.0 * math.log(ROPE_BASE) / HEAD))
    angle = position * frequency
    cosine = jnp.cos(angle)
    sine = jnp.where(low_half, -jnp.sin(angle), jnp.sin(angle))

    arrive(1, COLS, sq_copy)
    square = to_column(jnp.sum(square_all[...], axis=0), 32)
    x_all[row] = (x * inverse_rms(square) * gain_a[...].reshape(1, FEAT)).astype(BF16)

    def x_copy(d):
        return remote(x_all.at[row], x_all.at[row], x_s.at[d], x_r.at[d], row_at(d), col)

    start(1, ROWS, x_copy)
    swap("residual_pair", res_chip.at[core], res_chip.at[core])
    swap("gains_pair", mg.at[core], mg.at[core])
    swap("gains_pair", fg.at[core], fg.at[core])
    own("wo", w_out, wo.at[mine])
    swap("wo", w_out, wo.at[mine])
    ready("wqkv")
    arrive(1, ROWS, x_copy)

    part = jnp.dot(x_all[...].reshape(T, FEAT), wqkv[...], preferred_element_type=F32)
    part_own[...] = part.reshape(CHIPS, 2, 16, QKV)
    pair = remote(part_own.at[:, other], part_pair, pair_s, pair_r, row, sib)
    pair.start()
    pending.append(pair.wait_send)
    pair.wait_recv()
    part_send[...] = part_own[:, core] + part_pair[...]

    def part_copy(d):
        c = chip_at(d)
        return remote(part_send.at[c], part_recv.at[d], part_s.at[d], part_r.at[d], row, c * 2 + core)

    start(1, CHIPS, part_copy)
    own("wg", w_gate.at[core], wg.at[mine])
    own("wu", w_up.at[core], wu.at[mine])
    swap("wg", w_gate.at[other], wg.at[mine])
    swap("wu", w_up.at[other], wu.at[mine])
    part_recv[0] = part_send[chip]
    arrive(1, CHIPS, part_copy)

    total = jnp.sum(part_recv[...], axis=0)
    for h in range(Q_HEADS + 1):
        head = total[:, h * HEAD:(h + 1) * HEAD]
        turned = head * cosine + pltpu.roll(head, HEAD // 2, 1) * sine
        qkv_all[chip, core, :, h * HEAD:(h + 1) * HEAD] = turned.astype(BF16)
    qkv_all[chip, core, :, QW + HEAD:QKV] = total[:, QW + HEAD:QKV].astype(BF16)

    own_qkv = qkv_all.at[chip, core]
    own_kv = qkv_all.at[chip, core, :, QW:QKV]

    def qkv_copy(d):
        return remote(own_qkv, own_qkv, qkv_s.at[d], qkv_r.at[d], row, chip_at(d) * 2 + core)

    def kv_copy(d):
        return remote(own_kv, own_kv, qkv_s.at[CHIPS + d], qkv_r.at[CHIPS + d], row, chip_at(d) * 2 + other)

    start(1, CHIPS, qkv_copy)
    start(0, CHIPS, kv_copy)
    own("wd", w_down.at[core], wd.at[mine])
    swap("wd", w_down.at[other], wd.at[mine])

    row_i = lax.broadcasted_iota(jnp.int32, (T // 2, 1), 0)
    q_token = lax.div(row_i, 16) * 32 + core * 16 + lax.rem(row_i, 16)
    k_token = lax.broadcasted_iota(jnp.int32, (1, T), 1)
    q_segment = layout_of(lens, q_token)[0]
    k_segment = layout_of(lens, k_token)[0]
    allowed = (q_segment == k_segment) & (k_token <= q_token)

    arrive(1, CHIPS, qkv_copy)
    arrive(0, CHIPS, kv_copy)

    keys = qkv_all[:, :, :, QW:QW + HEAD].reshape(T, HEAD)
    values = qkv_all[:, :, :, QW + HEAD:QKV].reshape(T, HEAD)
    for h in range(Q_HEADS):
        query = qkv_all[:, core, :, h * HEAD:(h + 1) * HEAD].reshape(T // 2, HEAD)
        scores = dot_nt(query, keys)
        scores = jnp.where(allowed, scores * HEAD ** (-0.5), MASKED)
        weights = jnp.exp(scores - jnp.max(scores, axis=1, keepdims=True))
        weights = (weights / jnp.sum(weights, axis=1, keepdims=True)).astype(BF16)
        result = jnp.dot(weights, values, preferred_element_type=F32)
        attended[:, h * HEAD:(h + 1) * HEAD] = result.astype(BF16)

    ready("wo", "residual_pair")
    proj_send[...] = dot_nt(attended[...], wo[...]).reshape(ROWS, 16, CHIP)

    def proj_copy(d):
        r = row_at(d)
        return remote(proj_send.at[r], proj_recv.at[d], proj_s.at[d], proj_r.at[d], r, col)

    start(1, ROWS, proj_copy)
    proj_recv[0] = proj_send[row]
    arrive(1, ROWS, proj_copy)
    half_rows = pl.ds(pl.multiple_of(core * 16, 16), 16)
    residual = jnp.concatenate([res_chip[0, half_rows, :], res_chip[1, half_rows, :]], axis=1).astype(F32)
    stream_all[row, core] = (residual + jnp.sum(proj_recv[...], axis=0)).astype(BF16)

    own_stream = stream_all.at[row, core]

    def stream_copy(d):
        return remote(own_stream, own_stream, stream_s.at[d], stream_r.at[d], row_at(d), col)

    def stream_cross(d):
        return remote(own_stream, own_stream, stream_s.at[ROWS + d], stream_r.at[ROWS + d], row_at(d), sib)

    start(1, ROWS, stream_copy)
    start(0, ROWS, stream_cross)
    own("wh", w_head, wh.at[core])
    swap("wh", w_head, wh.at[core])
    wh_at = len(pending) - 1
    ready("wg", "wu", "gains_pair")
    arrive(1, ROWS, stream_copy)
    arrive(0, ROWS, stream_cross)

    stream = stream_all[...].reshape(T, CHIP).astype(F32)
    square_hi, square_lo = split_sum(jnp.sum(stream * stream, axis=1, keepdims=True), HALF - CHUNKS[0][1])
    stream = stream * jnp.concatenate([mg[0], mg[1]], axis=1)
    mlp_hi = stream.astype(BF16)
    mlp_lo = (stream - mlp_hi.astype(F32)).astype(BF16)

    def y_peer(d):
        return (lax.rem(cy + d, 4) * 2 + zl) * 2 + core

    z_peer = (cy * 2 + 1 - zl) * 2 + core

    def to_y(src, dst, i):
        def copy(d):
            return remote(src(lax.rem(cy + d, 4)), dst(d), y_s.at[i, d], y_r.at[i, d], row, y_peer(d))

        return copy

    def to_z(src, dst, i):
        return lambda d: remote(src, dst, z_s.at[i], z_r.at[i], row, z_peer)

    def gate_up(i, leave):
        low, width = CHUNKS[i]
        for half, weight in enumerate((wg, wu)):
            product = jnp.dot(mlp_hi, weight[:, low:low + width], preferred_element_type=F32)
            product += jnp.dot(mlp_lo, weight[:, low:low + width], preferred_element_type=F32)
            product = product.reshape(4, 2, 32, width)
            gu_own[i, :, :, :, half * HALF:half * HALF + width] = product
            gu_send[i, :, :, :, half * HALF:half * HALF + width] = product.astype(BF16)
            if width < HALF:
                rest = (square_hi, square_lo)[half].reshape(4, 2, 32, HALF - width)
                gu_own[i, :, :, :, half * HALF + width:(half + 1) * HALF] = rest.astype(F32)
                gu_send[i, :, :, :, half * HALF + width:(half + 1) * HALF] = rest
            leave(half)

    def half_lanes(half):
        return pl.ds(half * HALF, HALF)

    def sum_z0(half):
        part = half_lanes(half)
        return to_z(gu_send.at[0, :, 1 - zl, :, part], gu_z0.at[:, :, part], 4 * half)

    def sum_y1(half):
        part = half_lanes(half)
        return to_y(lambda y: gu_send.at[1, y, :, :, part], lambda d: gu_y1.at[d, :, :, part], 4 * half)

    gate_up(0, lambda half: start(0, 1, sum_z0(half)))
    gate_up(1, lambda half: start(1, 4, sum_y1(half)))
    held = pending[-4:]
    del pending[-4:]
    wh_swap = pending.pop(wh_at)
    flush()
    pending.extend([wh_swap] + held)

    for half in range(2):
        arrive(0, 1, sum_z0(half))
    middle = gu_own[0, :, zl] + gu_z0[...].astype(F32)
    mid_own[...] = middle
    mid_send[...] = middle.astype(BF16)
    width = CHUNKS[0][1]
    square = middle[:, :, width:width + 1] + middle[:, :, HALF + width:HALF + width + 1]
    for half, rest in enumerate(split_sum(square.reshape(HEAD, 1), HALF - width)):
        rest = rest.reshape(4, 32, HALF - width)
        mid_own[:, :, half * HALF + width:(half + 1) * HALF] = rest.astype(F32)
        mid_send[:, :, half * HALF + width:(half + 1) * HALF] = rest
    sum_y0 = to_y(lambda y: mid_send.at[y], lambda d: gu_y0.at[d], 1)
    start(1, 4, sum_y0)
    for half in range(2):
        arrive(1, 4, sum_y1(half))
    gu_y1[0] = jnp.zeros((2, 32, FFP), BF16)
    mid2_own[...] = gu_own[1, cy] + jnp.sum(gu_y1[...].astype(F32), axis=0)
    sum_z1 = to_z(mid2_own.at[1 - zl], gu_z1, 1)
    start(0, 1, sum_z1)

    def activate(i, total, scale):
        low, width = CHUNKS[i]
        gate = total[:, 0:width] * scale
        hidden = gate / (1.0 + jnp.exp(-gate)) * (total[:, HALF:HALF + width] * scale)
        hidden_all[cy, zl, :, low:low + width] = hidden.astype(BF16)

    def lanes(i):
        return pl.ds(CHUNKS[i][0], HALF)

    hidden_all[cy, zl, :, FF:FFP] = jnp.zeros((32, FFP - FF), BF16)
    arrive(1, 4, sum_y0)
    gu_y0[0] = jnp.zeros((32, FFP), BF16)
    total = mid_own[cy] + jnp.sum(gu_y0[...].astype(F32), axis=0)
    scale = inverse_rms(total[:, width:width + 1] + total[:, HALF + width:HALF + width + 1])
    activate(0, total, scale)
    own0 = hidden_all.at[cy, zl, :, lanes(0)]
    hid_z0 = to_z(own0, own0, 2)
    start(0, 1, hid_z0)
    arrive(0, 1, sum_z1)
    activate(1, mid2_own[zl] + gu_z1[...], scale)
    own1 = hidden_all.at[cy, zl, :, lanes(1)]
    hid_y1 = to_y(lambda y: own1, lambda d: own1, 2)
    start(1, 4, hid_y1)
    arrive(0, 1, hid_z0)
    both0 = hidden_all.at[cy, :, :, lanes(0)]
    hid_y0 = to_y(lambda y: both0, lambda d: both0, 3)
    start(1, 4, hid_y0)
    arrive(1, 4, hid_y1)
    four1 = hidden_all.at[:, zl, :, lanes(1)]
    hid_z1 = to_z(four1, four1, 3)
    start(0, 1, hid_z1)
    ready("wd")

    product = jnp.zeros((T, CHIP), F32)
    for i, (low, width) in enumerate(CHUNKS):
        arrive(*((1, 4, hid_y0) if i == 0 else (0, 1, hid_z1)))
        hidden = hidden_all[:, :, :, low:low + width].reshape(T, width)
        product += dot_nt(hidden, wd[:, low:low + width])
    down_send[...] = product.reshape(ROWS, 32, CHIP)

    def down_copy(d):
        r = row_at(d)
        return remote(down_send.at[r], down_recv.at[d], down_s.at[d], down_r.at[d], r, col)

    start(1, ROWS, down_copy)
    down_recv[0] = down_send[row]
    arrive(1, ROWS, down_copy)
    final = stream_all[row].reshape(32, CHIP).astype(F32) + jnp.sum(down_recv[...], axis=0)
    square_hi, square_lo = split_sum(jnp.sum(final * final, axis=1, keepdims=True), 64)
    final = (final * jnp.concatenate([fg[0], fg[1]], axis=1)).astype(BF16)

    fin_a[cy, zl, cx, zh] = final[:, 0:256]
    fin_b[cy, zl, cx, zh] = final[:, 256:512]
    fin_c[cy, zl, cx, zh, :, 0:128] = final[:, 512:640]
    fin_c[cy, zl, cx, zh, :, 128:192] = square_hi
    fin_c[cy, zl, cx, zh, :, 192:256] = square_lo

    parts = (fin_a, fin_b, fin_c)
    orders = ("zyx", "xzy", "yxz")

    def axis_copies(p, stage):
        order = orders[p % 3]
        axis, done = order[stage], order[:stage]
        one = {"y": pl.ds(cy, 1), "x": pl.ds(cx, 1), "zl": pl.ds(zl, 1), "zh": pl.ds(zh, 1)}
        full = {"y": pl.ds(0, 4), "x": pl.ds(0, 4), "zl": pl.ds(0, 2), "zh": pl.ds(0, 2)}
        pick = {k: full[k] if k[0] in done else one[k] for k in one}
        ref = parts[p % 3].at[pick["y"], pick["zl"], pick["x"], pick["zh"], pl.ds(p // 3 * 16, 16)]
        copies = []
        for d in (2, 1, 3):
            x = lax.rem(cx + d, 4) if axis == "x" else cx
            y = lax.rem(cy + d, 4) if axis == "y" else cy
            z = lax.rem(cz + d, 4) if axis == "z" else cz
            r, c = at_xyz(x, y, z)
            i = (p * 3 + stage) * 3 + d - 1
            copies.append(remote(ref, ref, fin_s.at[i], fin_r.at[i], r, c))
        return copies

    gathers = [[axis_copies(p, stage) for p in range(6)] for stage in range(3)]
    for stage in range(3):
        for p in range(6):
            if stage:
                for copy in gathers[stage - 1][p]:
                    copy.wait_recv()
            for copy in gathers[stage][p]:
                copy.start()
                pending.append(copy.wait_send)
    last = pending[-18:]
    del pending[-18:]
    flush()
    pending.extend(last)
    ready("wh")
    ready("targets")
    diagonal = lax.broadcasted_iota(jnp.int32, (T, T), 0) == lax.broadcasted_iota(jnp.int32, (T, T), 1)
    target = jnp.sum(jnp.where(diagonal, target_row[...].astype(F32), 0.0), axis=1, keepdims=True).astype(jnp.int32)
    for p in range(6):
        for copy in gathers[2][p]:
            copy.wait_recv()

    square = jnp.zeros((T, 1), F32)
    for y in range(4):
        pieces = []
        for z in range(2):
            c = fin_c[y, z].reshape(T, 256)
            square = square + c[:, 128:129].astype(F32) + c[:, 192:193].astype(F32)
            pieces += [fin_a[y, z].reshape(T, 256), fin_b[y, z].reshape(T, 256), c[:, 0:128]]
        states = jnp.concatenate(pieces, axis=1)
        for j in range(2):
            product = jnp.dot(states, wh[j, y * 2 * CHIP:(y + 1) * 2 * CHIP], preferred_element_type=F32)
            logits[j] = product if y == 0 else logits[j] + product
    scale = inverse_rms(square)
    both = [logits[j] * scale for j in range(2)]
    top = jnp.maximum(*[jnp.max(l, axis=1, keepdims=True) for l in both])
    exponential = sum(jnp.sum(jnp.exp(l - top), axis=1, keepdims=True) for l in both)
    picked = jnp.zeros((T, 1), F32)
    for j in range(2):
        first = (row * COLS + chip * 2 + j) * VOCAB
        ids = first + lax.broadcasted_iota(jnp.int32, (T, VOCAB), 1)
        picked = picked + jnp.sum(jnp.where(ids == target, both[j], 0.0), axis=1, keepdims=True)
    lane = lax.broadcasted_iota(jnp.int32, (T, HEAD), 1)
    packed = jnp.where(lane == 0, top, jnp.where(lane == 1, exponential, picked))
    stat_recv[0] = jnp.transpose(packed)[0:8, :]

    def merge(blocks):
        top = jnp.max(blocks[:, 0:1, :], axis=0)
        exponential = jnp.sum(blocks[:, 1:2, :] * jnp.exp(blocks[:, 0:1, :] - top[None]), axis=0)
        return top, exponential, jnp.sum(blocks[:, 2:3, :], axis=0)

    line = lax.broadcasted_iota(jnp.int32, (8, T), 0)

    def packed_merge(blocks):
        top, exponential, picked = merge(blocks)
        return jnp.where(line == 0, top, jnp.where(line == 1, exponential, picked))

    def st_copy(d):
        return remote(stat_recv.at[0], stat_recv.at[d], st_s.at[d], st_r.at[d], row, chip_at(d) * 2 + core)

    start(1, CHIPS, st_copy)
    arrive(1, CHIPS, st_copy)
    stat_send[...] = packed_merge(stat_recv[...])
    own_stat = stat2_recv.at[core, row]

    def st2_copy(d):
        return remote(stat_send, own_stat, st2_s.at[d], st2_r.at[d], row_at(d), col)

    def st2_cross(d):
        return remote(stat_send, own_stat, st2_s.at[ROWS + d], st2_r.at[ROWS + d], row_at(d), sib)

    start(1, ROWS, st2_copy)
    start(0, ROWS, st2_cross)
    stat2_recv[core, row] = stat_send[...]
    arrive(1, ROWS, st2_copy)
    arrive(0, ROWS, st2_cross)
    logprob = []
    for m in range(2):
        top, exponential, picked = merge(stat2_recv[m])
        logprob.append(picked - (top + jnp.log(exponential)))
    difference = logprob[0] - logprob[1]
    hit = line == k_segment
    sums = jnp.sum(jnp.where(hit, difference, 0.0), axis=1, keepdims=True)
    length = jnp.sum(jnp.where(hit, 1.0, 0.0), axis=1, keepdims=True)
    square8 = lax.broadcasted_iota(jnp.int32, (8, 8), 0) == lax.broadcasted_iota(jnp.int32, (8, 8), 1)
    out[...] = jnp.sum(jnp.where(square8, sums / length, 0.0), axis=0, keepdims=True)

    flush()


def per_device(
    residual, attn_gain, w_query, w_key, w_value, w_out, mlp_gain, w_gate, w_up, w_down, final_gain, w_head,
    seq_lengths, targets,
):
    anywhere = pl.BlockSpec(memory_space=pl.ANY)
    vmem = pl.BlockSpec(memory_space=pltpu.VMEM)
    dma = pltpu.SemaphoreType.DMA
    result = pl.pallas_call(
        kernel,
        out_shape=jax.ShapeDtypeStruct((1, SEQS), F32),
        in_specs=[anywhere] * 12 + [anywhere, anywhere],
        out_specs=vmem,
        scratch_shapes=[
            pltpu.SMEM((SEQS,), jnp.int32),
            pltpu.VMEM((1, T), jnp.int32),
            pltpu.VMEM((2, 32, FEAT), BF16),
            pltpu.VMEM((COLS, 8, HEAD), F32),
            pltpu.VMEM((ROWS, 32, FEAT), BF16),
            pltpu.VMEM((FEAT, QKV), BF16),
            pltpu.VMEM((CHIP, QW), BF16),
            pltpu.VMEM((CHIP, FF), BF16),
            pltpu.VMEM((CHIP, FF), BF16),
            pltpu.VMEM((CHIP, FF), BF16),
            pltpu.VMEM((2, D, VOCAB), BF16),
            pltpu.VMEM((FEAT,), F32),
            pltpu.VMEM((FEAT,), F32),
            pltpu.VMEM((FEAT,), F32),
            pltpu.VMEM((2, 1, FEAT), F32),
            pltpu.VMEM((2, 1, FEAT), F32),
            pltpu.VMEM((CHIPS, 2, 16, QKV), F32),
            pltpu.VMEM((CHIPS, 16, QKV), F32),
            pltpu.VMEM((CHIPS, 16, QKV), F32),
            pltpu.VMEM((CHIPS, 16, QKV), F32),
            pltpu.VMEM((CHIPS, 2, 16, QKV), BF16),
            pltpu.VMEM((T // 2, QW), BF16),
            pltpu.VMEM((ROWS, 16, CHIP), F32),
            pltpu.VMEM((ROWS, 16, CHIP), F32),
            pltpu.VMEM((ROWS, 2, 16, CHIP), BF16),
            pltpu.VMEM((2, 4, 2, 32, FFP), F32),
            pltpu.VMEM((2, 4, 2, 32, FFP), BF16),
            pltpu.VMEM((4, 32, FFP), BF16),
            pltpu.VMEM((4, 32, FFP), BF16),
            pltpu.VMEM((32, FFP), F32),
            pltpu.VMEM((4, 2, 32, FFP), BF16),
            pltpu.VMEM((4, 32, FFP), F32),
            pltpu.VMEM((4, 32, FFP), BF16),
            pltpu.VMEM((2, 32, FFP), F32),
            pltpu.VMEM((4, 2, 32, FFP), BF16),
            pltpu.VMEM((ROWS, 32, CHIP), F32),
            pltpu.VMEM((ROWS, 32, CHIP), F32),
            pltpu.VMEM((4, 2, 4, 2, 32, 256), BF16),
            pltpu.VMEM((4, 2, 4, 2, 32, 256), BF16),
            pltpu.VMEM((4, 2, 4, 2, 32, 256), BF16),
            pltpu.VMEM((2, T, VOCAB), F32),
            pltpu.VMEM((8, T), F32),
            pltpu.VMEM((CHIPS, 8, T), F32),
            pltpu.VMEM((2, ROWS, 8, T), F32),
            dma((14,)), dma((8,)), dma((8,)),
            dma((COLS,)), dma((COLS,)),
            dma((ROWS,)), dma((ROWS,)),
            dma, dma,
            dma((CHIPS,)), dma((CHIPS,)),
            dma((COLS,)), dma((COLS,)),
            dma((ROWS,)), dma((ROWS,)),
            dma((2 * ROWS,)), dma((2 * ROWS,)),
            dma((5, 4)), dma((5, 4)),
            dma((5,)), dma((5,)),
            dma((ROWS,)), dma((ROWS,)),
            dma((54,)), dma((54,)),
            dma((CHIPS,)), dma((CHIPS,)),
            dma((2 * ROWS,)), dma((2 * ROWS,)),
        ],
        compiler_params=pltpu.CompilerParams(
            collective_id=0, has_side_effects=True, vmem_limit_bytes=60 * 1024 * 1024
        ),
    )(
        residual, attn_gain, w_query, w_key, w_value, w_out.T, mlp_gain, w_gate, w_up,
        jnp.swapaxes(w_down, 1, 2), final_gain, w_head, seq_lengths, targets.reshape(1, T),
    )
    return result.reshape(SEQS)


def solution(mesh):
    placed = (
        P("row", "col"), P("col"), P("col", "row"), P("col", "row"), P("col", "row"), P("row", "col"), P("col"),
        P(None, "col", "row"), P(None, "col", "row"), P(None, "row", "col"), P("col"), P(None, ("row", "col")), P(), P(),
    )
    return jax.shard_map(per_device, mesh=mesh, in_specs=placed, out_specs=P(), check_vma=False)
```

```python
import math

import jax
import jax.numpy as jnp
from jax import lax
from jax.experimental import pallas as pl
from jax.experimental.pallas import tpu as pltpu
from jax.sharding import PartitionSpec as P

T = 256
D = 5120
HEAD = 128
Q_HEADS = 5
QW = Q_HEADS * HEAD
QKV = QW + 2 * HEAD
SEQS = 8
FEAT = 320
CHIP = 2 * FEAT
FF = 1728
FFP = 1792
HALF = FFP // 2
CHUNKS = ((HALF, FF - HALF), (0, HALF))
VOCAB = 640
ROWS = 8
COLS = 16
CHIPS = 8
EPSILON = 1e-06
ROPE_BASE = 1000000.0
MASKED = -1e30
MESH = pl.DeviceIdType.MESH
F32 = jnp.float32
BF16 = jnp.bfloat16


def remote(src, dst, send, recv, row, col):
    return pltpu.make_async_remote_copy(
        src_ref=src, dst_ref=dst, send_sem=send, recv_sem=recv,
        device_id={"row": row, "col": col}, device_id_type=MESH,
    )


def each(start, stop, body):
    def step(i, carry):
        body(i)
        return carry

    lax.fori_loop(start, stop, step, 0)


def dot_nt(a, b):
    return lax.dot_general(a, b, (((1,), (1,)), ((), ())), preferred_element_type=F32)


def diagonal_of(count):
    return lax.broadcasted_iota(jnp.int32, (count, HEAD), 0) == lax.broadcasted_iota(jnp.int32, (count, HEAD), 1)


def to_row(column):
    row = jnp.sum(jnp.where(diagonal_of(column.shape[0]), column, 0.0), axis=0, keepdims=True)
    return jnp.broadcast_to(row, (8, HEAD))


def to_column(rows, count):
    return jnp.sum(jnp.where(diagonal_of(count), rows[0:1], 0.0), axis=1, keepdims=True)


def split_sum(total, width):
    high = total.astype(BF16)
    low = (total - high.astype(F32)).astype(BF16)
    shape = (total.shape[0], width)
    return (
        jnp.broadcast_to(high.astype(F32), shape).astype(BF16),
        jnp.broadcast_to(low.astype(F32), shape).astype(BF16),
    )


def inverse_rms(total):
    return lax.rsqrt(total / D + EPSILON)


def layout_of(lens_ref, token):
    segment = jnp.zeros_like(token)
    start = jnp.zeros_like(token)
    end = jnp.int32(0)
    for s in range(SEQS):
        length = lens_ref[s]
        end = end + length
        before = end <= token
        segment = segment + jnp.where(before, 1, 0)
        start = start + jnp.where(before, length, 0)
    return segment, token - start


def kernel(
    res, attn_gain, w_query, w_key, w_value, w_out, mlp_gain, w_gate, w_up, w_down, final_gain, w_head, lengths, targets,
    out,
    lens, target_row, res_chip, square_all, x_all, wqkv, wo, wg, wu, wd, wh, gain_a, gain_m, gain_f, mg, fg,
    part_own, part_pair, part_send, part_recv, qkv_all, attended, proj_send, proj_recv, stream_all,
    gu_own, gu_send, gu_z0, gu_y0, gu_z1, gu_y1, mid_own, mid_send, mid2_own, hidden_all, down_send, down_recv,
    fin_a, fin_b, fin_c, logits, stat_send, stat_recv, stat2_recv,
    local_sem, swap_send, swap_recv, sq_s, sq_r, x_s, x_r, pair_s, pair_r, part_s, part_r, qkv_s, qkv_r, proj_s, proj_r,
    stream_s, stream_r, y_s, y_r, z_s, z_r, hid_s, hid_r, down_s, down_r, fin_s, fin_r, st_s, st_r, st2_s, st2_r,
):
    row, col = lax.axis_index("row"), lax.axis_index("col")
    core = lax.rem(col, 2)
    other = 1 - core
    chip = lax.div(col, 2)
    cx, zh = lax.div(row, 2), lax.rem(row, 2)
    cy, zl = lax.div(chip, 2), lax.rem(chip, 2)
    cz = zh * 2 + zl
    sib = chip * 2 + other

    def row_at(d):
        return lax.rem(row + d, ROWS)

    def chip_at(d):
        return lax.rem(chip + d, CHIPS)

    def col_at(d):
        return lax.rem(col + d, COLS)

    def at_xyz(x, y, z):
        return x * 2 + lax.div(z, 2), (y * 2 + lax.rem(z, 2)) * 2 + core

    mine = pl.ds(pl.multiple_of(core * FEAT, 64), FEAT)
    waits, pending, numbers = {}, [], {"own": 0, "pair": 0}

    def own(name, src, dst):
        copy = pltpu.make_async_copy(src, dst, local_sem.at[numbers["own"]])
        numbers["own"] += 1
        copy.start()
        waits.setdefault(name, []).append(copy.wait)

    def swap(name, src, dst):
        i = numbers["pair"]
        numbers["pair"] += 1
        copy = remote(src, dst, swap_send.at[i], swap_recv.at[i], row, sib)
        copy.start()
        waits.setdefault(name, []).append(copy.wait_recv)
        pending.append(copy.wait_send)

    def ready(*names):
        for name in names:
            for wait in waits.pop(name):
                wait()

    def start(first, stop, copy):
        each(first, stop, lambda d: copy(d).start())
        pending.append(lambda: each(first, stop, lambda d: copy(d).wait_send()))

    def arrive(first, stop, copy):
        each(first, stop, lambda d: copy(d).wait_recv())

    def flush():
        for finish in pending:
            finish()
        pending.clear()

    own("residual", res, res_chip.at[core])
    own("targets", targets, target_row)
    own("lens", lengths, lens)
    own("gains", attn_gain, gain_a)
    own("gains", mlp_gain, gain_m)
    own("gains", final_gain, gain_f)
    own("wqkv", w_query, wqkv.at[:, 0:QW])
    own("wqkv", w_key, wqkv.at[:, QW:QW + HEAD])
    own("wqkv", w_value, wqkv.at[:, QW + HEAD:QKV])

    barrier = pltpu.get_barrier_semaphore()

    def greet(r, c):
        pl.semaphore_signal(barrier, inc=1, device_id={"row": r, "col": c}, device_id_type=MESH)

    each(1, ROWS, lambda d: greet(row_at(d), col))
    each(1, ROWS, lambda d: greet(row_at(d), sib))
    each(1, COLS, lambda d: greet(row, col_at(d)))
    cross_z = lax.rem(cz + 1 + 2 * (1 - zl), 4)
    cross_row, cross_col = at_xyz(cx, cy, cross_z)
    greet(cross_row, cross_col)
    ready("residual", "gains")
    x = res_chip[core].astype(F32)
    square_all[0] = to_row(jnp.sum(x * x, axis=1, keepdims=True))
    pl.semaphore_wait(barrier, 2 * (ROWS - 1) + (COLS - 1) + 1)

    def sq_copy(d):
        return remote(square_all.at[0], square_all.at[d], sq_s.at[d], sq_r.at[d], row, col_at(d))

    start(1, COLS, sq_copy)
    mg[core] = gain_m[...].reshape(1, FEAT)
    fg[core] = gain_f[...].reshape(1, FEAT)

    ready("lens")
    own_token = COLS * col + lax.broadcasted_iota(jnp.int32, (16, HEAD), 0)
    position = layout_of(lens, own_token)[1].astype(F32)
    lane = lax.broadcasted_iota(jnp.int32, (16, HEAD), 1)
    low_half = lane < HEAD // 2
    frequency = jnp.exp(jnp.where(low_half, lane, lane - HEAD // 2).astype(F32) * (-2.0 * math.log(ROPE_BASE) / HEAD))
    angle = position * frequency
    cosine = jnp.cos(angle)
    sine = jnp.where(low_half, -jnp.sin(angle), jnp.sin(angle))

    arrive(1, COLS, sq_copy)
    square = to_column(jnp.sum(square_all[...], axis=0), 32)
    x_all[row] = (x * inverse_rms(square) * gain_a[...].reshape(1, FEAT)).astype(BF16)

    def x_copy(d):
        return remote(x_all.at[row], x_all.at[row], x_s.at[d], x_r.at[d], row_at(d), col)

    start(1, ROWS, x_copy)
    swap("residual_pair", res_chip.at[core], res_chip.at[core])
    swap("gains_pair", mg.at[core], mg.at[core])
    swap("gains_pair", fg.at[core], fg.at[core])
    own("wo", w_out, wo.at[mine])
    swap("wo", w_out, wo.at[mine])
    ready("wqkv")
    arrive(1, ROWS, x_copy)

    part = jnp.dot(x_all[...].reshape(T, FEAT), wqkv[...], preferred_element_type=F32)
    part_own[...] = part.reshape(CHIPS, 2, 16, QKV)
    pair = remote(part_own.at[:, other], part_pair, pair_s, pair_r, row, sib)
    pair.start()
    pending.append(pair.wait_send)
    pair.wait_recv()
    part_send[...] = part_own[:, core] + part_pair[...]

    def part_copy(d):
        c = chip_at(d)
        return remote(part_send.at[c], part_recv.at[d], part_s.at[d], part_r.at[d], row, c * 2 + core)

    start(1, CHIPS, part_copy)
    own("wg", w_gate.at[core], wg.at[mine])
    own("wu", w_up.at[core], wu.at[mine])
    swap("wg", w_gate.at[other], wg.at[mine])
    swap("wu", w_up.at[other], wu.at[mine])
    part_recv[0] = part_send[chip]
    arrive(1, CHIPS, part_copy)

    total = jnp.sum(part_recv[...], axis=0)
    for h in range(Q_HEADS + 1):
        head = total[:, h * HEAD:(h + 1) * HEAD]
        turned = head * cosine + pltpu.roll(head, HEAD // 2, 1) * sine
        qkv_all[chip, core, :, h * HEAD:(h + 1) * HEAD] = turned.astype(BF16)
    qkv_all[chip, core, :, QW + HEAD:QKV] = total[:, QW + HEAD:QKV].astype(BF16)

    own_qkv = qkv_all.at[chip, core]
    own_kv = qkv_all.at[chip, core, :, QW:QKV]

    def qkv_copy(d):
        return remote(own_qkv, own_qkv, qkv_s.at[d], qkv_r.at[d], row, chip_at(d) * 2 + core)

    def kv_copy(d):
        return remote(own_kv, own_kv, qkv_s.at[CHIPS + d], qkv_r.at[CHIPS + d], row, chip_at(d) * 2 + other)

    start(1, CHIPS, qkv_copy)
    start(0, CHIPS, kv_copy)
    own("wd", w_down.at[core], wd.at[mine])
    swap("wd", w_down.at[other], wd.at[mine])

    row_i = lax.broadcasted_iota(jnp.int32, (T // 2, 1), 0)
    q_token = lax.div(row_i, 16) * 32 + core * 16 + lax.rem(row_i, 16)
    k_token = lax.broadcasted_iota(jnp.int32, (1, T), 1)
    q_segment = layout_of(lens, q_token)[0]
    k_segment = layout_of(lens, k_token)[0]
    allowed = (q_segment == k_segment) & (k_token <= q_token)

    arrive(1, CHIPS, qkv_copy)
    arrive(0, CHIPS, kv_copy)

    keys = qkv_all[:, :, :, QW:QW + HEAD].reshape(T, HEAD)
    values = qkv_all[:, :, :, QW + HEAD:QKV].reshape(T, HEAD)
    for h in range(Q_HEADS):
        query = qkv_all[:, core, :, h * HEAD:(h + 1) * HEAD].reshape(T // 2, HEAD)
        scores = dot_nt(query, keys)
        scores = jnp.where(allowed, scores * HEAD ** (-0.5), MASKED)
        weights = jnp.exp(scores - jnp.max(scores, axis=1, keepdims=True))
        weights = (weights / jnp.sum(weights, axis=1, keepdims=True)).astype(BF16)
        result = jnp.dot(weights, values, preferred_element_type=F32)
        attended[:, h * HEAD:(h + 1) * HEAD] = result.astype(BF16)

    ready("wo", "residual_pair")
    proj_send[...] = dot_nt(attended[...], wo[...]).reshape(ROWS, 16, CHIP)

    def proj_copy(d):
        r = row_at(d)
        return remote(proj_send.at[r], proj_recv.at[d], proj_s.at[d], proj_r.at[d], r, col)

    start(1, ROWS, proj_copy)
    proj_recv[0] = proj_send[row]
    arrive(1, ROWS, proj_copy)
    half_rows = pl.ds(pl.multiple_of(core * 16, 16), 16)
    residual = jnp.concatenate([res_chip[0, half_rows, :], res_chip[1, half_rows, :]], axis=1).astype(F32)
    stream_all[row, core] = (residual + jnp.sum(proj_recv[...], axis=0)).astype(BF16)

    own_stream = stream_all.at[row, core]

    def stream_copy(d):
        return remote(own_stream, own_stream, stream_s.at[d], stream_r.at[d], row_at(d), col)

    def stream_cross(d):
        return remote(own_stream, own_stream, stream_s.at[ROWS + d], stream_r.at[ROWS + d], row_at(d), sib)

    start(1, ROWS, stream_copy)
    start(0, ROWS, stream_cross)
    own("wh", w_head, wh.at[core])
    swap("wh", w_head, wh.at[core])
    wh_at = len(pending) - 1
    ready("wg", "wu", "gains_pair")
    arrive(1, ROWS, stream_copy)
    arrive(0, ROWS, stream_cross)

    stream = stream_all[...].reshape(T, CHIP).astype(F32)
    square_hi, square_lo = split_sum(jnp.sum(stream * stream, axis=1, keepdims=True), HALF - CHUNKS[0][1])
    stream = stream * jnp.concatenate([mg[0], mg[1]], axis=1)
    mlp_hi = stream.astype(BF16)
    mlp_lo = (stream - mlp_hi.astype(F32)).astype(BF16)

    def y_peer(d):
        return (lax.rem(cy + d, 4) * 2 + zl) * 2 + core

    z_peer = (cy * 2 + 1 - zl) * 2 + core

    def to_y(src, dst, i):
        def copy(d):
            return remote(src(lax.rem(cy + d, 4)), dst(d), y_s.at[i, d], y_r.at[i, d], row, y_peer(d))

        return copy

    def to_z(src, dst, i):
        return lambda d: remote(src, dst, z_s.at[i], z_r.at[i], row, z_peer)

    def gate_up(i, leave):
        low, width = CHUNKS[i]
        for half, weight in enumerate((wg, wu)):
            product = jnp.dot(mlp_hi, weight[:, low:low + width], preferred_element_type=F32)
            product += jnp.dot(mlp_lo, weight[:, low:low + width], preferred_element_type=F32)
            product = product.reshape(4, 2, 32, width)
            gu_own[i, :, :, :, half * HALF:half * HALF + width] = product
            gu_send[i, :, :, :, half * HALF:half * HALF + width] = product.astype(BF16)
            if width < HALF:
                rest = (square_hi, square_lo)[half].reshape(4, 2, 32, HALF - width)
                gu_own[i, :, :, :, half * HALF + width:(half + 1) * HALF] = rest.astype(F32)
                gu_send[i, :, :, :, half * HALF + width:(half + 1) * HALF] = rest
            leave(half)

    def half_lanes(half):
        return pl.ds(half * HALF, HALF)

    def sum_z0(half):
        part = half_lanes(half)
        return to_z(gu_send.at[0, :, 1 - zl, :, part], gu_z0.at[:, :, part], 4 * half)

    def sum_y1(half):
        part = half_lanes(half)
        return to_y(lambda y: gu_send.at[1, y, :, :, part], lambda d: gu_y1.at[d, :, :, part], 4 * half)

    gate_up(0, lambda half: start(0, 1, sum_z0(half)))
    gate_up(1, lambda half: start(1, 4, sum_y1(half)))
    held = pending[-4:]
    del pending[-4:]
    wh_swap = pending.pop(wh_at)
    flush()
    pending.extend([wh_swap] + held)

    for half in range(2):
        arrive(0, 1, sum_z0(half))
    middle = gu_own[0, :, zl] + gu_z0[...].astype(F32)
    mid_own[...] = middle
    mid_send[...] = middle.astype(BF16)
    width = CHUNKS[0][1]
    square = middle[:, :, width:width + 1] + middle[:, :, HALF + width:HALF + width + 1]
    for half, rest in enumerate(split_sum(square.reshape(HEAD, 1), HALF - width)):
        rest = rest.reshape(4, 32, HALF - width)
        mid_own[:, :, half * HALF + width:(half + 1) * HALF] = rest.astype(F32)
        mid_send[:, :, half * HALF + width:(half + 1) * HALF] = rest
    sum_y0 = to_y(lambda y: mid_send.at[y], lambda d: gu_y0.at[d], 1)
    start(1, 4, sum_y0)
    for half in range(2):
        arrive(1, 4, sum_y1(half))
    gu_y1[0] = jnp.zeros((2, 32, FFP), BF16)
    mid2_own[...] = gu_own[1, cy] + jnp.sum(gu_y1[...].astype(F32), axis=0)
    sum_z1 = to_z(mid2_own.at[1 - zl], gu_z1, 1)
    start(0, 1, sum_z1)

    def activate(i, total, scale):
        low, width = CHUNKS[i]
        gate = total[:, 0:width] * scale
        hidden = gate / (1.0 + jnp.exp(-gate)) * (total[:, HALF:HALF + width] * scale)
        hidden_all[cy, zl, :, low:low + width] = hidden.astype(BF16)

    def lanes(i):
        return pl.ds(CHUNKS[i][0], HALF)

    hidden_all[cy, zl, :, FF:FFP] = jnp.zeros((32, FFP - FF), BF16)
    arrive(1, 4, sum_y0)
    gu_y0[0] = jnp.zeros((32, FFP), BF16)
    total = mid_own[cy] + jnp.sum(gu_y0[...].astype(F32), axis=0)
    scale = inverse_rms(total[:, width:width + 1] + total[:, HALF + width:HALF + width + 1])
    activate(0, total, scale)
    own0 = hidden_all.at[cy, zl, :, lanes(0)]
    hid_z0 = to_z(own0, own0, 2)
    start(0, 1, hid_z0)
    arrive(0, 1, sum_z1)
    activate(1, mid2_own[zl] + gu_z1[...], scale)
    own1 = hidden_all.at[cy, zl, :, lanes(1)]

    def hid_1(d):
        return remote(own1, own1, hid_s.at[d], hid_r.at[d], row, chip_at(d) * 2 + core)

    start(1, CHIPS, hid_1)
    arrive(0, 1, hid_z0)
    both0 = hidden_all.at[cy, :, :, lanes(0)]
    hid_y0 = to_y(lambda y: both0, lambda d: both0, 3)
    start(1, 4, hid_y0)
    ready("wd")

    product = jnp.zeros((T, CHIP), F32)
    for i, (low, width) in enumerate(CHUNKS):
        arrive(*((1, 4, hid_y0) if i == 0 else (1, CHIPS, hid_1)))
        hidden = hidden_all[:, :, :, low:low + width].reshape(T, width)
        product += dot_nt(hidden, wd[:, low:low + width])
    down_send[...] = product.reshape(ROWS, 32, CHIP)

    def down_copy(d):
        r = row_at(d)
        return remote(down_send.at[r], down_recv.at[d], down_s.at[d], down_r.at[d], r, col)

    start(1, ROWS, down_copy)
    down_recv[0] = down_send[row]
    arrive(1, ROWS, down_copy)
    final = stream_all[row].reshape(32, CHIP).astype(F32) + jnp.sum(down_recv[...], axis=0)
    square_hi, square_lo = split_sum(jnp.sum(final * final, axis=1, keepdims=True), 64)
    final = (final * jnp.concatenate([fg[0], fg[1]], axis=1)).astype(BF16)

    fin_a[cy, zl, cx, zh] = final[:, 0:256]
    fin_b[cy, zl, cx, zh] = final[:, 256:512]
    fin_c[cy, zl, cx, zh, :, 0:128] = final[:, 512:640]
    fin_c[cy, zl, cx, zh, :, 128:192] = square_hi
    fin_c[cy, zl, cx, zh, :, 192:256] = square_lo

    parts = (fin_a, fin_b, fin_c)
    orders = ("zyx", "xzy", "yxz")

    def axis_copies(p, stage):
        order = orders[p % 3]
        axis, done = order[stage], order[:stage]
        one = {"y": pl.ds(cy, 1), "x": pl.ds(cx, 1), "zl": pl.ds(zl, 1), "zh": pl.ds(zh, 1)}
        full = {"y": pl.ds(0, 4), "x": pl.ds(0, 4), "zl": pl.ds(0, 2), "zh": pl.ds(0, 2)}
        pick = {k: full[k] if k[0] in done else one[k] for k in one}
        ref = parts[p % 3].at[pick["y"], pick["zl"], pick["x"], pick["zh"], pl.ds(p // 3 * 16, 16)]
        copies = []
        for d in (2, 1, 3):
            x = lax.rem(cx + d, 4) if axis == "x" else cx
            y = lax.rem(cy + d, 4) if axis == "y" else cy
            z = lax.rem(cz + d, 4) if axis == "z" else cz
            r, c = at_xyz(x, y, z)
            i = (p * 3 + stage) * 3 + d - 1
            copies.append(remote(ref, ref, fin_s.at[i], fin_r.at[i], r, c))
        return copies

    gathers = [[axis_copies(p, stage) for p in range(6)] for stage in range(3)]
    for stage in range(3):
        for p in range(6):
            if stage:
                for copy in gathers[stage - 1][p]:
                    copy.wait_recv()
            for copy in gathers[stage][p]:
                copy.start()
                pending.append(copy.wait_send)
    last = pending[-18:]
    del pending[-18:]
    flush()
    pending.extend(last)
    ready("wh")
    ready("targets")
    diagonal = lax.broadcasted_iota(jnp.int32, (T, T), 0) == lax.broadcasted_iota(jnp.int32, (T, T), 1)
    target = jnp.sum(jnp.where(diagonal, target_row[...].astype(F32), 0.0), axis=1, keepdims=True).astype(jnp.int32)
    for p in range(6):
        for copy in gathers[2][p]:
            copy.wait_recv()

    square = jnp.zeros((T, 1), F32)
    for y in range(4):
        pieces = []
        for z in range(2):
            c = fin_c[y, z].reshape(T, 256)
            square = square + c[:, 128:129].astype(F32) + c[:, 192:193].astype(F32)
            pieces += [fin_a[y, z].reshape(T, 256), fin_b[y, z].reshape(T, 256), c[:, 0:128]]
        states = jnp.concatenate(pieces, axis=1)
        for j in range(2):
            product = jnp.dot(states, wh[j, y * 2 * CHIP:(y + 1) * 2 * CHIP], preferred_element_type=F32)
            logits[j] = product if y == 0 else logits[j] + product
    scale = inverse_rms(square)
    both = [logits[j] * scale for j in range(2)]
    top = jnp.maximum(*[jnp.max(l, axis=1, keepdims=True) for l in both])
    exponential = sum(jnp.sum(jnp.exp(l - top), axis=1, keepdims=True) for l in both)
    picked = jnp.zeros((T, 1), F32)
    for j in range(2):
        first = (row * COLS + chip * 2 + j) * VOCAB
        ids = first + lax.broadcasted_iota(jnp.int32, (T, VOCAB), 1)
        picked = picked + jnp.sum(jnp.where(ids == target, both[j], 0.0), axis=1, keepdims=True)
    lane = lax.broadcasted_iota(jnp.int32, (T, HEAD), 1)
    packed = jnp.where(lane == 0, top, jnp.where(lane == 1, exponential, picked))
    stat_recv[0] = jnp.transpose(packed)[0:8, :]

    def merge(blocks):
        top = jnp.max(blocks[:, 0:1, :], axis=0)
        exponential = jnp.sum(blocks[:, 1:2, :] * jnp.exp(blocks[:, 0:1, :] - top[None]), axis=0)
        return top, exponential, jnp.sum(blocks[:, 2:3, :], axis=0)

    line = lax.broadcasted_iota(jnp.int32, (8, T), 0)

    def packed_merge(blocks):
        top, exponential, picked = merge(blocks)
        return jnp.where(line == 0, top, jnp.where(line == 1, exponential, picked))

    def st_copy(d):
        return remote(stat_recv.at[0], stat_recv.at[d], st_s.at[d], st_r.at[d], row, chip_at(d) * 2 + core)

    start(1, CHIPS, st_copy)
    arrive(1, CHIPS, st_copy)
    stat_send[...] = packed_merge(stat_recv[...])
    own_stat = stat2_recv.at[core, row]

    def st2_copy(d):
        return remote(stat_send, own_stat, st2_s.at[d], st2_r.at[d], row_at(d), col)

    def st2_cross(d):
        return remote(stat_send, own_stat, st2_s.at[ROWS + d], st2_r.at[ROWS + d], row_at(d), sib)

    start(1, ROWS, st2_copy)
    start(0, ROWS, st2_cross)
    stat2_recv[core, row] = stat_send[...]
    arrive(1, ROWS, st2_copy)
    arrive(0, ROWS, st2_cross)
    logprob = []
    for m in range(2):
        top, exponential, picked = merge(stat2_recv[m])
        logprob.append(picked - (top + jnp.log(exponential)))
    difference = logprob[0] - logprob[1]
    hit = line == k_segment
    sums = jnp.sum(jnp.where(hit, difference, 0.0), axis=1, keepdims=True)
    length = jnp.sum(jnp.where(hit, 1.0, 0.0), axis=1, keepdims=True)
    square8 = lax.broadcasted_iota(jnp.int32, (8, 8), 0) == lax.broadcasted_iota(jnp.int32, (8, 8), 1)
    out[...] = jnp.sum(jnp.where(square8, sums / length, 0.0), axis=0, keepdims=True)

    flush()


def per_device(
    residual, attn_gain, w_query, w_key, w_value, w_out, mlp_gain, w_gate, w_up, w_down, final_gain, w_head,
    seq_lengths, targets,
):
    anywhere = pl.BlockSpec(memory_space=pl.ANY)
    vmem = pl.BlockSpec(memory_space=pltpu.VMEM)
    dma = pltpu.SemaphoreType.DMA
    result = pl.pallas_call(
        kernel,
        out_shape=jax.ShapeDtypeStruct((1, SEQS), F32),
        in_specs=[anywhere] * 12 + [anywhere, anywhere],
        out_specs=vmem,
        scratch_shapes=[
            pltpu.SMEM((SEQS,), jnp.int32),
            pltpu.VMEM((1, T), jnp.int32),
            pltpu.VMEM((2, 32, FEAT), BF16),
            pltpu.VMEM((COLS, 8, HEAD), F32),
            pltpu.VMEM((ROWS, 32, FEAT), BF16),
            pltpu.VMEM((FEAT, QKV), BF16),
            pltpu.VMEM((CHIP, QW), BF16),
            pltpu.VMEM((CHIP, FF), BF16),
            pltpu.VMEM((CHIP, FF), BF16),
            pltpu.VMEM((CHIP, FF), BF16),
            pltpu.VMEM((2, D, VOCAB), BF16),
            pltpu.VMEM((FEAT,), F32),
            pltpu.VMEM((FEAT,), F32),
            pltpu.VMEM((FEAT,), F32),
            pltpu.VMEM((2, 1, FEAT), F32),
            pltpu.VMEM((2, 1, FEAT), F32),
            pltpu.VMEM((CHIPS, 2, 16, QKV), F32),
            pltpu.VMEM((CHIPS, 16, QKV), F32),
            pltpu.VMEM((CHIPS, 16, QKV), F32),
            pltpu.VMEM((CHIPS, 16, QKV), F32),
            pltpu.VMEM((CHIPS, 2, 16, QKV), BF16),
            pltpu.VMEM((T // 2, QW), BF16),
            pltpu.VMEM((ROWS, 16, CHIP), F32),
            pltpu.VMEM((ROWS, 16, CHIP), F32),
            pltpu.VMEM((ROWS, 2, 16, CHIP), BF16),
            pltpu.VMEM((2, 4, 2, 32, FFP), F32),
            pltpu.VMEM((2, 4, 2, 32, FFP), BF16),
            pltpu.VMEM((4, 32, FFP), BF16),
            pltpu.VMEM((4, 32, FFP), BF16),
            pltpu.VMEM((32, FFP), F32),
            pltpu.VMEM((4, 2, 32, FFP), BF16),
            pltpu.VMEM((4, 32, FFP), F32),
            pltpu.VMEM((4, 32, FFP), BF16),
            pltpu.VMEM((2, 32, FFP), F32),
            pltpu.VMEM((4, 2, 32, FFP), BF16),
            pltpu.VMEM((ROWS, 32, CHIP), F32),
            pltpu.VMEM((ROWS, 32, CHIP), F32),
            pltpu.VMEM((4, 2, 4, 2, 32, 256), BF16),
            pltpu.VMEM((4, 2, 4, 2, 32, 256), BF16),
            pltpu.VMEM((4, 2, 4, 2, 32, 256), BF16),
            pltpu.VMEM((2, T, VOCAB), F32),
            pltpu.VMEM((8, T), F32),
            pltpu.VMEM((CHIPS, 8, T), F32),
            pltpu.VMEM((2, ROWS, 8, T), F32),
            dma((14,)), dma((8,)), dma((8,)),
            dma((COLS,)), dma((COLS,)),
            dma((ROWS,)), dma((ROWS,)),
            dma, dma,
            dma((CHIPS,)), dma((CHIPS,)),
            dma((COLS,)), dma((COLS,)),
            dma((ROWS,)), dma((ROWS,)),
            dma((2 * ROWS,)), dma((2 * ROWS,)),
            dma((5, 4)), dma((5, 4)),
            dma((5,)), dma((5,)),
            dma((CHIPS,)), dma((CHIPS,)),
            dma((ROWS,)), dma((ROWS,)),
            dma((54,)), dma((54,)),
            dma((CHIPS,)), dma((CHIPS,)),
            dma((2 * ROWS,)), dma((2 * ROWS,)),
        ],
        compiler_params=pltpu.CompilerParams(
            collective_id=0, has_side_effects=True, vmem_limit_bytes=60 * 1024 * 1024
        ),
    )(
        residual, attn_gain, w_query, w_key, w_value, w_out.T, mlp_gain, w_gate, w_up,
        jnp.swapaxes(w_down, 1, 2), final_gain, w_head, seq_lengths, targets.reshape(1, T),
    )
    return result.reshape(SEQS)


def solution(mesh):
    placed = (
        P("row", "col"), P("col"), P("col", "row"), P("col", "row"), P("col", "row"), P("row", "col"), P("col"),
        P(None, "col", "row"), P(None, "col", "row"), P(None, "row", "col"), P("col"), P(None, ("row", "col")), P(), P(),
    )
    return jax.shard_map(per_device, mesh=mesh, in_specs=placed, out_specs=P(), check_vma=False)
```
